32 devices in a mesh: dp: 16 (over z, x, core), ctx: 2 (over y).
Axes of the slice: x: 2, y: 2, z: 4, core: 2. Of those that a mesh axis runs over, the one named last changes fastest.
Arguments:
- tokens: bfloat16 [16, 256, 960], P('dp', 'ctx'), may hold values from -6 to 6
- segment_ids: int32 [16, 256], P('dp', 'ctx'), may hold values from 0 to 3, never falling along the last dimension, each value on 1 to 128 neighbouring positions
- norm_gains: float32 [2, 960], P(None, 'dp'), may hold values from 0.5 to 1.5
- w_query: bfloat16 [960, 960], P('dp', 'ctx'), may hold values from -0.1875 to 0.1875
- w_key: bfloat16 [960, 320], P('dp', 'ctx'), may hold values from -0.1875 to 0.1875
- w_value: bfloat16 [960, 320], P('dp', 'ctx'), may hold values from -0.1875 to 0.1875
- w_out: bfloat16 [960, 960], P('dp', 'ctx'), may hold values from -0.75 to 0.75
- w_gate: bfloat16 [960, 2560], P('dp', 'ctx'), may hold values from -0.1875 to 0.1875
- w_up: bfloat16 [960, 2560], P('dp', 'ctx'), may hold values from -0.1875 to 0.1875
- w_down: bfloat16 [2560, 960], P('dp', 'ctx'), may hold values from -0.125 to 0.125
- cotangent: bfloat16 [16, 256, 960], P('dp', 'ctx'), may hold values from -6 to 6
Outputs:
- block_output: bfloat16 [16, 256, 960], P('dp', 'ctx')
- input_grad: float32 [16, 256, 960], P('dp', 'ctx')
- query_grad: float32 [960, 960], P('dp', 'ctx')
- key_grad: float32 [960, 320], P('dp', 'ctx')
- value_grad: float32 [960, 320], P('dp', 'ctx')
- out_grad: float32 [960, 960], P('dp', 'ctx')
- gate_grad: float32 [960, 2560], P('dp', 'ctx')
- up_grad: float32 [960, 2560], P('dp', 'ctx')
- down_grad: float32 [2560, 960], P('dp', 'ctx')
- gain_grad: float32 [2, 960], P(None, 'dp')
The draws below stay inside these ranges and needn't reach their ends.
Inputs may be any that keep to these rules, and one draw needn't show every extreme that they name: `segment_ids`: along each sequence the segment number never falls; each segment holds 1 to 128 tokens, and one segment of each sequence holds exactly that many.
All inputs are finite; a program needn't handle non-finite values.
Results may differ from the reference program's by a relative error of at most 0.034.
Values may be sent and summed in bfloat16 or wider, within the bound.
No kernel may reach another device: no remote copies, remote signals or barrier semaphores. Data moves between devices by JAX's collectives and lax.ppermute only.
A program may use at most 192 MiB of HBM per device.

```python
import math
import jax
import jax.numpy as jnp
import numpy as np
from jax import lax

D = 960
H = 15
KV = 5
HD = 64
FF = 2560
SEQ = 256
SEQS = 16


def steps_of(rng, extent, cuts, smallest, largest):
    factor_of = 1.0
    for position, parts in cuts:
        heights = jax.random.uniform(jax.random.fold_in(jax.random.fold_in(rng, 6), position), (parts,), jnp.float32, smallest / len(cuts), largest / len(cuts))
        factor_of = factor_of * jnp.repeat(jnp.exp(heights), extent[position] // parts).reshape((-1,) + (1,) * (len(extent) - 1 - position))
    return factor_of


def split_up(count, total, limit, skew):
    portions = [(1 << 20) // math.isqrt(rank ** skew) + 1 for rank in range(2, count + 1)]
    rest, counts = total - limit - (count - 1), [1] * (count - 1)
    while rest > 0:
        movable = [i for i in range(count - 1) if counts[i] < limit]
        whole, left = sum([portions[i] for i in movable]), rest
        for i in movable:
            more = min(limit - counts[i], max(1, left * portions[i] // whole), rest)
            counts[i] = counts[i] + more
            rest = rest - more
    return np.array([limit] + counts)


def ragged(stream_key, count, total, bound, slope):
    if count == 2:
        one = jax.random.randint(stream_key, (), max(1, total - bound), min(bound, total - 1) + 1)
        return jnp.stack([one, total - one])
    tallies = jnp.asarray(split_up(count, total, bound, slope), jnp.int32)
    pairs = (count - 1) // 2
    source_of, sink = tallies[1:1 + 2 * pairs:2], tallies[2:2 + 2 * pairs:2]
    margin = jnp.minimum(source_of - 1, bound - sink)
    passed = jax.random.randint(jax.random.fold_in(stream_key, 1), (pairs,), 0, 1 << 20) % (margin + 1)
    tallies = tallies.at[1:1 + 2 * pairs:2].set(source_of - passed).at[2:2 + 2 * pairs:2].set(sink + passed)
    return tallies[jax.random.permutation(jax.random.fold_in(stream_key, 2), count)]


def gaussian(stream_key, dims, spread, reach, split=(), kind=jnp.bfloat16):
    level = steps_of(stream_key, dims, split, -0.22, 0.18) if split else 1.0
    values = jax.random.normal(stream_key, dims, jnp.float32) * spread * level
    return jnp.minimum(jnp.maximum(values, -reach), reach).astype(kind)


def setup_inputs(seed: int = 0) -> dict:
    key_of = jax.random.split(jax.random.key(seed), 12)
    tokens = gaussian(key_of[0], (SEQS, SEQ, D), 1.0, 6.0, ((0, 16), (1, 2)))
    segment_ids = jax.vmap(lambda own: jnp.searchsorted(jnp.cumsum(ragged(own, 4, SEQ, SEQ // 2, 0)), jnp.arange(SEQ), side="right"))(jax.random.split(key_of[1], SEQS)).reshape((SEQS, SEQ)).astype(jnp.int32)
    norm_gains = jnp.clip(1.0 + 0.1 * jax.random.normal(key_of[2], (2, D), jnp.float32), 0.5, 1.5)
    w_query = gaussian(key_of[3], (D, H * HD), D ** -0.5, 0.1875, ((0, 16), (1, 2)))
    w_key = gaussian(key_of[4], (D, KV * HD), D ** -0.5, 0.1875, ((0, 16), (1, 2)))
    w_value = gaussian(key_of[5], (D, KV * HD), D ** -0.5, 0.1875, ((0, 16), (1, 2)))
    w_out = gaussian(key_of[6], (H * HD, D), (H * HD // 16) ** -0.5, 0.75, ((0, 16), (1, 2)))
    w_gate = gaussian(key_of[7], (D, FF), D ** -0.5, 0.1875, ((0, 16), (1, 2)))
    w_up = gaussian(key_of[8], (D, FF), D ** -0.5, 0.1875, ((0, 16), (1, 2)))
    w_down = gaussian(key_of[9], (FF, D), FF ** -0.5, 0.125, ((0, 16), (1, 2)))
    cotangent = gaussian(key_of[10], (SEQS, SEQ, D), 1.0, 6.0, ((0, 16), (1, 2)))
    return dict(tokens=tokens, segment_ids=segment_ids, norm_gains=norm_gains, w_query=w_query, w_key=w_key, w_value=w_value, w_out=w_out, w_gate=w_gate, w_up=w_up, w_down=w_down, cotangent=cotangent)


norm_eps = 1e-05
rope_base = 100000.0

def normed(hidden, scales):
    factor = lax.rsqrt(lax.optimization_barrier(jnp.mean(hidden * hidden, axis=-1, keepdims=True)) + norm_eps)
    return hidden * factor * scales

def rope_tables(amount, offset, head_size):
    middle = head_size // 2
    inverse_rates = rope_base ** (-(jnp.arange(middle, dtype=jnp.float32) * 2.0) / head_size)
    places = (offset + jnp.arange(amount, dtype=jnp.int32)).astype(jnp.float32)
    angles = places[:, None] * inverse_rates[None, :]
    return (jnp.cos(angles)[:, None, :], jnp.sin(angles)[:, None, :])

def rotate(values, cosine, sine):
    middle = values.shape[-1] // 2
    first_half = values[..., :middle]
    second_half = values[..., middle:]
    return jnp.concatenate([first_half * cosine - second_half * sine, second_half * cosine + first_half * sine], axis=-1)

def unrotate(values, cosine, sine):
    middle = values.shape[-1] // 2
    first_half = values[..., :middle]
    second_half = values[..., middle:]
    return jnp.concatenate([first_half * cosine + second_half * sine, second_half * cosine - first_half * sine], axis=-1)

def matmul(left, right):
    return jnp.dot(left, right, preferred_element_type=jnp.float32)

def layer_pass(tokens, segments, cotangent, gains, w_query, w_key, w_value, w_out, w_gate, w_up, w_down):
    length = tokens.shape[0]
    groups = H // KV
    scale_factor = 1.0 / math.sqrt(HD)
    hidden = tokens.astype(jnp.float32)
    first_norm = normed(hidden, gains[0]).astype(jnp.bfloat16)
    cosine, sine = rope_tables(length, 0, HD)
    query = rotate(matmul(first_norm, w_query).reshape(length, H, HD), cosine, sine).astype(jnp.bfloat16)
    keys = rotate(matmul(first_norm, w_key).reshape(length, KV, HD), cosine, sine).astype(jnp.bfloat16)
    values = matmul(first_norm, w_value).reshape(length, KV, HD).astype(jnp.bfloat16)
    grouped = query.reshape(length, KV, groups, HD)
    places = jnp.arange(length, dtype=jnp.int32)
    allowed = (places[None, :] <= places[:, None]) & (segments[None, :] == segments[:, None])
    scores = jnp.einsum('tkgd,skd->kgts', grouped.astype(jnp.float32), keys.astype(jnp.float32)) * scale_factor
    totals = lax.optimization_barrier(jnp.sum(jnp.where(allowed, jnp.exp(scores), 0.0), axis=-1, keepdims=True))
    log_total = jnp.log(totals)
    exact_probs = jnp.where(allowed, jnp.exp(scores - log_total), 0.0)
    probs = exact_probs.astype(jnp.bfloat16)
    attended = jnp.einsum('kgts,skd->tkgd', probs.astype(jnp.float32), values.astype(jnp.float32))
    attended = attended.reshape(length, H * HD).astype(jnp.bfloat16)
    middle = hidden + matmul(attended, w_out)
    second_norm = normed(middle, gains[1]).astype(jnp.bfloat16)
    gate = matmul(second_norm, w_gate)
    upward = matmul(second_norm, w_up)
    sigma = jax.nn.sigmoid(gate)
    activated = gate * sigma
    mixed = (activated * upward).astype(jnp.bfloat16)
    block_output = (middle + matmul(mixed, w_down)).astype(jnp.bfloat16)
    grad_down = matmul(mixed.T, cotangent)
    grad_mixed = matmul(cotangent, w_down.T)
    grad_gate = (grad_mixed * upward * sigma * (1.0 + gate * (1.0 - sigma))).astype(jnp.bfloat16)
    grad_upward = (grad_mixed * activated).astype(jnp.bfloat16)
    grad_wgate = matmul(second_norm.T, grad_gate)
    grad_wup = matmul(second_norm.T, grad_upward)
    grad_second = matmul(grad_gate, w_gate.T) + matmul(grad_upward, w_up.T)
    unused, pull_second = jax.vjp(normed, middle, gains[1])
    grad_middle_norm, grad_gain_second = pull_second(grad_second)
    grad_middle = cotangent.astype(jnp.float32) + grad_middle_norm
    grad_branch = grad_middle.astype(jnp.bfloat16)
    grad_wout = matmul(attended.T, grad_branch)
    grad_attended = matmul(grad_branch, w_out.T).astype(jnp.bfloat16).reshape(length, KV, groups, HD)
    grad_values = jnp.einsum('kgts,tkgd->skd', probs.astype(jnp.float32), grad_attended.astype(jnp.float32))
    grad_probs = jnp.einsum('tkgd,skd->kgts', grad_attended.astype(jnp.float32), values.astype(jnp.float32))
    row_terms = lax.optimization_barrier(jnp.sum(exact_probs * grad_probs, axis=-1, keepdims=True))
    grad_scores = (exact_probs * (grad_probs - row_terms) * scale_factor).astype(jnp.bfloat16)
    grad_query = jnp.einsum('kgts,skd->tkgd', grad_scores.astype(jnp.float32), keys.astype(jnp.float32))
    grad_query = unrotate(grad_query.reshape(length, H, HD), cosine, sine).reshape(length, H * HD).astype(jnp.bfloat16)
    grad_keys = jnp.einsum('kgts,tkgd->skd', grad_scores.astype(jnp.float32), grouped.astype(jnp.float32))
    grad_keys = unrotate(grad_keys, cosine, sine).reshape(length, KV * HD).astype(jnp.bfloat16)
    grad_values = grad_values.reshape(length, KV * HD).astype(jnp.bfloat16)
    grad_wquery = matmul(first_norm.T, grad_query)
    grad_wkey = matmul(first_norm.T, grad_keys)
    grad_wvalue = matmul(first_norm.T, grad_values)
    grad_first = matmul(grad_query, w_query.T) + matmul(grad_keys, w_key.T) + matmul(grad_values, w_value.T)
    unused_two, pull_first = jax.vjp(normed, hidden, gains[0])
    grad_hidden_norm, grad_gain_first = pull_first(grad_first)
    input_grad = grad_middle + grad_hidden_norm
    gain_terms = jnp.stack([grad_gain_first, grad_gain_second])
    return (block_output, input_grad, (grad_wquery, grad_wkey, grad_wvalue, grad_wout, grad_wgate, grad_wup, grad_down, gain_terms))

def reference(tokens, segment_ids, norm_gains, w_query, w_key, w_value, w_out, w_gate, w_up, w_down, cotangent):
    weight_list = (w_query, w_key, w_value, w_out, w_gate, w_up, w_down, norm_gains)
    starting = tuple((jnp.zeros(item.shape, jnp.float32) for item in weight_list))

    def one_sequence(carry, items):
        seq_tokens, seq_segments, seq_cotangent = items
        output, grad_input, grads = layer_pass(seq_tokens, seq_segments, seq_cotangent, norm_gains, w_query, w_key, w_value, w_out, w_gate, w_up, w_down)
        summed = tuple((left + right for left, right in zip(carry, grads)))
        return (summed, (output, grad_input))
    totals, stacked = lax.scan(one_sequence, starting, (tokens, segment_ids, cotangent))
    return (stacked[0], stacked[1], totals[0], totals[1], totals[2], totals[3], totals[4], totals[5], totals[6], totals[7])
```

```python
import math

import jax
import jax.numpy as jnp
from jax import lax
from jax.sharding import PartitionSpec as P

H = 15
KV = 5
HD = 64


norm_eps = 1e-05
rope_base = 100000.0

AXES = ("dp", "ctx")


def normed(hidden, scales):
    factor = lax.rsqrt(jnp.mean(hidden * hidden, axis=-1, keepdims=True) + norm_eps)
    return hidden * factor * scales


def rope_tables(amount, offset, head_size):
    middle = head_size // 2
    inverse_rates = rope_base ** (-(jnp.arange(middle, dtype=jnp.float32) * 2.0) / head_size)
    places = (offset + jnp.arange(amount, dtype=jnp.int32)).astype(jnp.float32)
    angles = places[:, None] * inverse_rates[None, :]
    return (jnp.cos(angles)[:, None, :], jnp.sin(angles)[:, None, :])


def rotate(values, cosine, sine):
    middle = values.shape[-1] // 2
    first_half = values[..., :middle]
    second_half = values[..., middle:]
    return jnp.concatenate(
        [first_half * cosine - second_half * sine, second_half * cosine + first_half * sine],
        axis=-1,
    )


def unrotate(values, cosine, sine):
    middle = values.shape[-1] // 2
    first_half = values[..., :middle]
    second_half = values[..., middle:]
    return jnp.concatenate(
        [first_half * cosine + second_half * sine, second_half * cosine - first_half * sine],
        axis=-1,
    )


def matmul(left, right):
    return jnp.dot(left, right, preferred_element_type=jnp.float32)


def score_block(grouped, key_grid, scale_factor):
    return (
        jnp.einsum("tkgd,skd->kgts", grouped, key_grid, preferred_element_type=jnp.float32)
        * scale_factor
    )


def probabilities(scores, allowed, log_total):
    return jnp.where(allowed, jnp.exp(scores - log_total), 0.0)


bf16 = jnp.bfloat16
f32 = jnp.float32


class Links:
    def __init__(self):
        self.dp = lax.axis_size("dp")
        self.nz = self.dp // 4
        index = lax.axis_index("dp")
        self.y = lax.axis_index("ctx")
        self.c = index % 2
        self.x = (index // 2) % 2
        self.z = index // 4

    def _permute(self, value, target):
        pairs = []
        for z in range(self.nz):
            for x in range(2):
                for c in range(2):
                    for y in range(2):
                        z2, x2, c2, y2 = target(z, x, c, y)
                        pairs.append(
                            (((z * 2 + x) * 2 + c) * 2 + y, ((z2 * 2 + x2) * 2 + c2) * 2 + y2)
                        )
        return lax.ppermute(value, AXES, pairs)

    def core(self, value):
        return self._permute(value, lambda z, x, c, y: (z, x, 1 - c, y))

    def over_x(self, value):
        return self._permute(value, lambda z, x, c, y: (z, 1 - x, c, y))

    def over_y(self, value):
        return self._permute(value, lambda z, x, c, y: (z, x, c, 1 - y))

    def over_z(self, value, step):
        return self._permute(value, lambda z, x, c, y: ((z + step) % self.nz, x, c, y))

    def order(self, flag, own, other, axis):
        return jnp.where(
            flag == 0,
            jnp.concatenate([own, other], axis=axis),
            jnp.concatenate([other, own], axis=axis),
        )

    def gather_z(self, block):
        parts = [block] + [self.over_z(block, k) for k in range(1, self.nz)]
        slots = []
        for slot in range(self.nz):
            distance = (self.z - slot) % self.nz
            value = parts[0]
            for k in range(1, self.nz):
                value = jnp.where(distance == k, parts[k], value)
            slots.append(value)
        return jnp.stack(slots)

    def spread(self, line, first):
        by_x = self.over_x(line)
        by_y = self.over_y(line)
        diagonal = self.over_y(by_x) if first == "x" else self.over_x(by_y)
        nz, m, n = line.shape
        own = self.order(self.x, line[:, None], by_x[:, None], 1).reshape(nz * 2 * m, n)
        other = self.order(self.x, by_y[:, None], diagonal[:, None], 1).reshape(nz * 2 * m, n)
        return own, other

    def reduce(self, grads, first):
        own = grads[0][0].astype(f32)
        if first == "y":
            corner = self.over_y(grads[1][1])
            by_y = self.over_y(grads[1][0])
            by_x = self.over_x((grads[0][1].astype(f32) + corner.astype(f32)).astype(bf16))
        else:
            corner = self.over_x(grads[1][1])
            by_x = self.over_x(grads[0][1])
            by_y = self.over_y((grads[1][0].astype(f32) + corner.astype(f32)).astype(bf16))
        line = own + by_x.astype(f32) + by_y.astype(f32)
        low = line.astype(bf16)
        total = lax.dynamic_index_in_dim(line, self.z, 0, keepdims=False)
        for k in range(1, self.nz):
            block = lax.dynamic_index_in_dim(low, (self.z + k) % self.nz, 0, keepdims=False)
            total = total + self.over_z(block, k).astype(f32)
        return total


def pick(flag, pair):
    return jnp.where(flag == 0, pair[0], pair[1])


def fast_body(
    tokens, segment_ids, norm_gains, w_query, w_key, w_value, w_out, w_gate, w_up, w_down, cotangent
):
    net = Links()
    nz, c, x, y = net.nz, net.c, net.x, net.y
    local_rows = tokens.shape[1]
    width = tokens.shape[2]
    rows = w_query.shape[0]
    groups = H // KV
    scale_factor = 1.0 / math.sqrt(HD)
    q_cols, k_cols, o_cols = w_query.shape[1], w_key.shape[1], w_out.shape[1]
    attn_cols = q_cols + k_cols
    ff_rows = w_down.shape[0]
    half_ff = w_gate.shape[1] // 2
    half_rows = nz * rows * 2

    mine = tokens[0]
    facing = net.over_y(mine)
    segments_mine = segment_ids[0]
    segments_facing = net.over_y(segments_mine)
    incoming = cotangent[0]
    incoming_pair = jnp.concatenate([incoming, net.core(incoming)], axis=0)

    def by_core(w):
        return w.reshape(rows, half_ff // ff_rows, 2, ff_rows)

    qk = jnp.concatenate([w_query, w_key], axis=1)
    vo = jnp.concatenate([w_value, w_out], axis=1)
    gate_parts, up_parts = by_core(w_gate), by_core(w_up)
    gate_half = [gate_parts[:, :, i].reshape(rows, half_ff) for i in range(2)]
    up_half = [up_parts[:, :, i].reshape(rows, half_ff) for i in range(2)]
    gains_row = norm_gains.astype(bf16)
    keep_attn = pick(c, (qk, vo))
    got_attn, got_gains = net.core(pick(c, (vo, qk))), net.core(gains_row)
    got_gate = net.core(pick(c, (gate_half[1], gate_half[0])))
    got_up = net.core(pick(c, (up_half[1], up_half[0])))
    gains_chip = net.order(c, gains_row, got_gains, 1).reshape(1, 4 * rows)
    gains_chip = jnp.pad(gains_chip, ((0, 7), (0, attn_cols - 4 * rows)))
    attn_block = jnp.concatenate([net.order(c, keep_attn, got_attn, 0), gains_chip], axis=0)
    gate_block = net.order(c, pick(c, gate_half), got_gate, 0)
    up_block = net.order(c, pick(c, up_half), got_up, 0)

    cut = (rows + 4) // 8 * 8
    attn_top = net.gather_z(attn_block[:cut])
    attn_low = net.gather_z(attn_block[cut:])
    gate_block, up_block, attn_top, attn_low = lax.optimization_barrier(
        (gate_block, up_block, attn_top, attn_low)
    )
    gate_line, up_line = net.gather_z(gate_block), net.gather_z(up_block)
    top, low = net.spread(attn_top, "x"), net.spread(attn_low, "y")

    def joined(a, b):
        n = a.shape[1]
        return jnp.concatenate(
            [a.reshape(nz * 2, -1, n), b.reshape(nz * 2, -1, n)], axis=1
        )

    attn_all = [joined(top[i], low[i]) for i in range(2)]
    gains_all = attn_all[0][:, 2 * rows, : 4 * rows].reshape(nz * 2, 2, 2 * rows)
    gains_full = jnp.transpose(gains_all, (1, 0, 2)).reshape(2, width).astype(f32)
    attn_own = jnp.stack([a[:, : 2 * rows].reshape(width, attn_cols) for a in attn_all])
    attn_other = net.core(attn_own)
    qk_full = pick(c, (attn_own, attn_other))
    vo_full = pick(c, (attn_other, attn_own))

    gate_line, up_line, w_down_late = lax.optimization_barrier((gate_line, up_line, w_down))
    cut_down = ff_rows // 2
    gate_all = net.spread(gate_line, "x")
    up_all = net.spread(up_line, "y")
    down_top_line = net.gather_z(w_down_late[:cut_down])
    down_low_line = net.gather_z(w_down_late[cut_down:])
    down_top, down_low = net.spread(down_top_line, "x"), net.spread(down_low_line, "y")
    down_all = [joined(down_top[i], down_low[i]).reshape(2 * nz * ff_rows, -1) for i in range(2)]

    def in_order(a, b, axis):
        return net.order(y, a, b, axis)

    both = jnp.concatenate([mine, facing], axis=0).astype(f32)
    hidden = mine.astype(f32)
    first_both = normed(both, gains_full[0]).astype(bf16)
    first_norm = first_both[:local_rows]
    cosine, sine = rope_tables(local_rows, y * local_rows, HD)
    cosine_f, sine_f = rope_tables(local_rows, (1 - y) * local_rows, HD)
    cosine_b = jnp.concatenate([cosine, cosine_f], axis=0)
    sine_b = jnp.concatenate([sine, sine_f], axis=0)
    both_rows = 2 * local_rows
    wq = in_order(qk_full[0][:, :q_cols], qk_full[1][:, :q_cols], 1)
    wk = in_order(qk_full[0][:, q_cols:], qk_full[1][:, q_cols:], 1)
    wv = in_order(vo_full[0][:, :k_cols], vo_full[1][:, :k_cols], 1)
    wo = in_order(vo_full[0][:, k_cols:], vo_full[1][:, k_cols:], 1)
    query = rotate(matmul(first_norm, wq).reshape(local_rows, H, HD), cosine, sine).astype(bf16)
    key_grid = rotate(matmul(first_both, wk).reshape(both_rows, KV, HD), cosine_b, sine_b).astype(
        bf16
    )
    value_grid = matmul(first_both, wv).astype(bf16).reshape(both_rows, KV, HD)
    grouped = query.reshape(local_rows, KV, groups, HD)
    own_places = y * local_rows + jnp.arange(local_rows, dtype=jnp.int32)
    facing_places = (1 - y) * local_rows + jnp.arange(local_rows, dtype=jnp.int32)
    key_places = jnp.concatenate([own_places, facing_places])
    segment_all = jnp.concatenate([segments_mine, segments_facing])
    allowed = (key_places[None, :] <= own_places[:, None]) & (
        segment_all[None, :] == segments_mine[:, None]
    )
    scores = score_block(grouped, key_grid, scale_factor)
    totals = jnp.sum(jnp.where(allowed, jnp.exp(scores), 0.0), axis=-1, keepdims=True)
    log_total = jnp.log(totals)
    exact_probs = probabilities(scores, allowed, log_total)
    probs = exact_probs.astype(bf16)
    attended = jnp.einsum("kgts,skd->tkgd", probs, value_grid, preferred_element_type=f32)
    attended = attended.reshape(local_rows, H * HD).astype(bf16)
    middle = hidden + matmul(attended, wo)
    second_norm = normed(middle, gains_full[1]).astype(bf16)

    second_pair = jnp.concatenate([second_norm, net.core(second_norm)], axis=0)
    gate = [matmul(second_pair, w) for w in gate_all]
    upward = [matmul(second_pair, w) for w in up_all]
    sigma = [jax.nn.sigmoid(g) for g in gate]
    activated = [g * s for g, s in zip(gate, sigma)]
    mixed = [(a * u).astype(bf16) for a, u in zip(activated, upward)]
    mixed_all = in_order(mixed[0], mixed[1], 1)
    partial = in_order(matmul(mixed_all, down_all[0]), matmul(mixed_all, down_all[1]), 1)
    from_other = net.core(partial[local_rows:].astype(bf16))
    block_output = (middle + partial[:local_rows] + from_other.astype(f32)).astype(bf16)

    def halves(value, count):
        m = value.shape[0] // (count * 2)
        split = value.reshape(count, 2, m, value.shape[1])
        even, odd = split[:, 0], split[:, 1]
        return jnp.where(x == 0, even, odd), jnp.where(x == 0, odd, even)

    def weight_grads(left_t, rights, first):
        parts = halves(left_t, nz)
        m = parts[0].shape[1]
        grads = [
            [
                matmul(part.reshape(nz * m, -1), right).astype(bf16).reshape(nz, m, -1)
                for part in parts
            ]
            for right in rights
        ]
        return net.reduce(grads, first)

    incoming_half = jnp.split(incoming_pair, 2, axis=1)
    incoming_dy = [pick(y, incoming_half), pick(y, incoming_half[::-1])]
    mixed_t = mixed_all.T.reshape(nz * 2, 2, cut_down, both_rows)
    mixed_top_t = mixed_t[:, 0].reshape(nz * 2 * cut_down, both_rows)
    mixed_low_t = mixed_t[:, 1].reshape(nz * 2 * cut_down, both_rows)
    down_grad = jnp.concatenate(
        [
            weight_grads(mixed_top_t, incoming_dy, "y"),
            weight_grads(mixed_low_t, incoming_dy, "x"),
        ],
        axis=0,
    )
    grad_mixed_all = matmul(incoming_dy[0], down_all[0].T) + matmul(incoming_dy[1], down_all[1].T)
    grad_mixed_half = jnp.split(grad_mixed_all, 2, axis=1)
    grad_mixed = [pick(y, grad_mixed_half), pick(y, grad_mixed_half[::-1])]
    grad_gate = [
        (gm * u * s * (1.0 + g * (1.0 - s))).astype(bf16)
        for gm, u, s, g in zip(grad_mixed, upward, sigma, gate)
    ]
    grad_upward = [(gm * a).astype(bf16) for gm, a in zip(grad_mixed, activated)]
    second_t = second_pair.T
    gate_sum = weight_grads(second_t, grad_gate, "y")
    up_sum = weight_grads(second_t, grad_upward, "x")
    grad_second_pair = (
        matmul(grad_gate[0], gate_all[0].T)
        + matmul(grad_gate[1], gate_all[1].T)
        + matmul(grad_upward[0], up_all[0].T)
        + matmul(grad_upward[1], up_all[1].T)
    )
    grad_second = grad_second_pair[:local_rows] + net.core(
        grad_second_pair[local_rows:].astype(bf16)
    ).astype(f32)
    unused, pull_second = jax.vjp(normed, middle, gains_full[1])
    grad_middle_norm, grad_gain_second = pull_second(grad_second)
    grad_middle = incoming.astype(f32) + grad_middle_norm
    grad_branch = grad_middle.astype(bf16)
    grad_attended = matmul(grad_branch, wo.T).astype(bf16).reshape(local_rows, KV, groups, HD)
    grad_values_all = jnp.einsum(
        "kgts,tkgd->skd", probs, grad_attended, preferred_element_type=f32
    )
    grad_probs = jnp.einsum(
        "tkgd,skd->kgts", grad_attended, value_grid, preferred_element_type=f32
    )
    row_terms = jnp.sum(exact_probs * grad_probs, axis=-1, keepdims=True)
    grad_scores = (exact_probs * (grad_probs - row_terms) * scale_factor).astype(bf16)
    grad_query = jnp.einsum("kgts,skd->tkgd", grad_scores, key_grid, preferred_element_type=f32)
    grad_query = (
        unrotate(grad_query.reshape(local_rows, H, HD), cosine, sine)
        .reshape(local_rows, H * HD)
        .astype(bf16)
    )
    grad_keys_all = jnp.einsum(
        "kgts,tkgd->skd", grad_scores, grouped, preferred_element_type=f32
    )
    grad_kv_all = jnp.concatenate(
        [
            grad_keys_all.reshape(both_rows, KV * HD),
            grad_values_all.reshape(both_rows, KV * HD),
        ],
        axis=1,
    )
    from_facing = net.over_y(grad_kv_all[local_rows:].astype(bf16)).astype(f32)
    grad_kv = grad_kv_all[:local_rows] + from_facing
    grad_keys = (
        unrotate(grad_kv[:, : KV * HD].reshape(local_rows, KV, HD), cosine, sine)
        .reshape(local_rows, KV * HD)
        .astype(bf16)
    )
    grad_values = grad_kv[:, KV * HD :].astype(bf16)
    grad_first = (
        matmul(grad_query, wq.T) + matmul(grad_keys, wk.T) + matmul(grad_values, wv.T)
    )
    unused_two, pull_first = jax.vjp(normed, hidden, gains_full[0])
    grad_hidden_norm, grad_gain_first = pull_first(grad_first)
    input_grad = grad_middle + grad_hidden_norm

    def column_halves(value):
        pair = jnp.split(value, 2, axis=1)
        return pick(y, pair), pick(y, pair[::-1])

    first_t, attended_t = first_norm.T, attended.T
    gq, gk, gv, go = (
        column_halves(g) for g in (grad_query, grad_keys, grad_values, grad_branch)
    )
    gains_terms = jnp.stack([grad_gain_first, grad_gain_second]).reshape(2, nz * 2, 2 * rows)
    gains_terms = jnp.transpose(gains_terms, (1, 0, 2)).reshape(nz * 2, 1, 4 * rows)
    gains_terms = jnp.pad(gains_terms, ((0, 0), (0, 7), (0, attn_cols - 4 * rows))).astype(bf16)

    def with_gains(grad):
        grad = grad.reshape(nz * 2, 2 * rows, attn_cols)
        return jnp.concatenate([grad, gains_terms], axis=1)

    grads_qk = jnp.stack(
        [
            with_gains(
                matmul(first_t, jnp.concatenate([gq[i], gk[i]], axis=1)).astype(bf16)
            )
            for i in range(2)
        ]
    )
    grads_vo = jnp.stack(
        [
            with_gains(
                jnp.concatenate([matmul(first_t, gv[i]), matmul(attended_t, go[i])], axis=1).astype(
                    bf16
                )
            )
            for i in range(2)
        ]
    )
    from_core = net.core(pick(c, (grads_vo, grads_qk)))
    grads_attn = (pick(c, (grads_qk, grads_vo)).astype(f32) + from_core.astype(f32)).astype(bf16)
    split = grads_attn.reshape(2, nz, 2, 2 * rows + 8, attn_cols)
    by_x = (
        jnp.where(x == 0, split[:, :, 0], split[:, :, 1]),
        jnp.where(x == 0, split[:, :, 1], split[:, :, 0]),
    )
    top_sum = net.reduce([[by_x[dx][dy][:, :cut] for dx in range(2)] for dy in range(2)], "y")
    low_sum = net.reduce([[by_x[dx][dy][:, cut:] for dx in range(2)] for dy in range(2)], "x")
    attn_sum = jnp.concatenate([top_sum, low_sum], axis=0)

    def core_rows(total):
        own = pick(c, (total[:rows], total[rows : 2 * rows]))
        away = pick(c, (total[rows : 2 * rows], total[:rows]))
        return own, net.core(away.astype(bf16)).astype(f32)

    def ff_columns(total):
        own, other = core_rows(total)
        shape = (rows, half_ff // ff_rows, 1, ff_rows)
        return net.order(c, own.reshape(shape), other.reshape(shape), 2).reshape(rows, 2 * half_ff)

    attn_mine, attn_got = core_rows(attn_sum)
    qk_grad = pick(c, (attn_mine, attn_got))
    vo_grad = pick(c, (attn_got, attn_mine))
    gain_out = attn_sum[2 * rows, : 4 * rows].reshape(2, 2, rows)
    gain_out = pick(c, (gain_out[:, 0], gain_out[:, 1]))
    return (
        block_output[None],
        input_grad[None],
        qk_grad[:, :q_cols],
        qk_grad[:, q_cols:],
        vo_grad[:, :k_cols],
        vo_grad[:, k_cols:],
        ff_columns(gate_sum),
        ff_columns(up_sum),
        down_grad,
        gain_out,
    )


def body(
    tokens, segment_ids, norm_gains, w_query, w_key, w_value, w_out, w_gate, w_up, w_down, cotangent
):
    local_rows = tokens.shape[1]
    groups = H // KV
    scale_factor = 1.0 / math.sqrt(HD)
    offset = lax.axis_index("ctx") * local_rows
    column_parts = (
        lax.all_gather(w_query, "ctx", axis=1, tiled=True),
        lax.all_gather(w_key, "ctx", axis=1, tiled=True),
        lax.all_gather(w_value, "ctx", axis=1, tiled=True),
        lax.all_gather(w_out, "ctx", axis=1, tiled=True),
        lax.all_gather(w_gate, "ctx", axis=1, tiled=True),
        lax.all_gather(w_up, "ctx", axis=1, tiled=True),
        lax.all_gather(w_down, "ctx", axis=1, tiled=True),
    )
    forward_set = (
        lax.all_gather(column_parts[0], "dp", axis=0, tiled=True),
        lax.all_gather(column_parts[1], "dp", axis=0, tiled=True),
        lax.all_gather(column_parts[2], "dp", axis=0, tiled=True),
        lax.all_gather(column_parts[3], "dp", axis=0, tiled=True),
        lax.all_gather(column_parts[4], "dp", axis=0, tiled=True),
        lax.all_gather(column_parts[5], "dp", axis=0, tiled=True),
        lax.all_gather(column_parts[6], "dp", axis=0, tiled=True),
        lax.all_gather(norm_gains.astype(jnp.bfloat16), "dp", axis=1, tiled=True).astype(
            norm_gains.dtype
        ),
    )
    query_full, key_full, value_full, out_full, gate_full, up_full, down_full, gains_full = (
        forward_set
    )
    hidden = tokens[0].astype(jnp.float32)
    own_segments = segment_ids[0]
    first_norm = normed(hidden, gains_full[0]).astype(jnp.bfloat16)
    cosine, sine = rope_tables(local_rows, offset, HD)
    query = rotate(matmul(first_norm, query_full).reshape(local_rows, H, HD), cosine, sine).astype(
        jnp.bfloat16
    )
    keys_local = (
        rotate(matmul(first_norm, key_full).reshape(local_rows, KV, HD), cosine, sine)
        .astype(jnp.bfloat16)
        .reshape(local_rows, KV * HD)
    )
    values_local = matmul(first_norm, value_full).astype(jnp.bfloat16)
    key_all, value_all, segment_all = (
        lax.all_gather(keys_local, "ctx", axis=0, tiled=True),
        lax.all_gather(values_local, "ctx", axis=0, tiled=True),
        lax.all_gather(own_segments, "ctx", axis=0, tiled=True),
    )
    length_all = key_all.shape[0]
    key_grid = key_all.reshape(length_all, KV, HD)
    value_grid = value_all.reshape(length_all, KV, HD)
    grouped = query.reshape(local_rows, KV, groups, HD)
    query_places = offset + jnp.arange(local_rows, dtype=jnp.int32)
    key_places = jnp.arange(length_all, dtype=jnp.int32)
    allowed = (key_places[None, :] <= query_places[:, None]) & (
        segment_all[None, :] == own_segments[:, None]
    )
    scores = score_block(grouped, key_grid, scale_factor)
    totals = jnp.sum(jnp.where(allowed, jnp.exp(scores), 0.0), axis=-1, keepdims=True)
    log_total = jnp.log(totals)
    probs = probabilities(scores, allowed, log_total).astype(jnp.bfloat16)
    attended = jnp.einsum("kgts,skd->tkgd", probs, value_grid, preferred_element_type=jnp.float32)
    attended = attended.reshape(local_rows, H * HD).astype(jnp.bfloat16)
    middle = hidden + matmul(attended, out_full)
    second_norm = normed(middle, gains_full[1]).astype(jnp.bfloat16)
    gate = matmul(second_norm, gate_full)
    upward = matmul(second_norm, up_full)
    sigma = jax.nn.sigmoid(gate)
    activated = gate * sigma
    mixed = (activated * upward).astype(jnp.bfloat16)
    block_output = (middle + matmul(mixed, down_full)).astype(jnp.bfloat16)
    query_back, key_back, value_back, out_back, gate_back, up_back, down_back, gains_back = (
        forward_set
    )
    incoming = cotangent[0]
    grad_down = matmul(mixed.T, incoming)
    grad_mixed = matmul(incoming, down_back.T)
    grad_gate = (grad_mixed * upward * sigma * (1.0 + gate * (1.0 - sigma))).astype(jnp.bfloat16)
    grad_upward = (grad_mixed * activated).astype(jnp.bfloat16)
    grad_wgate = matmul(second_norm.T, grad_gate)
    grad_wup = matmul(second_norm.T, grad_upward)
    grad_second = matmul(grad_gate, gate_back.T) + matmul(grad_upward, up_back.T)
    unused, pull_second = jax.vjp(normed, middle, gains_back[1])
    grad_middle_norm, grad_gain_second = pull_second(grad_second)
    grad_middle = incoming.astype(jnp.float32) + grad_middle_norm
    grad_branch = grad_middle.astype(jnp.bfloat16)
    grad_wout = matmul(attended.T, grad_branch)
    grad_attended = (
        matmul(grad_branch, out_back.T).astype(jnp.bfloat16).reshape(local_rows, KV, groups, HD)
    )
    exact_probs = probabilities(score_block(grouped, key_grid, scale_factor), allowed, log_total)
    probs_again = exact_probs.astype(jnp.bfloat16)
    grad_values_all = jnp.einsum(
        "kgts,tkgd->skd", probs_again, grad_attended, preferred_element_type=jnp.float32
    )
    grad_probs = jnp.einsum(
        "tkgd,skd->kgts", grad_attended, value_grid, preferred_element_type=jnp.float32
    )
    row_terms = jnp.sum(exact_probs * grad_probs, axis=-1, keepdims=True)
    grad_scores = (exact_probs * (grad_probs - row_terms) * scale_factor).astype(jnp.bfloat16)
    grad_query = jnp.einsum(
        "kgts,skd->tkgd", grad_scores, key_grid, preferred_element_type=jnp.float32
    )
    grad_query = (
        unrotate(grad_query.reshape(local_rows, H, HD), cosine, sine)
        .reshape(local_rows, H * HD)
        .astype(jnp.bfloat16)
    )
    grad_keys_all = jnp.einsum(
        "kgts,tkgd->skd", grad_scores, grouped, preferred_element_type=jnp.float32
    )
    own_keys, own_values = (
        lax.psum_scatter(
            grad_keys_all.reshape(length_all, KV * HD).astype(jnp.bfloat16),
            "ctx",
            scatter_dimension=0,
            tiled=True,
        ).astype(jnp.float32),
        lax.psum_scatter(
            grad_values_all.reshape(length_all, KV * HD).astype(jnp.bfloat16),
            "ctx",
            scatter_dimension=0,
            tiled=True,
        ).astype(jnp.float32),
    )
    grad_keys = (
        unrotate(own_keys.reshape(local_rows, KV, HD), cosine, sine)
        .reshape(local_rows, KV * HD)
        .astype(jnp.bfloat16)
    )
    grad_values = own_values.astype(jnp.bfloat16)
    grad_wquery = matmul(first_norm.T, grad_query)
    grad_wkey = matmul(first_norm.T, grad_keys)
    grad_wvalue = matmul(first_norm.T, grad_values)
    grad_first = (
        matmul(grad_query, query_back.T)
        + matmul(grad_keys, key_back.T)
        + matmul(grad_values, value_back.T)
    )
    unused_two, pull_first = jax.vjp(normed, hidden, gains_back[0])
    grad_hidden_norm, grad_gain_first = pull_first(grad_first)
    input_grad = grad_middle + grad_hidden_norm
    gain_terms = jnp.stack([grad_gain_first, grad_gain_second])
    gain_copies = jnp.broadcast_to(gain_terms[None], (lax.axis_size("ctx"),) + gain_terms.shape)
    by_cols = (
        lax.psum_scatter(
            grad_wquery.astype(jnp.bfloat16), "ctx", scatter_dimension=1, tiled=True
        ).astype(jnp.float32),
        lax.psum_scatter(
            grad_wkey.astype(jnp.bfloat16), "ctx", scatter_dimension=1, tiled=True
        ).astype(jnp.float32),
        lax.psum_scatter(
            grad_wvalue.astype(jnp.bfloat16), "ctx", scatter_dimension=1, tiled=True
        ).astype(jnp.float32),
        lax.psum_scatter(
            grad_wout.astype(jnp.bfloat16), "ctx", scatter_dimension=1, tiled=True
        ).astype(jnp.float32),
        lax.psum_scatter(
            grad_wgate.astype(jnp.bfloat16), "ctx", scatter_dimension=1, tiled=True
        ).astype(jnp.float32),
        lax.psum_scatter(
            grad_wup.astype(jnp.bfloat16), "ctx", scatter_dimension=1, tiled=True
        ).astype(jnp.float32),
        lax.psum_scatter(
            grad_down.astype(jnp.bfloat16), "ctx", scatter_dimension=1, tiled=True
        ).astype(jnp.float32),
        lax.psum_scatter(
            gain_copies.astype(jnp.bfloat16), "ctx", scatter_dimension=0, tiled=True
        ).astype(jnp.float32),
    )
    finals = (
        lax.psum_scatter(
            by_cols[0].astype(jnp.bfloat16), "dp", scatter_dimension=0, tiled=True
        ).astype(jnp.float32),
        lax.psum_scatter(
            by_cols[1].astype(jnp.bfloat16), "dp", scatter_dimension=0, tiled=True
        ).astype(jnp.float32),
        lax.psum_scatter(
            by_cols[2].astype(jnp.bfloat16), "dp", scatter_dimension=0, tiled=True
        ).astype(jnp.float32),
        lax.psum_scatter(
            by_cols[3].astype(jnp.bfloat16), "dp", scatter_dimension=0, tiled=True
        ).astype(jnp.float32),
        lax.psum_scatter(
            by_cols[4].astype(jnp.bfloat16), "dp", scatter_dimension=0, tiled=True
        ).astype(jnp.float32),
        lax.psum_scatter(
            by_cols[5].astype(jnp.bfloat16), "dp", scatter_dimension=0, tiled=True
        ).astype(jnp.float32),
        lax.psum_scatter(
            by_cols[6].astype(jnp.bfloat16), "dp", scatter_dimension=0, tiled=True
        ).astype(jnp.float32),
        lax.psum_scatter(
            by_cols[7].astype(jnp.bfloat16), "dp", scatter_dimension=2, tiled=True
        ).astype(jnp.float32),
    )
    gain_out = finals[7][0]
    return (
        block_output[None],
        input_grad[None],
        finals[0],
        finals[1],
        finals[2],
        finals[3],
        finals[4],
        finals[5],
        finals[6],
        gain_out,
    )


def solution(mesh):
    two_blocks = mesh.shape["ctx"] == 2 and mesh.shape["dp"] % 4 == 0
    return jax.shard_map(
        fast_body if two_blocks else body,
        mesh=mesh,
        in_specs=(
            P("dp", "ctx", None),
            P("dp", "ctx"),
            P(None, "dp"),
            P("dp", "ctx"),
            P("dp", "ctx"),
            P("dp", "ctx"),
            P("dp", "ctx"),
            P("dp", "ctx"),
            P("dp", "ctx"),
            P("dp", "ctx"),
            P("dp", "ctx", None),
        ),
        out_specs=(
            P("dp", "ctx", None),
            P("dp", "ctx", None),
            P("dp", "ctx"),
            P("dp", "ctx"),
            P("dp", "ctx"),
            P("dp", "ctx"),
            P("dp", "ctx"),
            P("dp", "ctx"),
            P("dp", "ctx"),
            P(None, "dp"),
        ),
        check_vma=False,
    )
```

```python
import math

import jax
import jax.numpy as jnp
from jax import lax
from jax.sharding import PartitionSpec as P


H = 15
KV = 5
HD = 64


norm_eps = 1e-05
rope_base = 100000.0

AXES = ("dp", "ctx")


def normed(hidden, scales):
    factor = lax.rsqrt(jnp.mean(hidden * hidden, axis=-1, keepdims=True) + norm_eps)
    return hidden * factor * scales


def rope_tables(amount, offset, head_size):
    middle = head_size // 2
    inverse_rates = rope_base ** (-(jnp.arange(middle, dtype=jnp.float32) * 2.0) / head_size)
    places = (offset + jnp.arange(amount, dtype=jnp.int32)).astype(jnp.float32)
    angles = places[:, None] * inverse_rates[None, :]
    return (jnp.cos(angles)[:, None, :], jnp.sin(angles)[:, None, :])


def rotate(values, cosine, sine):
    middle = values.shape[-1] // 2
    first_half = values[..., :middle]
    second_half = values[..., middle:]
    return jnp.concatenate(
        [first_half * cosine - second_half * sine, second_half * cosine + first_half * sine],
        axis=-1,
    )


def unrotate(values, cosine, sine):
    middle = values.shape[-1] // 2
    first_half = values[..., :middle]
    second_half = values[..., middle:]
    return jnp.concatenate(
        [first_half * cosine + second_half * sine, second_half * cosine - first_half * sine],
        axis=-1,
    )


def matmul(left, right):
    return jnp.dot(left, right, preferred_element_type=jnp.float32)


def score_block(grouped, key_grid, scale_factor):
    return (
        jnp.einsum("tkgd,skd->kgts", grouped, key_grid, preferred_element_type=jnp.float32)
        * scale_factor
    )


def probabilities(scores, allowed, log_total):
    return jnp.where(allowed, jnp.exp(scores - log_total), 0.0)


bf16 = jnp.bfloat16
f32 = jnp.float32


class Links:
    def __init__(self):
        self.dp = lax.axis_size("dp")
        self.nz = self.dp // 4
        index = lax.axis_index("dp")
        self.y = lax.axis_index("ctx")
        self.c = index % 2
        self.x = (index // 2) % 2
        self.z = index // 4

    def _permute(self, value, target):
        pairs = []
        for z in range(self.nz):
            for x in range(2):
                for c in range(2):
                    for y in range(2):
                        z2, x2, c2, y2 = target(z, x, c, y)
                        pairs.append(
                            (((z * 2 + x) * 2 + c) * 2 + y, ((z2 * 2 + x2) * 2 + c2) * 2 + y2)
                        )
        return lax.ppermute(value, AXES, pairs)

    def core(self, value):
        return self._permute(value, lambda z, x, c, y: (z, x, 1 - c, y))

    def over_x(self, value):
        return self._permute(value, lambda z, x, c, y: (z, 1 - x, c, y))

    def over_y(self, value):
        return self._permute(value, lambda z, x, c, y: (z, x, c, 1 - y))

    def over_z(self, value, step):
        return self._permute(value, lambda z, x, c, y: ((z + step) % self.nz, x, c, y))

    def order(self, flag, own, other, axis):
        return jnp.where(
            flag == 0,
            jnp.concatenate([own, other], axis=axis),
            jnp.concatenate([other, own], axis=axis),
        )

    def gather_z(self, block):
        parts = [block] + [self.over_z(block, k) for k in range(1, self.nz)]
        slots = []
        for slot in range(self.nz):
            distance = (self.z - slot) % self.nz
            value = parts[0]
            for k in range(1, self.nz):
                value = jnp.where(distance == k, parts[k], value)
            slots.append(value)
        return jnp.stack(slots, axis=1)

    def spread(self, line):
        by_x = self.over_x(line)
        by_y = self.over_y(line)
        corner = (self.over_y(by_x[0]), self.over_x(by_y[1]))
        return [[[line[t], by_x[t]], [by_y[t], corner[t]]] for t in range(2)]

    def along_k(self, parts):
        nz, m, n = parts[0].shape
        return self.order(self.x, parts[0][:, None], parts[1][:, None], 1).reshape(nz * 2 * m, n)

    def reduce(self, grads):
        got_y = self.over_y(jnp.stack(grads[0][1]))
        got_x = self.over_x(jnp.stack([grads[1][0][1], grads[1][1][1]]))
        onward_x = (grads[0][0][1].astype(f32) + got_y[1].astype(f32)).astype(bf16)
        onward_y = (grads[1][1][0].astype(f32) + got_x[1].astype(f32)).astype(bf16)
        last_x = self.over_x(onward_x)
        last_y = self.over_y(onward_y)
        line = jnp.stack(
            [
                grads[0][0][0].astype(f32) + got_y[0].astype(f32) + last_x.astype(f32),
                grads[1][0][0].astype(f32) + got_x[0].astype(f32) + last_y.astype(f32),
            ],
            axis=1,
        )
        low = line.astype(bf16)
        total = lax.dynamic_index_in_dim(line, self.z, 0, keepdims=False)
        for k in range(1, self.nz):
            block = lax.dynamic_index_in_dim(low, (self.z + k) % self.nz, 0, keepdims=False)
            arrived = self.over_z(block, k)
            total = total + arrived.astype(f32)
        return total


def pick(flag, pair):
    return jnp.where(flag == 0, pair[0], pair[1])


def fast_pass(
    tokens, segment_ids, norm_gains, w_query, w_key, w_value, w_out, w_gate, w_up, w_down, cotangent
):
    net = Links()
    nz, c, x, y = net.nz, net.c, net.x, net.y
    local_rows = tokens.shape[1]
    width = tokens.shape[2]
    rows = w_query.shape[0]
    groups = H // KV
    scale_factor = 1.0 / math.sqrt(HD)
    q_cols, k_cols = w_query.shape[1], w_key.shape[1]
    attn_cols = q_cols + k_cols
    ff_rows = w_down.shape[0]
    half_ff = w_gate.shape[1] // 2

    mine = tokens[0]
    segments_mine = segment_ids[0]
    segment_row = jnp.pad(
        segments_mine[None].astype(bf16), ((0, 7), (0, width - local_rows))
    )
    facing_pack = net.over_y(jnp.concatenate([mine, segment_row], axis=0))
    facing = facing_pack[:local_rows]
    segments_facing = facing_pack[local_rows, :local_rows].astype(jnp.int32)
    incoming = cotangent[0]
    incoming_got = net.core(incoming)
    incoming_pair = jnp.concatenate([incoming, incoming_got], axis=0)

    def by_core(w):
        return w.reshape(rows, half_ff // ff_rows, 2, ff_rows)

    qk = jnp.concatenate([w_query, w_key], axis=1)
    vo = jnp.concatenate([w_value, w_out], axis=1)
    gate_parts, up_parts = by_core(w_gate), by_core(w_up)
    gate_half = [gate_parts[:, :, i].reshape(rows, half_ff) for i in range(2)]
    up_half = [up_parts[:, :, i].reshape(rows, half_ff) for i in range(2)]
    gains_row = norm_gains.astype(bf16)
    gains_slot = jnp.pad(
        gains_row.reshape(1, 2 * rows), ((0, rows - 1), (0, attn_cols - 2 * rows))
    )
    got = net.core(
        jnp.stack(
            [
                pick(c, (vo, qk)),
                pick(c, (gate_half[1], gate_half[0])),
                pick(c, (up_half[1], up_half[0])),
                gains_slot,
            ]
        )
    )
    got_gains = got[3, 0, : 2 * rows].reshape(2, rows)
    gains_chip = net.order(c, gains_row, got_gains, 1).reshape(1, 4 * rows)
    gains_chip = jnp.pad(gains_chip, ((0, 7), (0, attn_cols - 4 * rows)))
    attn_rows = 2 * rows + 8
    attn_block = jnp.concatenate([net.order(c, pick(c, (qk, vo)), got[0], 0), gains_chip], axis=0)
    attn_pack = attn_block.reshape(2, attn_rows // 2, attn_cols)
    gu_pack = jnp.stack(
        [net.order(c, pick(c, gate_half), got[1], 0), net.order(c, pick(c, up_half), got[2], 0)]
    )
    down_pack = w_down.reshape(2, ff_rows // 2, w_down.shape[1])
    cut_down = ff_rows // 2

    attn_line = net.gather_z(attn_pack)
    gu_line = net.gather_z(gu_pack)
    down_line = net.gather_z(down_pack)
    attn_parts = net.spread(attn_line)
    gu_parts = net.spread(gu_line)
    down_parts = net.spread(down_line)

    def whole(parts):
        return jnp.stack(
            [
                jnp.concatenate(
                    [net.along_k(parts[t][dy]).reshape(nz * 2, -1, parts[0][0][0].shape[2]) for t in range(2)],
                    axis=1,
                )
                for dy in range(2)
            ]
        )

    attn_all = whole(attn_parts)
    gains_all = attn_all[0][:, 2 * rows, : 4 * rows].reshape(nz * 2, 2, 2 * rows)
    gains_full = jnp.transpose(gains_all, (1, 0, 2)).reshape(2, width).astype(f32)
    attn_own = attn_all[:, :, : 2 * rows].reshape(2, width, attn_cols)
    attn_other = net.core(attn_own)
    qk_full = pick(c, (attn_own, attn_other))
    vo_full = pick(c, (attn_other, attn_own))

    gate_all = [net.along_k(gu_parts[0][dy]) for dy in range(2)]
    up_all = [net.along_k(gu_parts[1][dy]) for dy in range(2)]
    down_all = whole(down_parts).reshape(2, 2 * nz * ff_rows, -1)

    def in_order(a, b, axis):
        return net.order(y, a, b, axis)

    both = jnp.concatenate([mine, facing], axis=0).astype(f32)
    hidden = mine.astype(f32)
    first_both = normed(both, gains_full[0]).astype(bf16)
    first_norm = first_both[:local_rows]
    cosine, sine = rope_tables(local_rows, y * local_rows, HD)
    cosine_f, sine_f = rope_tables(local_rows, (1 - y) * local_rows, HD)
    cosine_b = jnp.concatenate([cosine, cosine_f], axis=0)
    sine_b = jnp.concatenate([sine, sine_f], axis=0)
    both_rows = 2 * local_rows
    wq = in_order(qk_full[0][:, :q_cols], qk_full[1][:, :q_cols], 1)
    wk = in_order(qk_full[0][:, q_cols:], qk_full[1][:, q_cols:], 1)
    wv = in_order(vo_full[0][:, :k_cols], vo_full[1][:, :k_cols], 1)
    wo = in_order(vo_full[0][:, k_cols:], vo_full[1][:, k_cols:], 1)
    query = matmul(first_norm, wq)
    query = rotate(query.reshape(local_rows, H, HD), cosine, sine).astype(bf16)
    key_grid = rotate(matmul(first_both, wk).reshape(both_rows, KV, HD), cosine_b, sine_b).astype(
        bf16
    )
    value_grid = matmul(first_both, wv).astype(bf16).reshape(both_rows, KV, HD)
    grouped = query.reshape(local_rows, KV, groups, HD)
    own_places = y * local_rows + jnp.arange(local_rows, dtype=jnp.int32)
    facing_places = (1 - y) * local_rows + jnp.arange(local_rows, dtype=jnp.int32)
    key_places = jnp.concatenate([own_places, facing_places])
    segment_all = jnp.concatenate([segments_mine, segments_facing])
    allowed = (key_places[None, :] <= own_places[:, None]) & (
        segment_all[None, :] == segments_mine[:, None]
    )
    scores = score_block(grouped, key_grid, scale_factor)
    totals = jnp.sum(jnp.where(allowed, jnp.exp(scores), 0.0), axis=-1, keepdims=True)
    log_total = jnp.log(totals)
    exact_probs = probabilities(scores, allowed, log_total)
    probs = exact_probs.astype(bf16)
    attended = jnp.einsum("kgts,skd->tkgd", probs, value_grid, preferred_element_type=f32)
    attended = attended.reshape(local_rows, H * HD).astype(bf16)
    branch = matmul(attended, wo)
    middle = hidden + branch
    second_norm = normed(middle, gains_full[1]).astype(bf16)

    second_got = net.core(second_norm)
    second_pair = jnp.concatenate([second_norm, second_got], axis=0)
    gate = [matmul(second_pair, w) for w in gate_all]
    upward = [matmul(second_pair, w) for w in up_all]
    sigma = [jax.nn.sigmoid(g) for g in gate]
    activated = [g * s for g, s in zip(gate, sigma)]
    mixed = [(a * u).astype(bf16) for a, u in zip(activated, upward)]
    mixed_all = in_order(mixed[0], mixed[1], 1)
    mixed_all, gate, upward = lax.optimization_barrier((mixed_all, gate, upward))
    sigma = [jax.nn.sigmoid(g) for g in gate]
    activated = [g * s for g, s in zip(gate, sigma)]
    partial = [matmul(mixed_all, w) for w in down_all]
    partial = in_order(partial[0], partial[1], 1)
    from_other = net.core(partial[local_rows:].astype(bf16))
    block_output = (middle + partial[:local_rows] + from_other.astype(f32)).astype(bf16)

    def halves(value, count):
        m = value.shape[0] // (count * 2)
        split = value.reshape(count, 2, m, value.shape[1])
        even, odd = split[:, 0], split[:, 1]
        return jnp.where(x == 0, even, odd), jnp.where(x == 0, odd, even)

    def weight_grads(left_t, rights):
        parts = halves(left_t, nz)
        m = parts[0].shape[1]
        return [
            [
                matmul(part.reshape(nz * m, -1), right).astype(bf16).reshape(nz, m, -1)
                for part in parts
            ]
            for right in rights
        ]

    incoming_half = jnp.split(incoming_pair, 2, axis=1)
    incoming_dy = [pick(y, incoming_half), pick(y, incoming_half[::-1])]
    mixed_t = mixed_all.T.reshape(nz * 2, 2, cut_down, both_rows)
    mixed_top_t = mixed_t[:, 0].reshape(nz * 2 * cut_down, both_rows)
    mixed_low_t = mixed_t[:, 1].reshape(nz * 2 * cut_down, both_rows)
    down_grads = [weight_grads(mixed_top_t, incoming_dy), weight_grads(mixed_low_t, incoming_dy)]
    down_grad = net.reduce(down_grads).reshape(ff_rows, -1)
    grad_mixed_all = matmul(incoming_dy[0], down_all[0].T) + matmul(incoming_dy[1], down_all[1].T)
    grad_mixed_half = jnp.split(grad_mixed_all, 2, axis=1)
    grad_mixed = [pick(y, grad_mixed_half), pick(y, grad_mixed_half[::-1])]
    grad_gate = [
        (gm * u * s * (1.0 + g * (1.0 - s))).astype(bf16)
        for gm, u, s, g in zip(grad_mixed, upward, sigma, gate)
    ]
    grad_upward = [(gm * a).astype(bf16) for gm, a in zip(grad_mixed, activated)]
    second_t = second_pair.T
    gu_grads = [weight_grads(second_t, grad_gate), weight_grads(second_t, grad_upward)]
    gu_sum = net.reduce(gu_grads)
    grad_second_pair = (
        matmul(grad_gate[0], gate_all[0].T)
        + matmul(grad_gate[1], gate_all[1].T)
        + matmul(grad_upward[0], up_all[0].T)
        + matmul(grad_upward[1], up_all[1].T)
    )
    grad_second = grad_second_pair[:local_rows] + net.core(
        grad_second_pair[local_rows:].astype(bf16)
    ).astype(f32)
    _, pull_second = jax.vjp(normed, middle, gains_full[1])
    grad_middle_norm, grad_gain_second = pull_second(grad_second)
    grad_middle = incoming.astype(f32) + grad_middle_norm
    grad_branch = grad_middle.astype(bf16)
    grad_attended = matmul(grad_branch, wo.T)
    grad_attended = grad_attended.astype(bf16).reshape(local_rows, KV, groups, HD)
    grad_values_all = jnp.einsum("kgts,tkgd->skd", probs, grad_attended, preferred_element_type=f32)
    grad_probs = jnp.einsum("tkgd,skd->kgts", grad_attended, value_grid, preferred_element_type=f32)
    row_terms = jnp.sum(exact_probs * grad_probs, axis=-1, keepdims=True)
    grad_scores = (exact_probs * (grad_probs - row_terms) * scale_factor).astype(bf16)
    grad_query = jnp.einsum(
        "kgts,skd->tkgd", grad_scores, key_grid, preferred_element_type=f32
    )
    grad_query = (
        unrotate(grad_query.reshape(local_rows, H, HD), cosine, sine)
        .reshape(local_rows, H * HD)
        .astype(bf16)
    )
    grad_keys_all = jnp.einsum("kgts,tkgd->skd", grad_scores, grouped, preferred_element_type=f32)
    grad_kv_all = jnp.concatenate(
        [
            grad_keys_all.reshape(both_rows, KV * HD),
            grad_values_all.reshape(both_rows, KV * HD),
        ],
        axis=1,
    )
    from_facing = net.over_y(grad_kv_all[local_rows:].astype(bf16)).astype(f32)
    grad_kv = grad_kv_all[:local_rows] + from_facing
    grad_keys = (
        unrotate(grad_kv[:, : KV * HD].reshape(local_rows, KV, HD), cosine, sine)
        .reshape(local_rows, KV * HD)
        .astype(bf16)
    )
    grad_values = grad_kv[:, KV * HD :].astype(bf16)
    grad_first = matmul(grad_query, wq.T) + matmul(grad_keys, wk.T) + matmul(grad_values, wv.T)
    _, pull_first = jax.vjp(normed, hidden, gains_full[0])
    grad_hidden_norm, grad_gain_first = pull_first(grad_first)
    input_grad = grad_middle + grad_hidden_norm

    def column_halves(value):
        pair = jnp.split(value, 2, axis=1)
        return pick(y, pair), pick(y, pair[::-1])

    first_t, attended_t = first_norm.T, attended.T
    gq, gk, gv, go = (
        column_halves(g) for g in (grad_query, grad_keys, grad_values, grad_branch)
    )
    gains_terms = jnp.stack([grad_gain_first, grad_gain_second]).reshape(2, nz * 2, 2 * rows)
    gains_terms = jnp.transpose(gains_terms, (1, 0, 2)).reshape(nz * 2, 1, 4 * rows)
    gains_terms = jnp.pad(gains_terms, ((0, 0), (0, 7), (0, attn_cols - 4 * rows))).astype(bf16)

    def with_gains(grad):
        grad = grad.reshape(nz * 2, 2 * rows, attn_cols)
        return jnp.concatenate([grad, gains_terms], axis=1)

    grads_qk = jnp.stack(
        [
            with_gains(
                matmul(first_t, jnp.concatenate([gq[i], gk[i]], axis=1)).astype(bf16)
            )
            for i in range(2)
        ]
    )
    grads_vo = jnp.stack(
        [
            with_gains(
                jnp.concatenate([matmul(first_t, gv[i]), matmul(attended_t, go[i])], axis=1).astype(
                    bf16
                )
            )
            for i in range(2)
        ]
    )
    from_core = net.core(pick(c, (grads_vo, grads_qk)))
    grads_attn = (pick(c, (grads_qk, grads_vo)).astype(f32) + from_core.astype(f32)).astype(bf16)
    split = grads_attn.reshape(2, nz, 2, 2 * rows + 8, attn_cols)
    by_x = (
        jnp.where(x == 0, split[:, :, 0], split[:, :, 1]),
        jnp.where(x == 0, split[:, :, 1], split[:, :, 0]),
    )
    attn_grads = [
        [
            [by_x[dx][dy][:, t * attn_rows // 2 : (t + 1) * attn_rows // 2] for dx in range(2)]
            for dy in range(2)
        ]
        for t in range(2)
    ]
    attn_sum = net.reduce(attn_grads).reshape(attn_rows, attn_cols)

    def core_rows(total):
        low_rows, high_rows = total[..., :rows, :], total[..., rows : 2 * rows, :]
        away = pick(c, (high_rows, low_rows)).astype(bf16)
        return pick(c, (low_rows, high_rows)), net.core(away).astype(f32)

    gu_mine, gu_got = core_rows(gu_sum)
    shape = (2, rows, half_ff // ff_rows, 1, ff_rows)
    gu_grad = net.order(c, gu_mine.reshape(shape), gu_got.reshape(shape), 3).reshape(
        2, rows, 2 * half_ff
    )
    attn_mine, attn_got = core_rows(attn_sum)
    qk_grad = pick(c, (attn_mine, attn_got))
    vo_grad = pick(c, (attn_got, attn_mine))
    gain_out = attn_sum[2 * rows, : 4 * rows].reshape(2, 2, rows)
    gain_out = pick(c, (gain_out[:, 0], gain_out[:, 1]))
    return (
        block_output[None],
        input_grad[None],
        qk_grad[:, :q_cols],
        qk_grad[:, q_cols:],
        vo_grad[:, :k_cols],
        vo_grad[:, k_cols:],
        gu_grad[0],
        gu_grad[1],
        down_grad,
        gain_out,
    )


def fast_body(*args):
    return fast_pass(*args)


def body(
    tokens, segment_ids, norm_gains, w_query, w_key, w_value, w_out, w_gate, w_up, w_down, cotangent
):
    local_rows = tokens.shape[1]
    groups = H // KV
    scale_factor = 1.0 / math.sqrt(HD)
    offset = lax.axis_index("ctx") * local_rows
    column_parts = (
        lax.all_gather(w_query, "ctx", axis=1, tiled=True),
        lax.all_gather(w_key, "ctx", axis=1, tiled=True),
        lax.all_gather(w_value, "ctx", axis=1, tiled=True),
        lax.all_gather(w_out, "ctx", axis=1, tiled=True),
        lax.all_gather(w_gate, "ctx", axis=1, tiled=True),
        lax.all_gather(w_up, "ctx", axis=1, tiled=True),
        lax.all_gather(w_down, "ctx", axis=1, tiled=True),
    )
    forward_set = (
        lax.all_gather(column_parts[0], "dp", axis=0, tiled=True),
        lax.all_gather(column_parts[1], "dp", axis=0, tiled=True),
        lax.all_gather(column_parts[2], "dp", axis=0, tiled=True),
        lax.all_gather(column_parts[3], "dp", axis=0, tiled=True),
        lax.all_gather(column_parts[4], "dp", axis=0, tiled=True),
        lax.all_gather(column_parts[5], "dp", axis=0, tiled=True),
        lax.all_gather(column_parts[6], "dp", axis=0, tiled=True),
        lax.all_gather(norm_gains.astype(jnp.bfloat16), "dp", axis=1, tiled=True).astype(
            norm_gains.dtype
        ),
    )
    query_full, key_full, value_full, out_full, gate_full, up_full, down_full, gains_full = (
        forward_set
    )
    hidden = tokens[0].astype(jnp.float32)
    own_segments = segment_ids[0]
    first_norm = normed(hidden, gains_full[0]).astype(jnp.bfloat16)
    cosine, sine = rope_tables(local_rows, offset, HD)
    query = rotate(matmul(first_norm, query_full).reshape(local_rows, H, HD), cosine, sine).astype(
        jnp.bfloat16
    )
    keys_local = (
        rotate(matmul(first_norm, key_full).reshape(local_rows, KV, HD), cosine, sine)
        .astype(jnp.bfloat16)
        .reshape(local_rows, KV * HD)
    )
    values_local = matmul(first_norm, value_full).astype(jnp.bfloat16)
    key_all, value_all, segment_all = (
        lax.all_gather(keys_local, "ctx", axis=0, tiled=True),
        lax.all_gather(values_local, "ctx", axis=0, tiled=True),
        lax.all_gather(own_segments, "ctx", axis=0, tiled=True),
    )
    length_all = key_all.shape[0]
    key_grid = key_all.reshape(length_all, KV, HD)
    value_grid = value_all.reshape(length_all, KV, HD)
    grouped = query.reshape(local_rows, KV, groups, HD)
    query_places = offset + jnp.arange(local_rows, dtype=jnp.int32)
    key_places = jnp.arange(length_all, dtype=jnp.int32)
    allowed = (key_places[None, :] <= query_places[:, None]) & (
        segment_all[None, :] == own_segments[:, None]
    )
    scores = score_block(grouped, key_grid, scale_factor)
    totals = jnp.sum(jnp.where(allowed, jnp.exp(scores), 0.0), axis=-1, keepdims=True)
    log_total = jnp.log(totals)
    probs = probabilities(scores, allowed, log_total).astype(jnp.bfloat16)
    attended = jnp.einsum("kgts,skd->tkgd", probs, value_grid, preferred_element_type=jnp.float32)
    attended = attended.reshape(local_rows, H * HD).astype(jnp.bfloat16)
    middle = hidden + matmul(attended, out_full)
    second_norm = normed(middle, gains_full[1]).astype(jnp.bfloat16)
    gate = matmul(second_norm, gate_full)
    upward = matmul(second_norm, up_full)
    sigma = jax.nn.sigmoid(gate)
    activated = gate * sigma
    mixed = (activated * upward).astype(jnp.bfloat16)
    block_output = (middle + matmul(mixed, down_full)).astype(jnp.bfloat16)
    query_back, key_back, value_back, out_back, gate_back, up_back, down_back, gains_back = (
        forward_set
    )
    incoming = cotangent[0]
    grad_down = matmul(mixed.T, incoming)
    grad_mixed = matmul(incoming, down_back.T)
    grad_gate = (grad_mixed * upward * sigma * (1.0 + gate * (1.0 - sigma))).astype(jnp.bfloat16)
    grad_upward = (grad_mixed * activated).astype(jnp.bfloat16)
    grad_wgate = matmul(second_norm.T, grad_gate)
    grad_wup = matmul(second_norm.T, grad_upward)
    grad_second = matmul(grad_gate, gate_back.T) + matmul(grad_upward, up_back.T)
    _, pull_second = jax.vjp(normed, middle, gains_back[1])
    grad_middle_norm, grad_gain_second = pull_second(grad_second)
    grad_middle = incoming.astype(jnp.float32) + grad_middle_norm
    grad_branch = grad_middle.astype(jnp.bfloat16)
    grad_wout = matmul(attended.T, grad_branch)
    grad_attended = (
        matmul(grad_branch, out_back.T).astype(jnp.bfloat16).reshape(local_rows, KV, groups, HD)
    )
    exact_probs = probabilities(score_block(grouped, key_grid, scale_factor), allowed, log_total)
    probs_again = exact_probs.astype(jnp.bfloat16)
    grad_values_all = jnp.einsum(
        "kgts,tkgd->skd", probs_again, grad_attended, preferred_element_type=jnp.float32
    )
    grad_probs = jnp.einsum(
        "tkgd,skd->kgts", grad_attended, value_grid, preferred_element_type=jnp.float32
    )
    row_terms = jnp.sum(exact_probs * grad_probs, axis=-1, keepdims=True)
    grad_scores = (exact_probs * (grad_probs - row_terms) * scale_factor).astype(jnp.bfloat16)
    grad_query = jnp.einsum(
        "kgts,skd->tkgd", grad_scores, key_grid, preferred_element_type=jnp.float32
    )
    grad_query = (
        unrotate(grad_query.reshape(local_rows, H, HD), cosine, sine)
        .reshape(local_rows, H * HD)
        .astype(jnp.bfloat16)
    )
    grad_keys_all = jnp.einsum(
        "kgts,tkgd->skd", grad_scores, grouped, preferred_element_type=jnp.float32
    )
    own_keys, own_values = (
        lax.psum_scatter(
            grad_keys_all.reshape(length_all, KV * HD).astype(jnp.bfloat16),
            "ctx",
            scatter_dimension=0,
            tiled=True,
        ).astype(jnp.float32),
        lax.psum_scatter(
            grad_values_all.reshape(length_all, KV * HD).astype(jnp.bfloat16),
            "ctx",
            scatter_dimension=0,
            tiled=True,
        ).astype(jnp.float32),
    )
    grad_keys = (
        unrotate(own_keys.reshape(local_rows, KV, HD), cosine, sine)
        .reshape(local_rows, KV * HD)
        .astype(jnp.bfloat16)
    )
    grad_values = own_values.astype(jnp.bfloat16)
    grad_wquery = matmul(first_norm.T, grad_query)
    grad_wkey = matmul(first_norm.T, grad_keys)
    grad_wvalue = matmul(first_norm.T, grad_values)
    grad_first = (
        matmul(grad_query, query_back.T)
        + matmul(grad_keys, key_back.T)
        + matmul(grad_values, value_back.T)
    )
    _, pull_first = jax.vjp(normed, hidden, gains_back[0])
    grad_hidden_norm, grad_gain_first = pull_first(grad_first)
    input_grad = grad_middle + grad_hidden_norm
    gain_terms = jnp.stack([grad_gain_first, grad_gain_second])
    gain_copies = jnp.broadcast_to(gain_terms[None], (lax.axis_size("ctx"),) + gain_terms.shape)
    by_cols = (
        lax.psum_scatter(
            grad_wquery.astype(jnp.bfloat16), "ctx", scatter_dimension=1, tiled=True
        ).astype(jnp.float32),
        lax.psum_scatter(
            grad_wkey.astype(jnp.bfloat16), "ctx", scatter_dimension=1, tiled=True
        ).astype(jnp.float32),
        lax.psum_scatter(
            grad_wvalue.astype(jnp.bfloat16), "ctx", scatter_dimension=1, tiled=True
        ).astype(jnp.float32),
        lax.psum_scatter(
            grad_wout.astype(jnp.bfloat16), "ctx", scatter_dimension=1, tiled=True
        ).astype(jnp.float32),
        lax.psum_scatter(
            grad_wgate.astype(jnp.bfloat16), "ctx", scatter_dimension=1, tiled=True
        ).astype(jnp.float32),
        lax.psum_scatter(
            grad_wup.astype(jnp.bfloat16), "ctx", scatter_dimension=1, tiled=True
        ).astype(jnp.float32),
        lax.psum_scatter(
            grad_down.astype(jnp.bfloat16), "ctx", scatter_dimension=1, tiled=True
        ).astype(jnp.float32),
        lax.psum_scatter(
            gain_copies.astype(jnp.bfloat16), "ctx", scatter_dimension=0, tiled=True
        ).astype(jnp.float32),
    )
    finals = (
        lax.psum_scatter(
            by_cols[0].astype(jnp.bfloat16), "dp", scatter_dimension=0, tiled=True
        ).astype(jnp.float32),
        lax.psum_scatter(
            by_cols[1].astype(jnp.bfloat16), "dp", scatter_dimension=0, tiled=True
        ).astype(jnp.float32),
        lax.psum_scatter(
            by_cols[2].astype(jnp.bfloat16), "dp", scatter_dimension=0, tiled=True
        ).astype(jnp.float32),
        lax.psum_scatter(
            by_cols[3].astype(jnp.bfloat16), "dp", scatter_dimension=0, tiled=True
        ).astype(jnp.float32),
        lax.psum_scatter(
            by_cols[4].astype(jnp.bfloat16), "dp", scatter_dimension=0, tiled=True
        ).astype(jnp.float32),
        lax.psum_scatter(
            by_cols[5].astype(jnp.bfloat16), "dp", scatter_dimension=0, tiled=True
        ).astype(jnp.float32),
        lax.psum_scatter(
            by_cols[6].astype(jnp.bfloat16), "dp", scatter_dimension=0, tiled=True
        ).astype(jnp.float32),
        lax.psum_scatter(
            by_cols[7].astype(jnp.bfloat16), "dp", scatter_dimension=2, tiled=True
        ).astype(jnp.float32),
    )
    gain_out = finals[7][0]
    return (
        block_output[None],
        input_grad[None],
        finals[0],
        finals[1],
        finals[2],
        finals[3],
        finals[4],
        finals[5],
        finals[6],
        gain_out,
    )


def solution(mesh):
    two_blocks = mesh.shape["ctx"] == 2 and mesh.shape["dp"] % 4 == 0
    return jax.shard_map(
        fast_body if two_blocks else body,
        mesh=mesh,
        in_specs=(
            P("dp", "ctx", None),
            P("dp", "ctx"),
            P(None, "dp"),
            P("dp", "ctx"),
            P("dp", "ctx"),
            P("dp", "ctx"),
            P("dp", "ctx"),
            P("dp", "ctx"),
            P("dp", "ctx"),
            P("dp", "ctx"),
            P("dp", "ctx", None),
        ),
        out_specs=(
            P("dp", "ctx", None),
            P("dp", "ctx", None),
            P("dp", "ctx"),
            P("dp", "ctx"),
            P("dp", "ctx"),
            P("dp", "ctx"),
            P("dp", "ctx"),
            P("dp", "ctx"),
            P("dp", "ctx"),
            P(None, "dp"),
        ),
        check_vma=False,
    )
```

```python
import functools
import math

import jax
import jax.numpy as jnp
from jax import lax
from jax.experimental import pallas as pl
from jax.experimental.pallas import tpu as pltpu
from jax.sharding import PartitionSpec as P


H = 15
KV = 5
HD = 64


norm_eps = 1e-05
rope_base = 100000.0

AXES = ("dp", "ctx")


def normed(hidden, scales):
    factor = lax.rsqrt(jnp.mean(hidden * hidden, axis=-1, keepdims=True) + norm_eps)
    return hidden * factor * scales


def rope_tables(amount, offset, head_size):
    middle = head_size // 2
    inverse_rates = rope_base ** (-(jnp.arange(middle, dtype=jnp.float32) * 2.0) / head_size)
    places = (offset + jnp.arange(amount, dtype=jnp.int32)).astype(jnp.float32)
    angles = places[:, None] * inverse_rates[None, :]
    return (jnp.cos(angles)[:, None, :], jnp.sin(angles)[:, None, :])


def rotate(values, cosine, sine):
    middle = values.shape[-1] // 2
    first_half = values[..., :middle]
    second_half = values[..., middle:]
    return jnp.concatenate(
        [first_half * cosine - second_half * sine, second_half * cosine + first_half * sine],
        axis=-1,
    )


def unrotate(values, cosine, sine):
    middle = values.shape[-1] // 2
    first_half = values[..., :middle]
    second_half = values[..., middle:]
    return jnp.concatenate(
        [first_half * cosine + second_half * sine, second_half * cosine - first_half * sine],
        axis=-1,
    )


def matmul(left, right):
    return jnp.dot(left, right, preferred_element_type=jnp.float32)


def score_block(grouped, key_grid, scale_factor):
    return (
        jnp.einsum("tkgd,skd->kgts", grouped, key_grid, preferred_element_type=jnp.float32)
        * scale_factor
    )


def probabilities(scores, allowed, log_total):
    return jnp.where(allowed, jnp.exp(scores - log_total), 0.0)


bf16 = jnp.bfloat16
f32 = jnp.float32


class Links:
    def __init__(self):
        self.dp = lax.axis_size("dp")
        self.nz = self.dp // 4
        index = lax.axis_index("dp")
        self.y = lax.axis_index("ctx")
        self.c = index % 2
        self.x = (index // 2) % 2
        self.z = index // 4

    def _permute(self, value, target):
        pairs = []
        for z in range(self.nz):
            for x in range(2):
                for c in range(2):
                    for y in range(2):
                        z2, x2, c2, y2 = target(z, x, c, y)
                        pairs.append(
                            (((z * 2 + x) * 2 + c) * 2 + y, ((z2 * 2 + x2) * 2 + c2) * 2 + y2)
                        )
        return lax.ppermute(value, AXES, pairs)

    def core(self, value):
        return self._permute(value, lambda z, x, c, y: (z, x, 1 - c, y))

    def over_x(self, value):
        return self._permute(value, lambda z, x, c, y: (z, 1 - x, c, y))

    def over_y(self, value):
        return self._permute(value, lambda z, x, c, y: (z, x, c, 1 - y))

    def over_z(self, value, step):
        return self._permute(value, lambda z, x, c, y: ((z + step) % self.nz, x, c, y))

    def order(self, flag, own, other, axis):
        return jnp.where(
            flag == 0,
            jnp.concatenate([own, other], axis=axis),
            jnp.concatenate([other, own], axis=axis),
        )

    def gather_z(self, block):
        parts = [block] + [self.over_z(block, k) for k in range(1, self.nz)]
        slots = []
        for slot in range(self.nz):
            distance = (self.z - slot) % self.nz
            value = parts[0]
            for k in range(1, self.nz):
                value = jnp.where(distance == k, parts[k], value)
            slots.append(value)
        return jnp.stack(slots, axis=1)

    def spread(self, line):
        by_x = self.over_x(line)
        by_y = self.over_y(line)
        corners = self.over_y(by_x[0]), self.over_x(by_y[1])
        return line, by_x, by_y, *corners

    def reduce(self, parts):
        send_y, send_x, by_x, by_y, own = parts
        got_y = self.over_y(send_y)
        got_x = self.over_x(send_x)
        onward_x = (by_x.astype(f32) + got_y[1].astype(f32)).astype(bf16)
        onward_y = (by_y.astype(f32) + got_x[1].astype(f32)).astype(bf16)
        last_x = self.over_x(onward_x)
        last_y = self.over_y(onward_y)
        line = jnp.stack(
            [
                own[0].astype(f32) + got_y[0].astype(f32) + last_x.astype(f32),
                own[1].astype(f32) + got_x[0].astype(f32) + last_y.astype(f32),
            ],
            axis=1,
        )
        low = line.astype(bf16)
        total = lax.dynamic_index_in_dim(line, self.z, 0, keepdims=False)
        for k in range(1, self.nz):
            block = lax.dynamic_index_in_dim(low, (self.z + k) % self.nz, 0, keepdims=False)
            arrived = self.over_z(block, k)
            total = total + arrived.astype(f32)
        return total


def pick(flag, pair):
    return jnp.where(flag == 0, pair[0], pair[1])


def padded_columns(count, block, wide, offset, total):
    target = jnp.arange(count // block * wide, dtype=jnp.int32)[None, :]
    lane = target % wide
    source = jnp.where(lane < block, offset + target // wide * block + lane, -1)
    source = lax.optimization_barrier(source)
    return (jnp.arange(total, dtype=jnp.int32)[:, None] == source).astype(bf16)


def dot_t(left, right):
    return lax.dot_general(left, right, (((0,), (0,)), ((), ())), preferred_element_type=f32)


def dot_nt(left, right):
    return lax.dot_general(left, right, (((1,), (1,)), ((), ())), preferred_element_type=f32)


def swapped(value):
    lanes = value.shape[1]
    lane = lax.broadcasted_iota(jnp.int32, value.shape, 1) % HD
    up = pltpu.roll(value, lanes - HD // 2, 1)
    down = pltpu.roll(value, HD // 2, 1)
    return jnp.where(lane < HD // 2, up, down)


def wide_table(table, lanes):
    return jnp.concatenate([table] * (lanes // table.shape[1]), axis=1)


def attention_forward(
    dims, place_ref, pad_ref, pick_ref, mine_ref, facing_ref, allowed_ref, cos_ref, sin_ref, *refs
):
    nz, rows, width, q_cols, k_cols = dims
    pieces, refs = refs[:10], refs[10:]
    (w_ref, wo_ref, gains_ref, x_ref, q_ref, k_ref, v_ref, p_ref, att_ref, middle_ref, second_ref) = refs[:11]
    wide_q, wide_k = refs[11:]
    c, x, y = place_ref[0], place_ref[1], place_ref[2]
    tokens = mine_ref.shape[0]
    for own in range(2):
        line, by_x, by_y, corner_0, corner_1 = pieces[own * 5 : own * 5 + 5]
        which = jnp.where(c == own, 0, 1)

        def store(t, y, z, x, piece, which=which):
            w_ref[which, y, z, x, t * 64 : (t + 1) * 64, :] = piece

        assemble(store, x, y, nz, line, by_x, by_y, corner_0, corner_1)
    gains = [[], []]
    for z in range(nz):
        for p in range(2):
            low, high = (w_ref[0, 0, z, p, at - 8 : at, :][4:5].astype(f32) for at in (64, 128))
            for i in range(2):
                gains[i].append((low + high)[:, i * 128 : (i + 1) * 128])
    gains = [jnp.concatenate(g, axis=1) for g in gains]
    gains_ref[...] = jnp.concatenate(gains + [jnp.zeros_like(gains[0])] * 6, axis=0)
    blank = jnp.zeros((64 - rows, w_ref.shape[-1]), bf16)

    @pl.loop(0, nz)
    def _(z):
        for s in range(2):
            for half in range(2):
                for p in range(2):
                    for at in (rows, rows + 64):
                        w_ref[s, half, z, p, at : at + 64 - rows, :] = blank

    hidden = matmul(jnp.concatenate([mine_ref[...], facing_ref[...]], axis=0), pad_ref[...])
    factor = lax.rsqrt(jnp.sum(hidden * hidden, axis=1, keepdims=True) / width + norm_eps)
    first = (hidden * factor * gains[0]).astype(bf16)
    x_ref[...] = first
    deep = nz * 2 * 128
    wide_q[...] = jnp.zeros_like(wide_q)
    wide_k[...] = jnp.zeros_like(wide_k)
    for half in range(2):
        both = matmul(first, w_ref[0, half].reshape(deep, q_cols + k_cols))
        wide_q[:, half * q_cols : (half + 1) * q_cols] = both[:tokens, :q_cols]
        wide_k[:, half * k_cols : (half + 1) * k_cols] = both[:, q_cols:]
        values = matmul(first, w_ref[1, half].reshape(deep, q_cols + k_cols)[:, :k_cols])
        v_ref[:, half * k_cols : (half + 1) * k_cols] = values.astype(bf16)
    cosine, sine = cos_ref[...], sin_ref[...]
    lanes = wide_q.shape[1]
    query = wide_q[...]
    query = query * wide_table(cosine[:tokens], lanes) + swapped(query) * wide_table(
        sine[:tokens], lanes
    )
    q_ref[...] = query.astype(bf16)
    lanes = wide_k.shape[1]
    keys = wide_k[...]
    keys = keys * wide_table(cosine, lanes) + swapped(keys) * wide_table(sine, lanes)
    k_ref[...] = keys.astype(bf16)
    groups = H // KV
    allowed = jnp.concatenate([allowed_ref[...]] * groups, axis=0) > 0
    for g in range(KV):
        heads = [
            q_ref[:, (g * groups + i) * HD : (g * groups + i + 1) * HD] for i in range(groups)
        ]
        scores = dot_nt(jnp.concatenate(heads, axis=0), k_ref[:, g * HD : (g + 1) * HD])
        scores = scores * (1.0 / math.sqrt(HD))
        totals = jnp.sum(jnp.where(allowed, jnp.exp(scores), 0.0), axis=1, keepdims=True)
        probs = jnp.where(allowed, jnp.exp(scores - jnp.log(totals)), 0.0)
        p_ref[g] = probs
        out = matmul(probs.astype(bf16), v_ref[:, g * HD : (g + 1) * HD])
        for i in range(groups):
            j = g * groups + i
            wide_q[:, j * HD : (j + 1) * HD] = out[i * tokens : (i + 1) * tokens]
    attended = matmul(wide_q[:, :width].astype(bf16), pad_ref[...]).astype(bf16)
    att_ref[...] = attended
    outs = []
    for half in range(2):
        w_out = matmul(w_ref[1, half].reshape(deep, q_cols + k_cols), pick_ref[...]).astype(bf16)
        wo_ref[half] = w_out
        outs.append(matmul(attended, w_out))
    middle = hidden[:tokens] + jnp.concatenate(outs, axis=1)
    middle_ref[...] = middle
    factor = lax.rsqrt(jnp.sum(middle * middle, axis=1, keepdims=True) / width + norm_eps)
    second_ref[...] = (middle * factor * gains[1]).astype(bf16)


def deal(item, x, y, nz, send_y, send_x, by_x, by_y, own):
    @pl.loop(0, nz)
    def _(z):
        for d in range(2):
            send_y[d, z] = item(0, 1 - y, z, x ^ d)
            send_x[d, z] = item(1, y ^ d, z, 1 - x)
            own[d, z] = item(d, y, z, x)
        by_x[z] = item(0, y, z, 1 - x)
        by_y[z] = item(1, 1 - y, z, x)


def pack_shapes(nz, *block):
    two, one = ((2, nz, *block), bf16), ((nz, *block), bf16)
    return [two, two, one, one, two]


def assemble(store, x, y, nz, line, by_x, by_y, corner_0, corner_1):
    @pl.loop(0, nz)
    def _(z):
        for t in range(2):
            corner = (corner_0, corner_1)[t]
            for dy in range(2):
                for dx in range(2):
                    piece = corner[z] if dy and dx else (line, by_x, by_y)[dx + 2 * dy][t, z]
                    store(t, y ^ dy, z, x ^ dx, piece)


def assemble_gate_up(w_ref, x, y, nz, gate_parts, up_parts):
    for which, parts in enumerate((gate_parts, up_parts)):

        def store(t, y, z, x, piece, which=which):
            w_ref[which, y, z, x, t * 64 : (t + 1) * 64, :] = piece

        assemble(store, x, y, nz, *parts)


def feed_forward(dims, place_ref, second_ref, got_ref, cot_ref, *refs):
    nz, ff_rows = dims
    x, y = place_ref[1], place_ref[2]
    (gate_ref, up_ref, mixed_ref, *dealt), (w_ref, sums) = refs[10:18], refs[18:]
    assemble_gate_up(w_ref, x, y, nz, refs[:5], refs[5:10])
    pair = jnp.concatenate([second_ref[...], got_ref[...]], axis=0)
    deep, n = nz * 2 * 128, w_ref.shape[-1]
    part, count = ff_rows // 2, n // ff_rows

    @pl.loop(0, 2)
    def _(half):
        gate = matmul(pair, w_ref[0, half].reshape(deep, n))
        upward = matmul(pair, w_ref[1, half].reshape(deep, n))
        gate_ref[half] = gate
        up_ref[half] = upward
        sigma = 1.0 / (1.0 + jnp.exp(-gate))
        mixed = (gate * sigma * upward).astype(bf16)
        mixed_ref[half] = mixed
        for columns in range(2):
            grads = dot_t(mixed, cot_ref[columns]).astype(bf16)
            for block in range(count):
                for t in range(2):
                    at = block * ff_rows + t * part
                    z = half * (count // 2) + block // 2
                    sums[t, columns, z, block % 2] = grads[at : at + part]

    deal(lambda t, y, z, x: sums[t, y, z, x], x, y, nz, *dealt)


def feed_backward(dims, place_ref, pad_ref, second_ref, got_ref, cot_ref, gate_ref, up_ref, mixed_ref, *refs):
    nz, ff_rows = dims
    x, y = place_ref[1], place_ref[2]
    (out_ref, out_away_ref, back_ref, back_away_ref, *dealt) = refs[15:24]
    (w_ref, d_ref, sums, back, out) = refs[24:]
    part = ff_rows // 2

    def store(t, y, z, x, piece):
        d_ref[y, z, x, t * part : (t + 1) * part, :] = piece

    assemble(store, x, y, nz, *refs[10:15])
    assemble_gate_up(w_ref, x, y, nz, refs[:5], refs[5:10])
    tokens = second_ref.shape[0]
    pair = jnp.concatenate([second_ref[...], got_ref[...]], axis=0)
    deep, n = nz * 2 * 128, w_ref.shape[-1]
    lanes = out.shape[1] // 2
    back[...] = jnp.zeros_like(back)
    out[...] = jnp.zeros_like(out)

    @pl.loop(0, 2)
    def _(half):
        mine = pl.ds(half * (nz // 2), nz // 2)
        down = [d_ref[columns, mine].reshape(n, d_ref.shape[-1]) for columns in range(2)]
        gm = dot_nt(cot_ref[0], down[0]) + dot_nt(cot_ref[1], down[1])
        gate, upward = gate_ref[half], up_ref[half]
        sigma = 1.0 / (1.0 + jnp.exp(-gate))
        grad_gate = (gm * upward * sigma * (1.0 + gate * (1.0 - sigma))).astype(bf16)
        grad_up = (gm * (gate * sigma)).astype(bf16)
        for which, grad in enumerate((grad_gate, grad_up)):
            total = dot_t(pair, grad).astype(bf16)
            for z in range(nz):
                for p in range(2):
                    for t in range(2):
                        at = ((z * 2 + p) * 2 + t) * 64
                        sums[t, half, z, p, which] = total[at : at + 64]
            back[...] += dot_nt(grad, w_ref[which, half].reshape(deep, n))
        for columns in range(2):
            wide = matmul(down[columns], pad_ref[...]).astype(bf16)
            out[:, columns * lanes : (columns + 1) * lanes] += matmul(mixed_ref[half], wide)

    deal(lambda t, y, z, x: sums[t, y, z, x], x, y, nz, *dealt)
    back_ref[...] = back[:tokens]
    back_away_ref[...] = back[tokens:].astype(bf16)
    out_ref[...] = out[:tokens]
    out_away_ref[...] = out[tokens:].astype(bf16)


def attention_backward(
    dims, place_ref, pad_ref, cot_ref, mine_ref, facing_ref, cos_ref, sin_ref, back_ref, back_got_ref, w_ref, wo_ref,
    gains_ref, x_ref, q_ref, k_ref, v_ref, p_ref, att_ref, middle_ref, keep_ref, away_ref, grad_middle_ref, first_ref,
    first_away_ref, wide_q, wide_k, wide_v, wide_g, sums, lefts, rights, outs, back,
):
    nz, rows, width, q_cols, k_cols = dims
    c, x, y = place_ref[0], place_ref[1], place_ref[2]
    tokens = middle_ref.shape[0]
    deep = nz * 2 * 128
    pad = pad_ref[...]
    gains = gains_ref[...]
    middle = middle_ref[...]
    factor = lax.rsqrt(jnp.sum(middle * middle, axis=1, keepdims=True) / width + norm_eps)
    incoming = back_ref[...] + back_got_ref[...].astype(f32)
    gain_second = jnp.sum(incoming * middle * factor, axis=0, keepdims=True)
    scaled = incoming * gains[1:2]
    mean = jnp.sum(scaled * middle, axis=1, keepdims=True) / width
    grad_middle = (
        matmul(cot_ref[...], pad) + factor * scaled - middle * (factor * factor * factor * mean)
    )
    grad_middle_ref[...] = grad_middle
    branch = grad_middle.astype(bf16)
    half_lanes = wo_ref.shape[-1]
    grad_att = dot_nt(branch[:, :half_lanes], wo_ref[0]) + dot_nt(branch[:, half_lanes:], wo_ref[1])
    grad_att = dot_nt(grad_att.astype(bf16), pad).astype(bf16)
    groups = H // KV
    wide_q[...] = jnp.zeros_like(wide_q)
    wide_k[...] = jnp.zeros_like(wide_k)
    wide_g[:, :width] = grad_att
    for g in range(KV):
        at = slice(g * HD, (g + 1) * HD)
        heads = [slice((g * groups + i) * HD, (g * groups + i + 1) * HD) for i in range(groups)]
        grad = jnp.concatenate([wide_g[:, h] for h in heads], axis=0)
        query = jnp.concatenate([q_ref[:, h] for h in heads], axis=0)
        probs = p_ref[g]
        wide_v[:, at] = dot_t(probs.astype(bf16), grad)
        grad_probs = dot_nt(grad, v_ref[:, at])
        row = jnp.sum(probs * grad_probs, axis=1, keepdims=True)
        grad_scores = (probs * (grad_probs - row) * (1.0 / math.sqrt(HD))).astype(bf16)
        wide_k[:, at] = dot_t(grad_scores, query)
        out = matmul(grad_scores, k_ref[:, at])
        for i in range(groups):
            wide_q[:, heads[i]] = out[i * tokens : (i + 1) * tokens]
    cosine, sine = cos_ref[...], sin_ref[...]
    lanes = wide_q.shape[1]
    value = wide_q[...]
    value = value * wide_table(cosine[:tokens], lanes) - swapped(value) * wide_table(
        sine[:tokens], lanes
    )
    wide_q[...] = value
    lanes = wide_k.shape[1]
    value = wide_k[...]
    value = value * wide_table(cosine, lanes) - swapped(value) * wide_table(sine, lanes)
    wide_k[...] = value
    plain = dot_nt(branch, pad)
    first = x_ref[...]
    attended = att_ref[...]
    zeros_q = jnp.zeros((tokens, q_cols), f32)
    zeros_o = jnp.zeros((2 * tokens, q_cols), f32)
    zeros_v = jnp.zeros((tokens, k_cols), f32)
    n = q_cols + k_cols
    for half in range(2):
        of_q = jnp.concatenate([wide_q[:, half * q_cols : (half + 1) * q_cols], zeros_q], axis=0)
        of_k = wide_k[:, half * k_cols : (half + 1) * k_cols]
        of_v = wide_v[:, half * k_cols : (half + 1) * k_cols]
        of_o = plain[:, half * q_cols : (half + 1) * q_cols]
        lefts[half] = jnp.concatenate([of_q, of_k], axis=1).astype(bf16)
        rights[half] = jnp.concatenate([of_v, zeros_o], axis=1).astype(bf16)
        outs[half] = jnp.concatenate([zeros_v, of_o], axis=1).astype(bf16)
    back[...] = jnp.zeros_like(back)

    @pl.loop(0, 2)
    def _(half):
        left, right = lefts[half], rights[half]
        totals = (dot_t(first, left), dot_t(first, right) + dot_t(attended, outs[half]))
        for s in range(2):
            total = totals[s].astype(bf16)
            for z in range(nz):
                for p in range(2):
                    for t in range(2):
                        at = ((z * 2 + p) * 2 + t) * 64
                        sums[s, t, half, z, p] = total[at : at + 64]
            back[...] += dot_nt((left, right)[s], w_ref[s, half].reshape(deep, n))

    hidden = matmul(jnp.concatenate([mine_ref[...], facing_ref[...]], axis=0), pad)
    factor = lax.rsqrt(jnp.sum(hidden * hidden, axis=1, keepdims=True) / width + norm_eps)
    gain_first = jnp.sum(back[...] * hidden * factor, axis=0, keepdims=True)
    first_ref[...] = back[:tokens]
    first_away_ref[...] = back[tokens:].astype(bf16)
    for z in range(nz):
        for p in range(2):
            lane = slice((z * 2 + p) * 128, (z * 2 + p + 1) * 128)
            gain_row = jnp.concatenate(
                [gain_first[:, lane], gain_second[:, lane], jnp.zeros((1, n - 256), f32)], axis=1
            )
            gain_rows = jnp.concatenate(
                [gain_row, jnp.zeros((63 - rows, n), f32)], axis=0
            ).astype(bf16)
            for half in range(2):
                for s in range(2):
                    for t in range(2):
                        sums[s, t, half, z, p, rows:64, :] = gain_rows
    for which, ref in ((c, keep_ref), (1 - c, away_ref)):
        views = (ref.at[0:2], ref.at[2:4], ref.at[4], ref.at[5], ref.at[6:8])
        deal(lambda t, y, z, x, s=which: sums[s, t, y, z, x], x, y, nz, *views)


def run_kernel(body, inputs, outs, scratch):
    moved = sum(math.prod(a.shape) * a.dtype.itemsize for a in inputs)
    vmem = pl.BlockSpec(memory_space=pltpu.VMEM)
    return pl.pallas_call(
        body,
        out_shape=[jax.ShapeDtypeStruct(shape, kind) for shape, kind in outs],
        in_specs=[pl.BlockSpec(memory_space=pltpu.SMEM)] + [vmem] * (len(inputs) - 1),
        out_specs=[vmem] * len(outs),
        scratch_shapes=scratch,
        compiler_params=pltpu.CompilerParams(vmem_limit_bytes=60 << 20),
        cost_estimate=pl.CostEstimate(flops=2 * 10**9, bytes_accessed=moved, transcendentals=0),
    )(*inputs)


def fast_pass(
    tokens, segment_ids, norm_gains, w_query, w_key, w_value, w_out, w_gate, w_up, w_down, cotangent
):
    net = Links()
    nz, c, x, y = net.nz, net.c, net.x, net.y
    local_rows = tokens.shape[1]
    width = tokens.shape[2]
    rows = w_query.shape[0]
    groups = H // KV
    q_cols, k_cols, o_cols = w_query.shape[1], w_key.shape[1], w_out.shape[1]
    attn_cols = q_cols + k_cols
    ff_rows = w_down.shape[0]
    half_ff = w_gate.shape[1] // 2

    mine = tokens[0]
    segments_mine = segment_ids[0]
    segment_row = jnp.pad(
        segments_mine[None].astype(bf16), ((0, 7), (0, width - local_rows))
    )
    facing_pack = net.over_y(jnp.concatenate([mine, segment_row], axis=0))
    facing = facing_pack[:local_rows]
    segments_facing = facing_pack[local_rows, :local_rows].astype(jnp.int32)
    incoming = cotangent[0]
    incoming_got = net.core(incoming)
    incoming_pair = jnp.concatenate([incoming, incoming_got], axis=0)

    def by_core(w):
        return w.reshape(rows, half_ff // ff_rows, 2, ff_rows)

    qk = jnp.concatenate([w_query, w_key], axis=1)
    vo = jnp.concatenate([w_value, w_out], axis=1)
    gate_parts, up_parts = by_core(w_gate), by_core(w_up)
    gate_half = [gate_parts[:, :, i].reshape(rows, half_ff) for i in range(2)]
    up_half = [up_parts[:, :, i].reshape(rows, half_ff) for i in range(2)]
    gains_row = jnp.pad(norm_gains.astype(bf16), ((0, 0), (0, 64 - rows)))
    gains_row = net.order(c, gains_row, jnp.zeros_like(gains_row), 1).reshape(1, 256)
    gains_row = jnp.pad(gains_row, ((0, 63 - rows), (0, attn_cols - 256)))

    def with_gains(w):
        return jnp.concatenate([w, gains_row], axis=0)

    def tall(w):
        return jnp.pad(w, ((0, 64 - rows), (0, 0)))

    got = net.core(
        jnp.stack(
            [
                with_gains(pick(c, (vo, qk))),
                tall(pick(c, (gate_half[1], gate_half[0]))),
                tall(pick(c, (up_half[1], up_half[0]))),
            ]
        )
    )
    attn_rows = 64

    def chip_pack(own, other):
        return net.order(c, own[None], other[None], 0)

    attn_pack = chip_pack(with_gains(pick(c, (qk, vo))), got[0])
    gate_pack = chip_pack(tall(pick(c, gate_half)), got[1])
    up_pack = chip_pack(tall(pick(c, up_half)), got[2])
    down_pack = w_down.reshape(2, ff_rows // 2, w_down.shape[1])

    attn_line = net.gather_z(attn_pack)
    gate_line = net.gather_z(gate_pack)
    up_line = net.gather_z(up_pack)
    down_line = net.gather_z(down_pack)
    attn_own = net.spread(attn_line)
    attn_other = [net.core(piece) for piece in attn_own]
    gate_parts = net.spread(gate_line)
    up_parts = net.spread(up_line)
    down_parts = net.spread(down_line)

    place = jnp.stack([c, x, y]).astype(jnp.int32)
    both_rows = 2 * local_rows
    blocks = nz * 2
    lanes = blocks * 128
    deep = blocks * 128
    pad = padded_columns(width, rows, 64, 0, width)
    pad_half = padded_columns(o_cols, rows, 64, 0, o_cols)
    pick_half = padded_columns(o_cols, rows, 64, k_cols, attn_cols)
    tables = [
        rope_tables(local_rows, start, HD) for start in (y * local_rows, (1 - y) * local_rows)
    ]
    cosine = jnp.concatenate([t[0][:, 0] for t in tables], axis=0)
    sine = jnp.concatenate([t[1][:, 0] for t in tables], axis=0)
    cosine = jnp.concatenate([cosine] * 4, axis=1)
    sine = jnp.concatenate([-sine, sine] * 2, axis=1)
    own_places = y * local_rows + jnp.arange(local_rows, dtype=jnp.int32)
    facing_places = (1 - y) * local_rows + jnp.arange(local_rows, dtype=jnp.int32)
    key_places = jnp.concatenate([own_places, facing_places])
    segment_all = jnp.concatenate([segments_mine, segments_facing])
    allowed = (
        (key_places[None, :] <= own_places[:, None])
        & (segment_all[None, :] == segments_mine[:, None])
    ).astype(f32)
    dims = (nz, rows, width, q_cols, k_cols)
    wide_k = KV * HD + 64
    (w_attn, w_out_wide, gains, first_norm, query, keys, values, probs, attended, middle, second_norm) = (
        run_kernel(
            functools.partial(attention_forward, dims),
            (place, pad, pick_half, mine, facing, allowed, cosine, sine, *attn_own, *attn_other),
            [
                ((2, 2, nz, 2, 128, attn_cols), bf16),
                ((2, deep, lanes // 2), bf16),
                ((8, lanes), f32),
                ((both_rows, lanes), bf16),
                ((local_rows, lanes), bf16),
                ((both_rows, wide_k), bf16),
                ((both_rows, KV * HD), bf16),
                ((KV, groups * local_rows, both_rows), f32),
                ((local_rows, lanes), bf16),
                ((local_rows, lanes), f32),
                ((local_rows, lanes), bf16),
            ],
            [pltpu.VMEM((local_rows, lanes), f32), pltpu.VMEM((both_rows, wide_k), f32)],
        )
    )

    second_got = net.core(second_norm)
    incoming_halves = jnp.stack(jnp.split(incoming_pair, 2, axis=1))
    ff_dims = (nz, ff_rows)
    chip_w = pltpu.VMEM((2, 2, nz, 2, 128, half_ff), bf16)
    gate, upward, mixed, *down_grads = run_kernel(
        functools.partial(feed_forward, ff_dims),
        (place, second_norm, second_got, incoming_halves, *gate_parts, *up_parts),
        [
            ((2, both_rows, half_ff), f32),
            ((2, both_rows, half_ff), f32),
            ((2, both_rows, half_ff), bf16),
            *pack_shapes(nz, ff_rows // 2, o_cols),
        ],
        [chip_w, pltpu.VMEM((2, 2, nz, 2, ff_rows // 2, o_cols), bf16)],
    )
    down_grad = net.reduce(down_grads).reshape(ff_rows, -1)
    out_mine, out_away, back_mine, back_away, *gu_grads = run_kernel(
        functools.partial(feed_backward, ff_dims),
        (place, pad_half, second_norm, second_got, incoming_halves, gate, upward, mixed,
         *gate_parts, *up_parts, *down_parts),
        [
            ((local_rows, lanes), f32),
            ((local_rows, lanes), bf16),
            ((local_rows, lanes), f32),
            ((local_rows, lanes), bf16),
            *pack_shapes(nz, 2, 64, half_ff),
        ],
        [
            chip_w,
            pltpu.VMEM((2, nz, 2, ff_rows, o_cols), bf16),
            pltpu.VMEM((2, 2, nz, 2, 2, 64, half_ff), bf16),
            pltpu.VMEM((both_rows, lanes), f32),
            pltpu.VMEM((both_rows, lanes), f32),
        ],
    )
    gu_sum = net.reduce(gu_grads)
    back_got = net.core(back_away)
    attn_keep, attn_away, grad_middle, first_mine, first_away = run_kernel(
        functools.partial(attention_backward, dims),
        (place, pad, incoming, mine, facing, cosine, sine, back_mine, back_got, w_attn, w_out_wide, gains,
         first_norm, query, keys, values, probs, attended, middle),
        [
            ((8, nz, attn_rows, attn_cols), bf16),
            ((8, nz, attn_rows, attn_cols), bf16),
            ((local_rows, lanes), f32),
            ((local_rows, lanes), f32),
            ((local_rows, lanes), bf16),
        ],
        [
            pltpu.VMEM((local_rows, lanes), f32),
            pltpu.VMEM((both_rows, wide_k), f32),
            pltpu.VMEM((both_rows, KV * HD), f32),
            pltpu.VMEM((local_rows, lanes), bf16),
            pltpu.VMEM((2, 2, 2, nz, 2, attn_rows, attn_cols), bf16),
            pltpu.VMEM((2, both_rows, attn_cols), bf16),
            pltpu.VMEM((2, both_rows, attn_cols), bf16),
            pltpu.VMEM((2, local_rows, attn_cols), bf16),
            pltpu.VMEM((both_rows, lanes), f32),
        ],
    )
    from_core = net.core(attn_away)

    def both_cores(at):
        return (attn_keep[at].astype(f32) + from_core[at].astype(f32)).astype(bf16)

    attn_both = [both_cores(at) for at in (slice(0, 2), slice(2, 4), 4, 5, slice(6, 8))]
    attn_sum = net.reduce(attn_both)

    def narrow(value):
        return value.reshape(local_rows, 2 * blocks, 64)[:, :, :rows].reshape(local_rows, width)

    out_got = net.core(out_away)
    block_output = narrow(middle + out_mine + out_got.astype(f32)).astype(bf16)
    first_got = net.over_y(first_away)
    grad_first = narrow(first_mine + first_got.astype(f32))
    hidden = mine.astype(f32)
    gain = narrow(jnp.broadcast_to(gains[0:1], (local_rows, lanes)))[0]
    _, pull_first = jax.vjp(normed, hidden, gain)
    input_grad = narrow(grad_middle) + pull_first(grad_first)[0]

    def core_rows(total):
        return pick(c, total), net.core(pick(c, (total[1], total[0])).astype(bf16)).astype(f32)

    gu_mine, gu_got = (part[:, :rows] for part in core_rows(gu_sum))
    shape = (2, rows, half_ff // ff_rows, 1, ff_rows)
    gu_grad = net.order(c, gu_mine.reshape(shape), gu_got.reshape(shape), 3).reshape(
        2, rows, 2 * half_ff
    )
    attn_mine, attn_got = (part[:rows] for part in core_rows(attn_sum))
    qk_grad = pick(c, (attn_mine, attn_got))
    vo_grad = pick(c, (attn_got, attn_mine))
    gain_out = attn_sum[0, rows, :256].reshape(2, 2, 64)
    gain_out = pick(c, (gain_out[:, 0, :rows], gain_out[:, 1, :rows]))
    return (
        block_output[None],
        input_grad[None],
        qk_grad[:, :q_cols],
        qk_grad[:, q_cols:],
        vo_grad[:, :k_cols],
        vo_grad[:, k_cols:],
        gu_grad[0],
        gu_grad[1],
        down_grad,
        gain_out,
    )


def fast_body(*args):
    return fast_pass(*args)


def body(
    tokens, segment_ids, norm_gains, w_query, w_key, w_value, w_out, w_gate, w_up, w_down, cotangent
):
    local_rows = tokens.shape[1]
    groups = H // KV
    scale_factor = 1.0 / math.sqrt(HD)
    offset = lax.axis_index("ctx") * local_rows
    column_parts = (
        lax.all_gather(w_query, "ctx", axis=1, tiled=True),
        lax.all_gather(w_key, "ctx", axis=1, tiled=True),
        lax.all_gather(w_value, "ctx", axis=1, tiled=True),
        lax.all_gather(w_out, "ctx", axis=1, tiled=True),
        lax.all_gather(w_gate, "ctx", axis=1, tiled=True),
        lax.all_gather(w_up, "ctx", axis=1, tiled=True),
        lax.all_gather(w_down, "ctx", axis=1, tiled=True),
    )
    forward_set = (
        lax.all_gather(column_parts[0], "dp", axis=0, tiled=True),
        lax.all_gather(column_parts[1], "dp", axis=0, tiled=True),
        lax.all_gather(column_parts[2], "dp", axis=0, tiled=True),
        lax.all_gather(column_parts[3], "dp", axis=0, tiled=True),
        lax.all_gather(column_parts[4], "dp", axis=0, tiled=True),
        lax.all_gather(column_parts[5], "dp", axis=0, tiled=True),
        lax.all_gather(column_parts[6], "dp", axis=0, tiled=True),
        lax.all_gather(norm_gains.astype(jnp.bfloat16), "dp", axis=1, tiled=True).astype(
            norm_gains.dtype
        ),
    )
    query_full, key_full, value_full, out_full, gate_full, up_full, down_full, gains_full = (
        forward_set
    )
    hidden = tokens[0].astype(jnp.float32)
    own_segments = segment_ids[0]
    first_norm = normed(hidden, gains_full[0]).astype(jnp.bfloat16)
    cosine, sine = rope_tables(local_rows, offset, HD)
    query = rotate(matmul(first_norm, query_full).reshape(local_rows, H, HD), cosine, sine).astype(
        jnp.bfloat16
    )
    keys_local = (
        rotate(matmul(first_norm, key_full).reshape(local_rows, KV, HD), cosine, sine)
        .astype(jnp.bfloat16)
        .reshape(local_rows, KV * HD)
    )
    values_local = matmul(first_norm, value_full).astype(jnp.bfloat16)
    key_all, value_all, segment_all = (
        lax.all_gather(keys_local, "ctx", axis=0, tiled=True),
        lax.all_gather(values_local, "ctx", axis=0, tiled=True),
        lax.all_gather(own_segments, "ctx", axis=0, tiled=True),
    )
    length_all = key_all.shape[0]
    key_grid = key_all.reshape(length_all, KV, HD)
    value_grid = value_all.reshape(length_all, KV, HD)
    grouped = query.reshape(local_rows, KV, groups, HD)
    query_places = offset + jnp.arange(local_rows, dtype=jnp.int32)
    key_places = jnp.arange(length_all, dtype=jnp.int32)
    allowed = (key_places[None, :] <= query_places[:, None]) & (
        segment_all[None, :] == own_segments[:, None]
    )
    scores = score_block(grouped, key_grid, scale_factor)
    totals = jnp.sum(jnp.where(allowed, jnp.exp(scores), 0.0), axis=-1, keepdims=True)
    log_total = jnp.log(totals)
    probs = probabilities(scores, allowed, log_total).astype(jnp.bfloat16)
    attended = jnp.einsum("kgts,skd->tkgd", probs, value_grid, preferred_element_type=jnp.float32)
    attended = attended.reshape(local_rows, H * HD).astype(jnp.bfloat16)
    middle = hidden + matmul(attended, out_full)
    second_norm = normed(middle, gains_full[1]).astype(jnp.bfloat16)
    gate = matmul(second_norm, gate_full)
    upward = matmul(second_norm, up_full)
    sigma = jax.nn.sigmoid(gate)
    activated = gate * sigma
    mixed = (activated * upward).astype(jnp.bfloat16)
    block_output = (middle + matmul(mixed, down_full)).astype(jnp.bfloat16)
    query_back, key_back, value_back, out_back, gate_back, up_back, down_back, gains_back = (
        forward_set
    )
    incoming = cotangent[0]
    grad_down = matmul(mixed.T, incoming)
    grad_mixed = matmul(incoming, down_back.T)
    grad_gate = (grad_mixed * upward * sigma * (1.0 + gate * (1.0 - sigma))).astype(jnp.bfloat16)
    grad_upward = (grad_mixed * activated).astype(jnp.bfloat16)
    grad_wgate = matmul(second_norm.T, grad_gate)
    grad_wup = matmul(second_norm.T, grad_upward)
    grad_second = matmul(grad_gate, gate_back.T) + matmul(grad_upward, up_back.T)
    _, pull_second = jax.vjp(normed, middle, gains_back[1])
    grad_middle_norm, grad_gain_second = pull_second(grad_second)
    grad_middle = incoming.astype(jnp.float32) + grad_middle_norm
    grad_branch = grad_middle.astype(jnp.bfloat16)
    grad_wout = matmul(attended.T, grad_branch)
    grad_attended = (
        matmul(grad_branch, out_back.T).astype(jnp.bfloat16).reshape(local_rows, KV, groups, HD)
    )
    exact_probs = probabilities(score_block(grouped, key_grid, scale_factor), allowed, log_total)
    probs_again = exact_probs.astype(jnp.bfloat16)
    grad_values_all = jnp.einsum(
        "kgts,tkgd->skd", probs_again, grad_attended, preferred_element_type=jnp.float32
    )
    grad_probs = jnp.einsum(
        "tkgd,skd->kgts", grad_attended, value_grid, preferred_element_type=jnp.float32
    )
    row_terms = jnp.sum(exact_probs * grad_probs, axis=-1, keepdims=True)
    grad_scores = (exact_probs * (grad_probs - row_terms) * scale_factor).astype(jnp.bfloat16)
    grad_query = jnp.einsum(
        "kgts,skd->tkgd", grad_scores, key_grid, preferred_element_type=jnp.float32
    )
    grad_query = (
        unrotate(grad_query.reshape(local_rows, H, HD), cosine, sine)
        .reshape(local_rows, H * HD)
        .astype(jnp.bfloat16)
    )
    grad_keys_all = jnp.einsum(
        "kgts,tkgd->skd", grad_scores, grouped, preferred_element_type=jnp.float32
    )
    own_keys, own_values = (
        lax.psum_scatter(
            grad_keys_all.reshape(length_all, KV * HD).astype(jnp.bfloat16),
            "ctx",
            scatter_dimension=0,
            tiled=True,
        ).astype(jnp.float32),
        lax.psum_scatter(
            grad_values_all.reshape(length_all, KV * HD).astype(jnp.bfloat16),
            "ctx",
            scatter_dimension=0,
            tiled=True,
        ).astype(jnp.float32),
    )
    grad_keys = (
        unrotate(own_keys.reshape(local_rows, KV, HD), cosine, sine)
        .reshape(local_rows, KV * HD)
        .astype(jnp.bfloat16)
    )
    grad_values = own_values.astype(jnp.bfloat16)
    grad_wquery = matmul(first_norm.T, grad_query)
    grad_wkey = matmul(first_norm.T, grad_keys)
    grad_wvalue = matmul(first_norm.T, grad_values)
    grad_first = (
        matmul(grad_query, query_back.T)
        + matmul(grad_keys, key_back.T)
        + matmul(grad_values, value_back.T)
    )
    _, pull_first = jax.vjp(normed, hidden, gains_back[0])
    grad_hidden_norm, grad_gain_first = pull_first(grad_first)
    input_grad = grad_middle + grad_hidden_norm
    gain_terms = jnp.stack([grad_gain_first, grad_gain_second])
    gain_copies = jnp.broadcast_to(gain_terms[None], (lax.axis_size("ctx"),) + gain_terms.shape)
    by_cols = (
        lax.psum_scatter(
            grad_wquery.astype(jnp.bfloat16), "ctx", scatter_dimension=1, tiled=True
        ).astype(jnp.float32),
        lax.psum_scatter(
            grad_wkey.astype(jnp.bfloat16), "ctx", scatter_dimension=1, tiled=True
        ).astype(jnp.float32),
        lax.psum_scatter(
            grad_wvalue.astype(jnp.bfloat16), "ctx", scatter_dimension=1, tiled=True
        ).astype(jnp.float32),
        lax.psum_scatter(
            grad_wout.astype(jnp.bfloat16), "ctx", scatter_dimension=1, tiled=True
        ).astype(jnp.float32),
        lax.psum_scatter(
            grad_wgate.astype(jnp.bfloat16), "ctx", scatter_dimension=1, tiled=True
        ).astype(jnp.float32),
        lax.psum_scatter(
            grad_wup.astype(jnp.bfloat16), "ctx", scatter_dimension=1, tiled=True
        ).astype(jnp.float32),
        lax.psum_scatter(
            grad_down.astype(jnp.bfloat16), "ctx", scatter_dimension=1, tiled=True
        ).astype(jnp.float32),
        lax.psum_scatter(
            gain_copies.astype(jnp.bfloat16), "ctx", scatter_dimension=0, tiled=True
        ).astype(jnp.float32),
    )
    finals = (
        lax.psum_scatter(
            by_cols[0].astype(jnp.bfloat16), "dp", scatter_dimension=0, tiled=True
        ).astype(jnp.float32),
        lax.psum_scatter(
            by_cols[1].astype(jnp.bfloat16), "dp", scatter_dimension=0, tiled=True
        ).astype(jnp.float32),
        lax.psum_scatter(
            by_cols[2].astype(jnp.bfloat16), "dp", scatter_dimension=0, tiled=True
        ).astype(jnp.float32),
        lax.psum_scatter(
            by_cols[3].astype(jnp.bfloat16), "dp", scatter_dimension=0, tiled=True
        ).astype(jnp.float32),
        lax.psum_scatter(
            by_cols[4].astype(jnp.bfloat16), "dp", scatter_dimension=0, tiled=True
        ).astype(jnp.float32),
        lax.psum_scatter(
            by_cols[5].astype(jnp.bfloat16), "dp", scatter_dimension=0, tiled=True
        ).astype(jnp.float32),
        lax.psum_scatter(
            by_cols[6].astype(jnp.bfloat16), "dp", scatter_dimension=0, tiled=True
        ).astype(jnp.float32),
        lax.psum_scatter(
            by_cols[7].astype(jnp.bfloat16), "dp", scatter_dimension=2, tiled=True
        ).astype(jnp.float32),
    )
    gain_out = finals[7][0]
    return (
        block_output[None],
        input_grad[None],
        finals[0],
        finals[1],
        finals[2],
        finals[3],
        finals[4],
        finals[5],
        finals[6],
        gain_out,
    )


def solution(mesh):
    two_blocks = mesh.shape["ctx"] == 2 and mesh.shape["dp"] % 4 == 0
    return jax.shard_map(
        fast_body if two_blocks else body,
        mesh=mesh,
        in_specs=(
            P("dp", "ctx", None),
            P("dp", "ctx"),
            P(None, "dp"),
            P("dp", "ctx"),
            P("dp", "ctx"),
            P("dp", "ctx"),
            P("dp", "ctx"),
            P("dp", "ctx"),
            P("dp", "ctx"),
            P("dp", "ctx"),
            P("dp", "ctx", None),
        ),
        out_specs=(
            P("dp", "ctx", None),
            P("dp", "ctx", None),
            P("dp", "ctx"),
            P("dp", "ctx"),
            P("dp", "ctx"),
            P("dp", "ctx"),
            P("dp", "ctx"),
            P("dp", "ctx"),
            P("dp", "ctx"),
            P(None, "dp"),
        ),
        check_vma=False,
    )
```

```python
import functools
import math

import jax
import jax.numpy as jnp
from jax import lax
from jax.experimental import pallas as pl
from jax.experimental.pallas import tpu as pltpu
from jax.sharding import PartitionSpec as P


H = 15
KV = 5
HD = 64


norm_eps = 1e-05
rope_base = 100000.0

AXES = ("dp", "ctx")


def normed(hidden, scales):
    factor = lax.rsqrt(jnp.mean(hidden * hidden, axis=-1, keepdims=True) + norm_eps)
    return hidden * factor * scales


def rope_tables(amount, offset, head_size):
    middle = head_size // 2
    inverse_rates = rope_base ** (-(jnp.arange(middle, dtype=jnp.float32) * 2.0) / head_size)
    places = (offset + jnp.arange(amount, dtype=jnp.int32)).astype(jnp.float32)
    angles = places[:, None] * inverse_rates[None, :]
    return (jnp.cos(angles)[:, None, :], jnp.sin(angles)[:, None, :])


def rotate(values, cosine, sine):
    middle = values.shape[-1] // 2
    first_half = values[..., :middle]
    second_half = values[..., middle:]
    return jnp.concatenate(
        [first_half * cosine - second_half * sine, second_half * cosine + first_half * sine],
        axis=-1,
    )


def unrotate(values, cosine, sine):
    middle = values.shape[-1] // 2
    first_half = values[..., :middle]
    second_half = values[..., middle:]
    return jnp.concatenate(
        [first_half * cosine + second_half * sine, second_half * cosine - first_half * sine],
        axis=-1,
    )


def matmul(left, right):
    return jnp.dot(left, right, preferred_element_type=jnp.float32)


def score_block(grouped, key_grid, scale_factor):
    return (
        jnp.einsum("tkgd,skd->kgts", grouped, key_grid, preferred_element_type=jnp.float32)
        * scale_factor
    )


def probabilities(scores, allowed, log_total):
    return jnp.where(allowed, jnp.exp(scores - log_total), 0.0)


bf16 = jnp.bfloat16
f32 = jnp.float32


class Links:
    def __init__(self):
        self.dp = lax.axis_size("dp")
        self.nz = self.dp // 4
        index = lax.axis_index("dp")
        self.y = lax.axis_index("ctx")
        self.c = index % 2
        self.x = (index // 2) % 2
        self.z = index // 4

    def _permute(self, value, target):
        pairs = []
        for z in range(self.nz):
            for x in range(2):
                for c in range(2):
                    for y in range(2):
                        z2, x2, c2, y2 = target(z, x, c, y)
                        pairs.append(
                            (((z * 2 + x) * 2 + c) * 2 + y, ((z2 * 2 + x2) * 2 + c2) * 2 + y2)
                        )
        return lax.ppermute(value, AXES, pairs)

    def core(self, value):
        return self._permute(value, lambda z, x, c, y: (z, x, 1 - c, y))

    def over_x(self, value):
        return self._permute(value, lambda z, x, c, y: (z, 1 - x, c, y))

    def over_y(self, value):
        return self._permute(value, lambda z, x, c, y: (z, x, c, 1 - y))

    def over_z(self, value, step):
        return self._permute(value, lambda z, x, c, y: ((z + step) % self.nz, x, c, y))

    def order(self, flag, own, other, axis):
        return jnp.where(
            flag == 0,
            jnp.concatenate([own, other], axis=axis),
            jnp.concatenate([other, own], axis=axis),
        )

    def gather_z(self, block):
        parts = [block] + [self.over_z(block, k) for k in range(1, self.nz)]
        slots = []
        for slot in range(self.nz):
            distance = (self.z - slot) % self.nz
            value = parts[0]
            for k in range(1, self.nz):
                value = jnp.where(distance == k, parts[k], value)
            slots.append(value)
        return jnp.stack(slots, axis=1)

    def spread(self, line):
        by_x = self.over_x(line)
        by_y = self.over_y(line)
        corners = self.over_y(by_x[0]), self.over_x(by_y[1])
        return line, by_x, by_y, *corners

    def reduce(self, parts):
        send_y, send_x, by_x, by_y, own = parts
        got_y = self.over_y(send_y)
        got_x = self.over_x(send_x)
        onward_x = (by_x.astype(f32) + got_y[1].astype(f32)).astype(bf16)
        onward_y = (by_y.astype(f32) + got_x[1].astype(f32)).astype(bf16)
        last_x = self.over_x(onward_x)
        last_y = self.over_y(onward_y)
        line = jnp.stack(
            [
                own[0].astype(f32) + got_y[0].astype(f32) + last_x.astype(f32),
                own[1].astype(f32) + got_x[0].astype(f32) + last_y.astype(f32),
            ],
            axis=1,
        )
        low = line.astype(bf16)
        total = lax.dynamic_index_in_dim(line, self.z, 0, keepdims=False)
        for k in range(1, self.nz):
            block = lax.dynamic_index_in_dim(low, (self.z + k) % self.nz, 0, keepdims=False)
            arrived = self.over_z(block, k)
            total = total + arrived.astype(f32)
        return total


def pick(flag, pair):
    return jnp.where(flag == 0, pair[0], pair[1])


def padded_columns(count, block, wide, offset, total):
    target = jnp.arange(count // block * wide, dtype=jnp.int32)[None, :]
    lane = target % wide
    source = jnp.where(lane < block, offset + target // wide * block + lane, -1)
    source = lax.optimization_barrier(source)
    return (jnp.arange(total, dtype=jnp.int32)[:, None] == source).astype(bf16)


def dot_t(left, right):
    return lax.dot_general(left, right, (((0,), (0,)), ((), ())), preferred_element_type=f32)


def dot_nt(left, right):
    return lax.dot_general(left, right, (((1,), (1,)), ((), ())), preferred_element_type=f32)


def swapped(value):
    lanes = value.shape[1]
    lane = lax.broadcasted_iota(jnp.int32, value.shape, 1) % HD
    up = pltpu.roll(value, lanes - HD // 2, 1)
    down = pltpu.roll(value, HD // 2, 1)
    return jnp.where(lane < HD // 2, up, down)


def wide_table(table, lanes):
    return jnp.concatenate([table] * (lanes // table.shape[1]), axis=1)


def attention_forward(
    dims, place_ref, pad_ref, pick_ref, mine_ref, facing_ref, allowed_ref, cos_ref, sin_ref, *refs
):
    nz, rows, width, q_cols, k_cols = dims
    pieces, refs = refs[:10], refs[10:]
    (w_ref, wo_ref, gains_ref, x_ref, q_ref, k_ref, v_ref, p_ref, att_ref, middle_ref, second_ref) = refs[:11]
    wide_q, wide_k = refs[11:]
    c, x, y = place_ref[0], place_ref[1], place_ref[2]
    tokens = mine_ref.shape[0]
    for own in range(2):
        line, by_x, by_y, corner_0, corner_1 = pieces[own * 5 : own * 5 + 5]
        which = jnp.where(c == own, 0, 1)

        def store(t, y, z, x, piece, which=which):
            w_ref[which, y, z, x, t * 64 : (t + 1) * 64, :] = piece

        assemble(store, x, y, nz, line, by_x, by_y, corner_0, corner_1)
    gains = [[], []]
    for z in range(nz):
        for p in range(2):
            low, high = (w_ref[0, 0, z, p, at - 8 : at, :][4:5].astype(f32) for at in (64, 128))
            for i in range(2):
                gains[i].append((low + high)[:, i * 128 : (i + 1) * 128])
    gains = [jnp.concatenate(g, axis=1) for g in gains]
    gains_ref[...] = jnp.concatenate(gains + [jnp.zeros_like(gains[0])] * 6, axis=0)
    blank = jnp.zeros((64 - rows, w_ref.shape[-1]), bf16)

    @pl.loop(0, nz)
    def _(z):
        for s in range(2):
            for half in range(2):
                for p in range(2):
                    for at in (rows, rows + 64):
                        w_ref[s, half, z, p, at : at + 64 - rows, :] = blank

    hidden = matmul(jnp.concatenate([mine_ref[...], facing_ref[...]], axis=0), pad_ref[...])
    factor = lax.rsqrt(jnp.sum(hidden * hidden, axis=1, keepdims=True) / width + norm_eps)
    first = (hidden * factor * gains[0]).astype(bf16)
    x_ref[...] = first
    deep = nz * 2 * 128
    wide_q[...] = jnp.zeros_like(wide_q)
    wide_k[...] = jnp.zeros_like(wide_k)
    for half in range(2):
        both = matmul(first, w_ref[0, half].reshape(deep, q_cols + k_cols))
        wide_q[:, half * q_cols : (half + 1) * q_cols] = both[:tokens, :q_cols]
        wide_k[:, half * k_cols : (half + 1) * k_cols] = both[:, q_cols:]
        values = matmul(first, w_ref[1, half].reshape(deep, q_cols + k_cols)[:, :k_cols])
        v_ref[:, half * k_cols : (half + 1) * k_cols] = values.astype(bf16)
    cosine, sine = cos_ref[...], sin_ref[...]
    lanes = wide_q.shape[1]
    query = wide_q[...]
    query = query * wide_table(cosine[:tokens], lanes) + swapped(query) * wide_table(
        sine[:tokens], lanes
    )
    q_ref[...] = query.astype(bf16)
    lanes = wide_k.shape[1]
    keys = wide_k[...]
    keys = keys * wide_table(cosine, lanes) + swapped(keys) * wide_table(sine, lanes)
    k_ref[...] = keys.astype(bf16)
    groups = H // KV
    allowed = jnp.concatenate([allowed_ref[...]] * groups, axis=0) > 0
    for g in range(KV):
        heads = [
            q_ref[:, (g * groups + i) * HD : (g * groups + i + 1) * HD] for i in range(groups)
        ]
        scores = dot_nt(jnp.concatenate(heads, axis=0), k_ref[:, g * HD : (g + 1) * HD])
        scores = scores * (1.0 / math.sqrt(HD))
        totals = jnp.sum(jnp.where(allowed, jnp.exp(scores), 0.0), axis=1, keepdims=True)
        probs = jnp.where(allowed, jnp.exp(scores - jnp.log(totals)), 0.0)
        p_ref[g] = probs
        out = matmul(probs.astype(bf16), v_ref[:, g * HD : (g + 1) * HD])
        for i in range(groups):
            j = g * groups + i
            wide_q[:, j * HD : (j + 1) * HD] = out[i * tokens : (i + 1) * tokens]
    attended = matmul(wide_q[:, :width].astype(bf16), pad_ref[...]).astype(bf16)
    att_ref[...] = attended
    outs = []
    for half in range(2):
        w_out = matmul(w_ref[1, half].reshape(deep, q_cols + k_cols), pick_ref[...]).astype(bf16)
        wo_ref[half] = w_out
        outs.append(matmul(attended, w_out))
    middle = hidden[:tokens] + jnp.concatenate(outs, axis=1)
    middle_ref[...] = middle
    factor = lax.rsqrt(jnp.sum(middle * middle, axis=1, keepdims=True) / width + norm_eps)
    second_ref[...] = (middle * factor * gains[1]).astype(bf16)


def deal(item, x, y, nz, send_y, send_x, by_x, by_y, own):
    @pl.loop(0, nz)
    def _(z):
        for d in range(2):
            send_y[d, z] = item(0, 1 - y, z, x ^ d)
            send_x[d, z] = item(1, y ^ d, z, 1 - x)
            own[d, z] = item(d, y, z, x)
        by_x[z] = item(0, y, z, 1 - x)
        by_y[z] = item(1, 1 - y, z, x)


def pack_shapes(nz, *block):
    two, one = ((2, nz, *block), bf16), ((nz, *block), bf16)
    return [two, two, one, one, two]


def assemble(store, x, y, nz, line, by_x, by_y, corner_0, corner_1):
    @pl.loop(0, nz)
    def _(z):
        for t in range(2):
            corner = (corner_0, corner_1)[t]
            for dy in range(2):
                for dx in range(2):
                    piece = corner[z] if dy and dx else (line, by_x, by_y)[dx + 2 * dy][t, z]
                    store(t, y ^ dy, z, x ^ dx, piece)


def assemble_gate_up(w_ref, x, y, nz, gate_parts, up_parts):
    for which, parts in enumerate((gate_parts, up_parts)):

        def store(t, y, z, x, piece, which=which):
            w_ref[which, y, z, x, t * 64 : (t + 1) * 64, :] = piece

        assemble(store, x, y, nz, *parts)


def feed_forward(dims, place_ref, second_ref, got_ref, cot_ref, *refs):
    nz, ff_rows = dims
    x, y = place_ref[1], place_ref[2]
    (gate_ref, up_ref, mixed_ref, *dealt), (w_ref, sums) = refs[10:18], refs[18:]
    assemble_gate_up(w_ref, x, y, nz, refs[:5], refs[5:10])
    pair = jnp.concatenate([second_ref[...], got_ref[...]], axis=0)
    deep, n = nz * 2 * 128, w_ref.shape[-1]
    part, count = ff_rows // 2, n // ff_rows

    @pl.loop(0, 2)
    def _(half):
        gate = matmul(pair, w_ref[0, half].reshape(deep, n))
        upward = matmul(pair, w_ref[1, half].reshape(deep, n))
        gate_ref[half] = gate
        up_ref[half] = upward
        sigma = 1.0 / (1.0 + jnp.exp(-gate))
        mixed = (gate * sigma * upward).astype(bf16)
        mixed_ref[half] = mixed
        for columns in range(2):
            grads = dot_t(mixed, cot_ref[columns]).astype(bf16)
            for block in range(count):
                for t in range(2):
                    at = block * ff_rows + t * part
                    z = half * (count // 2) + block // 2
                    sums[t, columns, z, block % 2] = grads[at : at + part]

    deal(lambda t, y, z, x: sums[t, y, z, x], x, y, nz, *dealt)


def feed_backward(dims, place_ref, pad_ref, second_ref, got_ref, cot_ref, gate_ref, up_ref, mixed_ref, *refs):
    nz, ff_rows = dims
    x, y = place_ref[1], place_ref[2]
    (out_ref, out_away_ref, back_ref, back_away_ref, *dealt) = refs[15:24]
    (w_ref, d_ref, sums, back, out) = refs[24:]
    part = ff_rows // 2

    def store(t, y, z, x, piece):
        d_ref[y, z, x, t * part : (t + 1) * part, :] = piece

    assemble(store, x, y, nz, *refs[10:15])
    assemble_gate_up(w_ref, x, y, nz, refs[:5], refs[5:10])
    tokens = second_ref.shape[0]
    pair = jnp.concatenate([second_ref[...], got_ref[...]], axis=0)
    deep, n = nz * 2 * 128, w_ref.shape[-1]
    lanes = out.shape[1] // 2
    back[...] = jnp.zeros_like(back)
    out[...] = jnp.zeros_like(out)

    @pl.loop(0, 2)
    def _(half):
        mine = pl.ds(half * (nz // 2), nz // 2)
        down = [d_ref[columns, mine].reshape(n, d_ref.shape[-1]) for columns in range(2)]
        gm = dot_nt(cot_ref[0], down[0]) + dot_nt(cot_ref[1], down[1])
        gate, upward = gate_ref[half], up_ref[half]
        sigma = 1.0 / (1.0 + jnp.exp(-gate))
        grad_gate = (gm * upward * sigma * (1.0 + gate * (1.0 - sigma))).astype(bf16)
        grad_up = (gm * (gate * sigma)).astype(bf16)
        for which, grad in enumerate((grad_gate, grad_up)):
            total = dot_t(pair, grad).astype(bf16)
            for z in range(nz):
                for p in range(2):
                    for t in range(2):
                        at = ((z * 2 + p) * 2 + t) * 64
                        sums[t, half, z, p, which] = total[at : at + 64]
            back[...] += dot_nt(grad, w_ref[which, half].reshape(deep, n))
        for columns in range(2):
            wide = matmul(down[columns], pad_ref[...]).astype(bf16)
            out[:, columns * lanes : (columns + 1) * lanes] += matmul(mixed_ref[half], wide)

    deal(lambda t, y, z, x: sums[t, y, z, x], x, y, nz, *dealt)
    back_ref[...] = back[:tokens]
    back_away_ref[...] = back[tokens:].astype(bf16)
    out_ref[...] = out[:tokens]
    out_away_ref[...] = out[tokens:].astype(bf16)


def attention_backward(
    dims, place_ref, pad_ref, cot_ref, mine_ref, facing_ref, cos_ref, sin_ref, back_ref, back_got_ref, w_ref, wo_ref,
    gains_ref, x_ref, q_ref, k_ref, v_ref, p_ref, att_ref, middle_ref, keep_ref, away_ref, grad_middle_ref, first_ref,
    first_away_ref, wide_q, wide_k, wide_v, wide_g, sums, lefts, rights, outs, back,
):
    nz, rows, width, q_cols, k_cols = dims
    c, x, y = place_ref[0], place_ref[1], place_ref[2]
    tokens = middle_ref.shape[0]
    deep = nz * 2 * 128
    pad = pad_ref[...]
    gains = gains_ref[...]
    middle = middle_ref[...]
    factor = lax.rsqrt(jnp.sum(middle * middle, axis=1, keepdims=True) / width + norm_eps)
    incoming = back_ref[...] + back_got_ref[...].astype(f32)
    gain_second = jnp.sum(incoming * middle * factor, axis=0, keepdims=True)
    scaled = incoming * gains[1:2]
    mean = jnp.sum(scaled * middle, axis=1, keepdims=True) / width
    grad_middle = (
        matmul(cot_ref[...], pad) + factor * scaled - middle * (factor * factor * factor * mean)
    )
    grad_middle_ref[...] = grad_middle
    branch = grad_middle.astype(bf16)
    half_lanes = wo_ref.shape[-1]
    grad_att = dot_nt(branch[:, :half_lanes], wo_ref[0]) + dot_nt(branch[:, half_lanes:], wo_ref[1])
    grad_att = dot_nt(grad_att.astype(bf16), pad).astype(bf16)
    groups = H // KV
    wide_q[...] = jnp.zeros_like(wide_q)
    wide_k[...] = jnp.zeros_like(wide_k)
    wide_g[:, :width] = grad_att
    for g in range(KV):
        at = slice(g * HD, (g + 1) * HD)
        heads = [slice((g * groups + i) * HD, (g * groups + i + 1) * HD) for i in range(groups)]
        grad = jnp.concatenate([wide_g[:, h] for h in heads], axis=0)
        query = jnp.concatenate([q_ref[:, h] for h in heads], axis=0)
        probs = p_ref[g]
        wide_v[:, at] = dot_t(probs.astype(bf16), grad)
        grad_probs = dot_nt(grad, v_ref[:, at])
        row = jnp.sum(probs * grad_probs, axis=1, keepdims=True)
        grad_scores = (probs * (grad_probs - row) * (1.0 / math.sqrt(HD))).astype(bf16)
        wide_k[:, at] = dot_t(grad_scores, query)
        out = matmul(grad_scores, k_ref[:, at])
        for i in range(groups):
            wide_q[:, heads[i]] = out[i * tokens : (i + 1) * tokens]
    cosine, sine = cos_ref[...], sin_ref[...]
    lanes = wide_q.shape[1]
    value = wide_q[...]
    value = value * wide_table(cosine[:tokens], lanes) - swapped(value) * wide_table(
        sine[:tokens], lanes
    )
    wide_q[...] = value
    lanes = wide_k.shape[1]
    value = wide_k[...]
    value = value * wide_table(cosine, lanes) - swapped(value) * wide_table(sine, lanes)
    wide_k[...] = value
    plain = dot_nt(branch, pad)
    first = x_ref[...]
    attended = att_ref[...]
    zeros_q = jnp.zeros((tokens, q_cols), f32)
    zeros_o = jnp.zeros((2 * tokens, q_cols), f32)
    zeros_v = jnp.zeros((tokens, k_cols), f32)
    n = q_cols + k_cols
    for half in range(2):
        of_q = jnp.concatenate([wide_q[:, half * q_cols : (half + 1) * q_cols], zeros_q], axis=0)
        of_k = wide_k[:, half * k_cols : (half + 1) * k_cols]
        of_v = wide_v[:, half * k_cols : (half + 1) * k_cols]
        of_o = plain[:, half * q_cols : (half + 1) * q_cols]
        lefts[half] = jnp.concatenate([of_q, of_k], axis=1).astype(bf16)
        rights[half] = jnp.concatenate([of_v, zeros_o], axis=1).astype(bf16)
        outs[half] = jnp.concatenate([zeros_v, of_o], axis=1).astype(bf16)
    back[...] = jnp.zeros_like(back)

    @pl.loop(0, 2)
    def _(half):
        left, right = lefts[half], rights[half]
        totals = (dot_t(first, left), dot_t(first, right) + dot_t(attended, outs[half]))
        for s in range(2):
            total = totals[s].astype(bf16)
            for z in range(nz):
                for p in range(2):
                    for t in range(2):
                        at = ((z * 2 + p) * 2 + t) * 64
                        sums[s, t, half, z, p] = total[at : at + 64]
            back[...] += dot_nt((left, right)[s], w_ref[s, half].reshape(deep, n))

    hidden = matmul(jnp.concatenate([mine_ref[...], facing_ref[...]], axis=0), pad)
    factor = lax.rsqrt(jnp.sum(hidden * hidden, axis=1, keepdims=True) / width + norm_eps)
    gain_first = jnp.sum(back[...] * hidden * factor, axis=0, keepdims=True)
    first_ref[...] = back[:tokens]
    first_away_ref[...] = back[tokens:].astype(bf16)
    for z in range(nz):
        for p in range(2):
            lane = slice((z * 2 + p) * 128, (z * 2 + p + 1) * 128)
            gain_row = jnp.concatenate(
                [gain_first[:, lane], gain_second[:, lane], jnp.zeros((1, n - 256), f32)], axis=1
            )
            gain_rows = jnp.concatenate(
                [gain_row, jnp.zeros((63 - rows, n), f32)], axis=0
            ).astype(bf16)
            for half in range(2):
                for s in range(2):
                    for t in range(2):
                        sums[s, t, half, z, p, rows:64, :] = gain_rows
    for which, ref in ((c, keep_ref), (1 - c, away_ref)):
        views = (ref.at[0:2], ref.at[2:4], ref.at[4], ref.at[5], ref.at[6:8])
        deal(lambda t, y, z, x, s=which: sums[s, t, y, z, x], x, y, nz, *views)


def run_kernel(body, inputs, outs, scratch):
    moved = sum(math.prod(a.shape) * a.dtype.itemsize for a in inputs)
    vmem = pl.BlockSpec(memory_space=pltpu.VMEM)
    return pl.pallas_call(
        body,
        out_shape=[jax.ShapeDtypeStruct(shape, kind) for shape, kind in outs],
        in_specs=[pl.BlockSpec(memory_space=pltpu.SMEM)] + [vmem] * (len(inputs) - 1),
        out_specs=[vmem] * len(outs),
        scratch_shapes=scratch,
        compiler_params=pltpu.CompilerParams(vmem_limit_bytes=60 << 20),
        cost_estimate=pl.CostEstimate(flops=2 * 10**9, bytes_accessed=moved, transcendentals=0),
    )(*inputs)


def fast_pass(
    tokens, segment_ids, norm_gains, w_query, w_key, w_value, w_out, w_gate, w_up, w_down, cotangent
):
    net = Links()
    nz, c, x, y = net.nz, net.c, net.x, net.y
    local_rows = tokens.shape[1]
    width = tokens.shape[2]
    rows = w_query.shape[0]
    groups = H // KV
    q_cols, k_cols, o_cols = w_query.shape[1], w_key.shape[1], w_out.shape[1]
    attn_cols = q_cols + k_cols
    ff_rows = w_down.shape[0]
    half_ff = w_gate.shape[1] // 2

    mine = tokens[0]
    segments_mine = segment_ids[0]
    segment_row = jnp.pad(
        segments_mine[None].astype(bf16), ((0, 7), (0, width - local_rows))
    )
    facing_pack = net.over_y(jnp.concatenate([mine, segment_row], axis=0))
    facing = facing_pack[:local_rows]
    segments_facing = facing_pack[local_rows, :local_rows].astype(jnp.int32)
    incoming = cotangent[0]
    incoming_got = net.core(incoming)
    incoming_pair = jnp.concatenate([incoming, incoming_got], axis=0)

    def by_core(w):
        starts = range(0, 2 * half_ff, 2 * ff_rows)
        return [
            jnp.concatenate(
                [w[:, at + i * ff_rows : at + (i + 1) * ff_rows] for at in starts], axis=1
            )
            for i in range(2)
        ]

    qk = jnp.concatenate([w_query, w_key], axis=1)
    vo = jnp.concatenate([w_value, w_out], axis=1)
    gate_half, up_half = by_core(w_gate), by_core(w_up)
    gains_row = jnp.pad(norm_gains.astype(bf16), ((0, 0), (0, 64 - rows)))
    gains_row = net.order(c, gains_row, jnp.zeros_like(gains_row), 1).reshape(1, 256)
    gains_row = jnp.pad(gains_row, ((0, 63 - rows), (0, attn_cols - 256)))

    def with_gains(w):
        return jnp.concatenate([w, gains_row], axis=0)

    def tall(w):
        return jnp.pad(w, ((0, 64 - rows), (0, 0)))

    got = net.core(
        jnp.stack(
            [
                with_gains(pick(c, (vo, qk))),
                tall(pick(c, (gate_half[1], gate_half[0]))),
                tall(pick(c, (up_half[1], up_half[0]))),
            ]
        )
    )
    attn_rows = 64

    def chip_pack(own, other):
        return net.order(c, own[None], other[None], 0)

    attn_pack = chip_pack(with_gains(pick(c, (qk, vo))), got[0])
    gate_pack = chip_pack(tall(pick(c, gate_half)), got[1])
    up_pack = chip_pack(tall(pick(c, up_half)), got[2])
    down_pack = w_down.reshape(2, ff_rows // 2, w_down.shape[1])

    attn_line = net.gather_z(attn_pack)
    gate_line = net.gather_z(gate_pack)
    up_line = net.gather_z(up_pack)
    down_line = net.gather_z(down_pack)
    attn_own = net.spread(attn_line)
    attn_other = [net.core(piece) for piece in attn_own]
    gate_parts = net.spread(gate_line)
    up_parts = net.spread(up_line)
    down_parts = net.spread(down_line)

    place = jnp.stack([c, x, y]).astype(jnp.int32)
    both_rows = 2 * local_rows
    blocks = nz * 2
    lanes = blocks * 128
    deep = blocks * 128
    pad = padded_columns(width, rows, 64, 0, width)
    pad_half = padded_columns(o_cols, rows, 64, 0, o_cols)
    pick_half = padded_columns(o_cols, rows, 64, k_cols, attn_cols)
    tables = [
        rope_tables(local_rows, start, HD) for start in (y * local_rows, (1 - y) * local_rows)
    ]
    cosine = jnp.concatenate([t[0][:, 0] for t in tables], axis=0)
    sine = jnp.concatenate([t[1][:, 0] for t in tables], axis=0)
    cosine = jnp.concatenate([cosine] * 4, axis=1)
    sine = jnp.concatenate([-sine, sine] * 2, axis=1)
    own_places = y * local_rows + jnp.arange(local_rows, dtype=jnp.int32)
    facing_places = (1 - y) * local_rows + jnp.arange(local_rows, dtype=jnp.int32)
    key_places = jnp.concatenate([own_places, facing_places])
    segment_all = jnp.concatenate([segments_mine, segments_facing])
    allowed = (
        (key_places[None, :] <= own_places[:, None])
        & (segment_all[None, :] == segments_mine[:, None])
    ).astype(f32)
    dims = (nz, rows, width, q_cols, k_cols)
    wide_k = KV * HD + 64
    (w_attn, w_out_wide, gains, first_norm, query, keys, values, probs, attended, middle, second_norm) = (
        run_kernel(
            functools.partial(attention_forward, dims),
            (place, pad, pick_half, mine, facing, allowed, cosine, sine, *attn_own, *attn_other),
            [
                ((2, 2, nz, 2, 128, attn_cols), bf16),
                ((2, deep, lanes // 2), bf16),
                ((8, lanes), f32),
                ((both_rows, lanes), bf16),
                ((local_rows, lanes), bf16),
                ((both_rows, wide_k), bf16),
                ((both_rows, KV * HD), bf16),
                ((KV, groups * local_rows, both_rows), f32),
                ((local_rows, lanes), bf16),
                ((local_rows, lanes), f32),
                ((local_rows, lanes), bf16),
            ],
            [pltpu.VMEM((local_rows, lanes), f32), pltpu.VMEM((both_rows, wide_k), f32)],
        )
    )

    second_got = net.core(second_norm)
    incoming_halves = jnp.stack(jnp.split(incoming_pair, 2, axis=1))
    ff_dims = (nz, ff_rows)
    chip_w = pltpu.VMEM((2, 2, nz, 2, 128, half_ff), bf16)
    gate, upward, mixed, *down_grads = run_kernel(
        functools.partial(feed_forward, ff_dims),
        (place, second_norm, second_got, incoming_halves, *gate_parts, *up_parts),
        [
            ((2, both_rows, half_ff), f32),
            ((2, both_rows, half_ff), f32),
            ((2, both_rows, half_ff), bf16),
            *pack_shapes(nz, ff_rows // 2, o_cols),
        ],
        [chip_w, pltpu.VMEM((2, 2, nz, 2, ff_rows // 2, o_cols), bf16)],
    )
    down_grad = net.reduce(down_grads).reshape(ff_rows, -1)
    out_mine, out_away, back_mine, back_away, *gu_grads = run_kernel(
        functools.partial(feed_backward, ff_dims),
        (place, pad_half, second_norm, second_got, incoming_halves, gate, upward, mixed,
         *gate_parts, *up_parts, *down_parts),
        [
            ((local_rows, lanes), f32),
            ((local_rows, lanes), bf16),
            ((local_rows, lanes), f32),
            ((local_rows, lanes), bf16),
            *pack_shapes(nz, 2, 64, half_ff),
        ],
        [
            chip_w,
            pltpu.VMEM((2, nz, 2, ff_rows, o_cols), bf16),
            pltpu.VMEM((2, 2, nz, 2, 2, 64, half_ff), bf16),
            pltpu.VMEM((both_rows, lanes), f32),
            pltpu.VMEM((both_rows, lanes), f32),
        ],
    )
    gu_sum = net.reduce(gu_grads)
    back_got = net.core(back_away)
    attn_keep, attn_away, grad_middle, first_mine, first_away = run_kernel(
        functools.partial(attention_backward, dims),
        (place, pad, incoming, mine, facing, cosine, sine, back_mine, back_got, w_attn, w_out_wide, gains,
         first_norm, query, keys, values, probs, attended, middle),
        [
            ((8, nz, attn_rows, attn_cols), bf16),
            ((8, nz, attn_rows, attn_cols), bf16),
            ((local_rows, lanes), f32),
            ((local_rows, lanes), f32),
            ((local_rows, lanes), bf16),
        ],
        [
            pltpu.VMEM((local_rows, lanes), f32),
            pltpu.VMEM((both_rows, wide_k), f32),
            pltpu.VMEM((both_rows, KV * HD), f32),
            pltpu.VMEM((local_rows, lanes), bf16),
            pltpu.VMEM((2, 2, 2, nz, 2, attn_rows, attn_cols), bf16),
            pltpu.VMEM((2, both_rows, attn_cols), bf16),
            pltpu.VMEM((2, both_rows, attn_cols), bf16),
            pltpu.VMEM((2, local_rows, attn_cols), bf16),
            pltpu.VMEM((both_rows, lanes), f32),
        ],
    )
    from_core = net.core(attn_away)

    def both_cores(at):
        return (attn_keep[at].astype(f32) + from_core[at].astype(f32)).astype(bf16)

    attn_both = [both_cores(at) for at in (slice(0, 2), slice(2, 4), 4, 5, slice(6, 8))]
    attn_sum = net.reduce(attn_both)

    def narrow(value):
        return value.reshape(local_rows, 2 * blocks, 64)[:, :, :rows].reshape(local_rows, width)

    out_got = net.core(out_away)
    block_output = narrow(middle + out_mine + out_got.astype(f32)).astype(bf16)
    first_got = net.over_y(first_away)
    grad_first = narrow(first_mine + first_got.astype(f32))
    hidden = mine.astype(f32)
    gain = narrow(jnp.broadcast_to(gains[0:1], (local_rows, lanes)))[0]
    _, pull_first = jax.vjp(normed, hidden, gain)
    input_grad = narrow(grad_middle) + pull_first(grad_first)[0]

    def core_rows(total):
        return pick(c, total), net.core(pick(c, (total[1], total[0])).astype(bf16)).astype(f32)

    gu_mine, gu_got = core_rows(gu_sum)

    def columns(which):
        pair = (gu_mine[which, :rows], gu_got[which, :rows])
        parts = (pick(c, pair), pick(c, pair[::-1]))
        starts = range(0, half_ff, ff_rows)
        return jnp.concatenate(
            [part[:, at : at + ff_rows] for at in starts for part in parts], axis=1
        )

    gu_grad = columns(0), columns(1)
    attn_mine, attn_got = (part[:rows] for part in core_rows(attn_sum))
    qk_grad = pick(c, (attn_mine, attn_got))
    vo_grad = pick(c, (attn_got, attn_mine))
    gain_out = attn_sum[0, rows, :256].reshape(2, 2, 64)
    gain_out = pick(c, (gain_out[:, 0, :rows], gain_out[:, 1, :rows]))
    return (
        block_output[None],
        input_grad[None],
        qk_grad[:, :q_cols],
        qk_grad[:, q_cols:],
        vo_grad[:, :k_cols],
        vo_grad[:, k_cols:],
        gu_grad[0],
        gu_grad[1],
        down_grad,
        gain_out,
    )


def fast_body(*args):
    return fast_pass(*args)


def body(
    tokens, segment_ids, norm_gains, w_query, w_key, w_value, w_out, w_gate, w_up, w_down, cotangent
):
    local_rows = tokens.shape[1]
    groups = H // KV
    scale_factor = 1.0 / math.sqrt(HD)
    offset = lax.axis_index("ctx") * local_rows
    column_parts = (
        lax.all_gather(w_query, "ctx", axis=1, tiled=True),
        lax.all_gather(w_key, "ctx", axis=1, tiled=True),
        lax.all_gather(w_value, "ctx", axis=1, tiled=True),
        lax.all_gather(w_out, "ctx", axis=1, tiled=True),
        lax.all_gather(w_gate, "ctx", axis=1, tiled=True),
        lax.all_gather(w_up, "ctx", axis=1, tiled=True),
        lax.all_gather(w_down, "ctx", axis=1, tiled=True),
    )
    forward_set = (
        lax.all_gather(column_parts[0], "dp", axis=0, tiled=True),
        lax.all_gather(column_parts[1], "dp", axis=0, tiled=True),
        lax.all_gather(column_parts[2], "dp", axis=0, tiled=True),
        lax.all_gather(column_parts[3], "dp", axis=0, tiled=True),
        lax.all_gather(column_parts[4], "dp", axis=0, tiled=True),
        lax.all_gather(column_parts[5], "dp", axis=0, tiled=True),
        lax.all_gather(column_parts[6], "dp", axis=0, tiled=True),
        lax.all_gather(norm_gains.astype(jnp.bfloat16), "dp", axis=1, tiled=True).astype(
            norm_gains.dtype
        ),
    )
    query_full, key_full, value_full, out_full, gate_full, up_full, down_full, gains_full = (
        forward_set
    )
    hidden = tokens[0].astype(jnp.float32)
    own_segments = segment_ids[0]
    first_norm = normed(hidden, gains_full[0]).astype(jnp.bfloat16)
    cosine, sine = rope_tables(local_rows, offset, HD)
    query = rotate(matmul(first_norm, query_full).reshape(local_rows, H, HD), cosine, sine).astype(
        jnp.bfloat16
    )
    keys_local = (
        rotate(matmul(first_norm, key_full).reshape(local_rows, KV, HD), cosine, sine)
        .astype(jnp.bfloat16)
        .reshape(local_rows, KV * HD)
    )
    values_local = matmul(first_norm, value_full).astype(jnp.bfloat16)
    key_all, value_all, segment_all = (
        lax.all_gather(keys_local, "ctx", axis=0, tiled=True),
        lax.all_gather(values_local, "ctx", axis=0, tiled=True),
        lax.all_gather(own_segments, "ctx", axis=0, tiled=True),
    )
    length_all = key_all.shape[0]
    key_grid = key_all.reshape(length_all, KV, HD)
    value_grid = value_all.reshape(length_all, KV, HD)
    grouped = query.reshape(local_rows, KV, groups, HD)
    query_places = offset + jnp.arange(local_rows, dtype=jnp.int32)
    key_places = jnp.arange(length_all, dtype=jnp.int32)
    allowed = (key_places[None, :] <= query_places[:, None]) & (
        segment_all[None, :] == own_segments[:, None]
    )
    scores = score_block(grouped, key_grid, scale_factor)
    totals = jnp.sum(jnp.where(allowed, jnp.exp(scores), 0.0), axis=-1, keepdims=True)
    log_total = jnp.log(totals)
    probs = probabilities(scores, allowed, log_total).astype(jnp.bfloat16)
    attended = jnp.einsum("kgts,skd->tkgd", probs, value_grid, preferred_element_type=jnp.float32)
    attended = attended.reshape(local_rows, H * HD).astype(jnp.bfloat16)
    middle = hidden + matmul(attended, out_full)
    second_norm = normed(middle, gains_full[1]).astype(jnp.bfloat16)
    gate = matmul(second_norm, gate_full)
    upward = matmul(second_norm, up_full)
    sigma = jax.nn.sigmoid(gate)
    activated = gate * sigma
    mixed = (activated * upward).astype(jnp.bfloat16)
    block_output = (middle + matmul(mixed, down_full)).astype(jnp.bfloat16)
    query_back, key_back, value_back, out_back, gate_back, up_back, down_back, gains_back = (
        forward_set
    )
    incoming = cotangent[0]
    grad_down = matmul(mixed.T, incoming)
    grad_mixed = matmul(incoming, down_back.T)
    grad_gate = (grad_mixed * upward * sigma * (1.0 + gate * (1.0 - sigma))).astype(jnp.bfloat16)
    grad_upward = (grad_mixed * activated).astype(jnp.bfloat16)
    grad_wgate = matmul(second_norm.T, grad_gate)
    grad_wup = matmul(second_norm.T, grad_upward)
    grad_second = matmul(grad_gate, gate_back.T) + matmul(grad_upward, up_back.T)
    _, pull_second = jax.vjp(normed, middle, gains_back[1])
    grad_middle_norm, grad_gain_second = pull_second(grad_second)
    grad_middle = incoming.astype(jnp.float32) + grad_middle_norm
    grad_branch = grad_middle.astype(jnp.bfloat16)
    grad_wout = matmul(attended.T, grad_branch)
    grad_attended = (
        matmul(grad_branch, out_back.T).astype(jnp.bfloat16).reshape(local_rows, KV, groups, HD)
    )
    exact_probs = probabilities(score_block(grouped, key_grid, scale_factor), allowed, log_total)
    probs_again = exact_probs.astype(jnp.bfloat16)
    grad_values_all = jnp.einsum(
        "kgts,tkgd->skd", probs_again, grad_attended, preferred_element_type=jnp.float32
    )
    grad_probs = jnp.einsum(
        "tkgd,skd->kgts", grad_attended, value_grid, preferred_element_type=jnp.float32
    )
    row_terms = jnp.sum(exact_probs * grad_probs, axis=-1, keepdims=True)
    grad_scores = (exact_probs * (grad_probs - row_terms) * scale_factor).astype(jnp.bfloat16)
    grad_query = jnp.einsum(
        "kgts,skd->tkgd", grad_scores, key_grid, preferred_element_type=jnp.float32
    )
    grad_query = (
        unrotate(grad_query.reshape(local_rows, H, HD), cosine, sine)
        .reshape(local_rows, H * HD)
        .astype(jnp.bfloat16)
    )
    grad_keys_all = jnp.einsum(
        "kgts,tkgd->skd", grad_scores, grouped, preferred_element_type=jnp.float32
    )
    own_keys, own_values = (
        lax.psum_scatter(
            grad_keys_all.reshape(length_all, KV * HD).astype(jnp.bfloat16),
            "ctx",
            scatter_dimension=0,
            tiled=True,
        ).astype(jnp.float32),
        lax.psum_scatter(
            grad_values_all.reshape(length_all, KV * HD).astype(jnp.bfloat16),
            "ctx",
            scatter_dimension=0,
            tiled=True,
        ).astype(jnp.float32),
    )
    grad_keys = (
        unrotate(own_keys.reshape(local_rows, KV, HD), cosine, sine)
        .reshape(local_rows, KV * HD)
        .astype(jnp.bfloat16)
    )
    grad_values = own_values.astype(jnp.bfloat16)
    grad_wquery = matmul(first_norm.T, grad_query)
    grad_wkey = matmul(first_norm.T, grad_keys)
    grad_wvalue = matmul(first_norm.T, grad_values)
    grad_first = (
        matmul(grad_query, query_back.T)
        + matmul(grad_keys, key_back.T)
        + matmul(grad_values, value_back.T)
    )
    _, pull_first = jax.vjp(normed, hidden, gains_back[0])
    grad_hidden_norm, grad_gain_first = pull_first(grad_first)
    input_grad = grad_middle + grad_hidden_norm
    gain_terms = jnp.stack([grad_gain_first, grad_gain_second])
    gain_copies = jnp.broadcast_to(gain_terms[None], (lax.axis_size("ctx"),) + gain_terms.shape)
    by_cols = (
        lax.psum_scatter(
            grad_wquery.astype(jnp.bfloat16), "ctx", scatter_dimension=1, tiled=True
        ).astype(jnp.float32),
        lax.psum_scatter(
            grad_wkey.astype(jnp.bfloat16), "ctx", scatter_dimension=1, tiled=True
        ).astype(jnp.float32),
        lax.psum_scatter(
            grad_wvalue.astype(jnp.bfloat16), "ctx", scatter_dimension=1, tiled=True
        ).astype(jnp.float32),
        lax.psum_scatter(
            grad_wout.astype(jnp.bfloat16), "ctx", scatter_dimension=1, tiled=True
        ).astype(jnp.float32),
        lax.psum_scatter(
            grad_wgate.astype(jnp.bfloat16), "ctx", scatter_dimension=1, tiled=True
        ).astype(jnp.float32),
        lax.psum_scatter(
            grad_wup.astype(jnp.bfloat16), "ctx", scatter_dimension=1, tiled=True
        ).astype(jnp.float32),
        lax.psum_scatter(
            grad_down.astype(jnp.bfloat16), "ctx", scatter_dimension=1, tiled=True
        ).astype(jnp.float32),
        lax.psum_scatter(
            gain_copies.astype(jnp.bfloat16), "ctx", scatter_dimension=0, tiled=True
        ).astype(jnp.float32),
    )
    finals = (
        lax.psum_scatter(
            by_cols[0].astype(jnp.bfloat16), "dp", scatter_dimension=0, tiled=True
        ).astype(jnp.float32),
        lax.psum_scatter(
            by_cols[1].astype(jnp.bfloat16), "dp", scatter_dimension=0, tiled=True
        ).astype(jnp.float32),
        lax.psum_scatter(
            by_cols[2].astype(jnp.bfloat16), "dp", scatter_dimension=0, tiled=True
        ).astype(jnp.float32),
        lax.psum_scatter(
            by_cols[3].astype(jnp.bfloat16), "dp", scatter_dimension=0, tiled=True
        ).astype(jnp.float32),
        lax.psum_scatter(
            by_cols[4].astype(jnp.bfloat16), "dp", scatter_dimension=0, tiled=True
        ).astype(jnp.float32),
        lax.psum_scatter(
            by_cols[5].astype(jnp.bfloat16), "dp", scatter_dimension=0, tiled=True
        ).astype(jnp.float32),
        lax.psum_scatter(
            by_cols[6].astype(jnp.bfloat16), "dp", scatter_dimension=0, tiled=True
        ).astype(jnp.float32),
        lax.psum_scatter(
            by_cols[7].astype(jnp.bfloat16), "dp", scatter_dimension=2, tiled=True
        ).astype(jnp.float32),
    )
    gain_out = finals[7][0]
    return (
        block_output[None],
        input_grad[None],
        finals[0],
        finals[1],
        finals[2],
        finals[3],
        finals[4],
        finals[5],
        finals[6],
        gain_out,
    )


def solution(mesh):
    two_blocks = mesh.shape["ctx"] == 2 and mesh.shape["dp"] % 4 == 0
    return jax.shard_map(
        fast_body if two_blocks else body,
        mesh=mesh,
        in_specs=(
            P("dp", "ctx", None),
            P("dp", "ctx"),
            P(None, "dp"),
            P("dp", "ctx"),
            P("dp", "ctx"),
            P("dp", "ctx"),
            P("dp", "ctx"),
            P("dp", "ctx"),
            P("dp", "ctx"),
            P("dp", "ctx"),
            P("dp", "ctx", None),
        ),
        out_specs=(
            P("dp", "ctx", None),
            P("dp", "ctx", None),
            P("dp", "ctx"),
            P("dp", "ctx"),
            P("dp", "ctx"),
            P("dp", "ctx"),
            P("dp", "ctx"),
            P("dp", "ctx"),
            P("dp", "ctx"),
            P(None, "dp"),
        ),
        check_vma=False,
    )
```

```python
import functools
import math

import jax
import jax.numpy as jnp
from jax import lax
from jax.experimental import pallas as pl
from jax.experimental.pallas import tpu as pltpu
from jax.sharding import PartitionSpec as P


H = 15
KV = 5
HD = 64


norm_eps = 1e-05
rope_base = 100000.0

AXES = ("dp", "ctx")


def normed(hidden, scales):
    factor = lax.rsqrt(jnp.mean(hidden * hidden, axis=-1, keepdims=True) + norm_eps)
    return hidden * factor * scales


def rope_tables(amount, offset, head_size):
    middle = head_size // 2
    inverse_rates = rope_base ** (-(jnp.arange(middle, dtype=jnp.float32) * 2.0) / head_size)
    places = (offset + jnp.arange(amount, dtype=jnp.int32)).astype(jnp.float32)
    angles = places[:, None] * inverse_rates[None, :]
    return (jnp.cos(angles)[:, None, :], jnp.sin(angles)[:, None, :])


def rotate(values, cosine, sine):
    middle = values.shape[-1] // 2
    first_half = values[..., :middle]
    second_half = values[..., middle:]
    return jnp.concatenate(
        [first_half * cosine - second_half * sine, second_half * cosine + first_half * sine],
        axis=-1,
    )


def unrotate(values, cosine, sine):
    middle = values.shape[-1] // 2
    first_half = values[..., :middle]
    second_half = values[..., middle:]
    return jnp.concatenate(
        [first_half * cosine + second_half * sine, second_half * cosine - first_half * sine],
        axis=-1,
    )


def matmul(left, right):
    return jnp.dot(left, right, preferred_element_type=jnp.float32)


def score_block(grouped, key_grid, scale_factor):
    return (
        jnp.einsum("tkgd,skd->kgts", grouped, key_grid, preferred_element_type=jnp.float32)
        * scale_factor
    )


def probabilities(scores, allowed, log_total):
    return jnp.where(allowed, jnp.exp(scores - log_total), 0.0)


bf16 = jnp.bfloat16
f32 = jnp.float32


class Links:
    def __init__(self):
        self.dp = lax.axis_size("dp")
        self.nz = self.dp // 4
        index = lax.axis_index("dp")
        self.y = lax.axis_index("ctx")
        self.c = index % 2
        self.x = (index // 2) % 2
        self.z = index // 4

    def _permute(self, value, target):
        pairs = []
        for z in range(self.nz):
            for x in range(2):
                for c in range(2):
                    for y in range(2):
                        z2, x2, c2, y2 = target(z, x, c, y)
                        pairs.append(
                            (((z * 2 + x) * 2 + c) * 2 + y, ((z2 * 2 + x2) * 2 + c2) * 2 + y2)
                        )
        return lax.ppermute(value, AXES, pairs)

    def core(self, value):
        return self._permute(value, lambda z, x, c, y: (z, x, 1 - c, y))

    def over_x(self, value):
        return self._permute(value, lambda z, x, c, y: (z, 1 - x, c, y))

    def over_y(self, value):
        return self._permute(value, lambda z, x, c, y: (z, x, c, 1 - y))

    def over_z(self, value, step):
        return self._permute(value, lambda z, x, c, y: ((z + step) % self.nz, x, c, y))

    def order(self, flag, own, other, axis):
        return jnp.where(
            flag == 0,
            jnp.concatenate([own, other], axis=axis),
            jnp.concatenate([other, own], axis=axis),
        )

    def gather_z(self, block, axis):
        parts = [block] + [self.over_z(block, k) for k in range(1, self.nz)]
        slots = []
        for slot in range(self.nz):
            distance = (self.z - slot) % self.nz
            value = parts[0]
            for k in range(1, self.nz):
                value = jnp.where(distance == k, parts[k], value)
            slots.append(value)
        return jnp.stack(slots, axis=axis)

    def spread(self, line, axis):
        by_x = self.over_x(line)
        by_y = self.over_y(line)
        item = (slice(None),) * (1 - axis)
        corners = self.over_y(by_x[item + (0,)]), self.over_x(by_y[item + (1,)])
        return line, by_x, by_y, *corners

    def reduce(self, parts):
        send_y, send_x, by_x, by_y, own = parts
        got_y = self.over_y(send_y)
        got_x = self.over_x(send_x)
        onward_x = (by_x.astype(f32) + got_y[1].astype(f32)).astype(bf16)
        onward_y = (by_y.astype(f32) + got_x[1].astype(f32)).astype(bf16)
        last_x = self.over_x(onward_x)
        last_y = self.over_y(onward_y)
        line = jnp.stack(
            [
                own[0].astype(f32) + got_y[0].astype(f32) + last_x.astype(f32),
                own[1].astype(f32) + got_x[0].astype(f32) + last_y.astype(f32),
            ],
            axis=1,
        )
        low = line.astype(bf16)
        total = lax.dynamic_index_in_dim(line, self.z, 0, keepdims=False)
        for k in range(1, self.nz):
            block = lax.dynamic_index_in_dim(low, (self.z + k) % self.nz, 0, keepdims=False)
            arrived = self.over_z(block, k)
            total = total + arrived.astype(f32)
        return total


def pick(flag, pair):
    return jnp.where(flag == 0, pair[0], pair[1])


def padded_columns(count, block, wide, offset, total):
    target = jnp.arange(count // block * wide, dtype=jnp.int32)[None, :]
    lane = target % wide
    source = jnp.where(lane < block, offset + target // wide * block + lane, -1)
    source = lax.optimization_barrier(source)
    return (jnp.arange(total, dtype=jnp.int32)[:, None] == source).astype(bf16)


def dot_t(left, right):
    return lax.dot_general(left, right, (((0,), (0,)), ((), ())), preferred_element_type=f32)


def dot_nt(left, right):
    return lax.dot_general(left, right, (((1,), (1,)), ((), ())), preferred_element_type=f32)


def swapped(value):
    lanes = value.shape[1]
    lane = lax.broadcasted_iota(jnp.int32, value.shape, 1) % HD
    up = pltpu.roll(value, lanes - HD // 2, 1)
    down = pltpu.roll(value, HD // 2, 1)
    return jnp.where(lane < HD // 2, up, down)


def wide_table(table, lanes):
    return jnp.concatenate([table] * (lanes // table.shape[1]), axis=1)


def attention_forward(
    dims, place_ref, pad_ref, pick_ref, mine_ref, facing_ref, allowed_ref, cos_ref, sin_ref, *refs
):
    nz, rows, width, q_cols, k_cols = dims
    pieces, refs = refs[:10], refs[10:]
    (w_ref, wo_ref, gains_ref, x_ref, q_ref, k_ref, v_ref, p_ref, att_ref, middle_ref, second_ref) = refs[:11]
    wide_q, wide_k = refs[11:]
    c, x, y = place_ref[0], place_ref[1], place_ref[2]
    tokens = mine_ref.shape[0]
    for own in range(2):
        line, by_x, by_y, corner_0, corner_1 = pieces[own * 5 : own * 5 + 5]
        which = jnp.where(c == own, 0, 1)

        def store(t, y, z, x, piece, which=which):
            w_ref[which, y, z, x, t * 64 : (t + 1) * 64, :] = piece

        assemble(store, x, y, nz, 0, line, by_x, by_y, corner_0, corner_1)
    gains = [[], []]
    for z in range(nz):
        for p in range(2):
            low, high = (w_ref[0, 0, z, p, at - 8 : at, :][4:5].astype(f32) for at in (64, 128))
            for i in range(2):
                gains[i].append((low + high)[:, i * 128 : (i + 1) * 128])
    gains = [jnp.concatenate(g, axis=1) for g in gains]
    gains_ref[...] = jnp.concatenate(gains + [jnp.zeros_like(gains[0])] * 6, axis=0)
    blank = jnp.zeros((64 - rows, w_ref.shape[-1]), bf16)

    @pl.loop(0, nz)
    def _(z):
        for s in range(2):
            for half in range(2):
                for p in range(2):
                    for at in (rows, rows + 64):
                        w_ref[s, half, z, p, at : at + 64 - rows, :] = blank

    hidden = matmul(jnp.concatenate([mine_ref[...], facing_ref[...]], axis=0), pad_ref[...])
    factor = lax.rsqrt(jnp.sum(hidden * hidden, axis=1, keepdims=True) / width + norm_eps)
    first = (hidden * factor * gains[0]).astype(bf16)
    x_ref[...] = first
    deep = nz * 2 * 128
    wide_q[...] = jnp.zeros_like(wide_q)
    wide_k[...] = jnp.zeros_like(wide_k)
    for half in range(2):
        both = matmul(first, w_ref[0, half].reshape(deep, q_cols + k_cols))
        wide_q[:, half * q_cols : (half + 1) * q_cols] = both[:tokens, :q_cols]
        wide_k[:, half * k_cols : (half + 1) * k_cols] = both[:, q_cols:]
        values = matmul(first, w_ref[1, half].reshape(deep, q_cols + k_cols)[:, :k_cols])
        v_ref[:, half * k_cols : (half + 1) * k_cols] = values.astype(bf16)
    cosine, sine = cos_ref[...], sin_ref[...]
    lanes = wide_q.shape[1]
    query = wide_q[...]
    query = query * wide_table(cosine[:tokens], lanes) + swapped(query) * wide_table(
        sine[:tokens], lanes
    )
    q_ref[...] = query.astype(bf16)
    lanes = wide_k.shape[1]
    keys = wide_k[...]
    keys = keys * wide_table(cosine, lanes) + swapped(keys) * wide_table(sine, lanes)
    k_ref[...] = keys.astype(bf16)
    groups = H // KV
    allowed = jnp.concatenate([allowed_ref[...]] * groups, axis=0) > 0
    for g in range(KV):
        heads = [
            q_ref[:, (g * groups + i) * HD : (g * groups + i + 1) * HD] for i in range(groups)
        ]
        scores = dot_nt(jnp.concatenate(heads, axis=0), k_ref[:, g * HD : (g + 1) * HD])
        scores = scores * (1.0 / math.sqrt(HD))
        totals = jnp.sum(jnp.where(allowed, jnp.exp(scores), 0.0), axis=1, keepdims=True)
        probs = jnp.where(allowed, jnp.exp(scores - jnp.log(totals)), 0.0)
        p_ref[g] = probs
        out = matmul(probs.astype(bf16), v_ref[:, g * HD : (g + 1) * HD])
        for i in range(groups):
            j = g * groups + i
            wide_q[:, j * HD : (j + 1) * HD] = out[i * tokens : (i + 1) * tokens]
    attended = matmul(wide_q[:, :width].astype(bf16), pad_ref[...]).astype(bf16)
    att_ref[...] = attended
    outs = []
    for half in range(2):
        w_out = matmul(w_ref[1, half].reshape(deep, q_cols + k_cols), pick_ref[...]).astype(bf16)
        wo_ref[half] = w_out
        outs.append(matmul(attended, w_out))
    middle = hidden[:tokens] + jnp.concatenate(outs, axis=1)
    middle_ref[...] = middle
    factor = lax.rsqrt(jnp.sum(middle * middle, axis=1, keepdims=True) / width + norm_eps)
    second_ref[...] = (middle * factor * gains[1]).astype(bf16)


def deal(item, x, y, nz, send_y, send_x, by_x, by_y, own):
    @pl.loop(0, nz)
    def _(z):
        for d in range(2):
            send_y[d, z] = item(0, 1 - y, z, x ^ d)
            send_x[d, z] = item(1, y ^ d, z, 1 - x)
            own[d, z] = item(d, y, z, x)
        by_x[z] = item(0, y, z, 1 - x)
        by_y[z] = item(1, 1 - y, z, x)


def pack_shapes(nz, *block):
    two, one = ((2, nz, *block), bf16), ((nz, *block), bf16)
    return [two, two, one, one, two]


def assemble(store, x, y, nz, axis, line, by_x, by_y, corner_0, corner_1):
    @pl.loop(0, nz)
    def _(z):
        for t in range(2):
            corner = (corner_0, corner_1)[t]
            for dy in range(2):
                for dx in range(2):
                    at = (z, t) if axis == 0 else (t, z)
                    piece = corner[z] if dy and dx else (line, by_x, by_y)[dx + 2 * dy][at]
                    store(t, y ^ dy, z, x ^ dx, piece)


def assemble_gate_up(w_ref, x, y, nz, gate_parts, up_parts):
    for which, parts in enumerate((gate_parts, up_parts)):

        def store(t, y, z, x, piece, which=which):
            w_ref[which, y, z, x, t * 64 : (t + 1) * 64, :] = piece

        assemble(store, x, y, nz, which, *parts)


def feed_forward(dims, place_ref, second_ref, got_ref, cot_ref, *refs):
    nz, ff_rows = dims
    x, y = place_ref[1], place_ref[2]
    (gate_ref, up_ref, mixed_ref, *dealt), (w_ref, sums) = refs[10:18], refs[18:]
    assemble_gate_up(w_ref, x, y, nz, refs[:5], refs[5:10])
    pair = jnp.concatenate([second_ref[...], got_ref[...]], axis=0)
    deep, n = nz * 2 * 128, w_ref.shape[-1]
    part, count = ff_rows // 2, n // ff_rows

    @pl.loop(0, 2)
    def _(half):
        gate = matmul(pair, w_ref[0, half].reshape(deep, n))
        upward = matmul(pair, w_ref[1, half].reshape(deep, n))
        gate_ref[half] = gate
        up_ref[half] = upward
        sigma = 1.0 / (1.0 + jnp.exp(-gate))
        mixed = (gate * sigma * upward).astype(bf16)
        mixed_ref[half] = mixed
        for columns in range(2):
            grads = dot_t(mixed, cot_ref[columns]).astype(bf16)
            for block in range(count):
                for t in range(2):
                    at = block * ff_rows + t * part
                    z = half * (count // 2) + block // 2
                    sums[t, columns, z, block % 2] = grads[at : at + part]

    deal(lambda t, y, z, x: sums[t, y, z, x], x, y, nz, *dealt)


def feed_backward(dims, place_ref, pad_ref, second_ref, got_ref, cot_ref, gate_ref, up_ref, mixed_ref, *refs):
    nz, ff_rows = dims
    x, y = place_ref[1], place_ref[2]
    (out_ref, out_away_ref, back_ref, back_away_ref, *dealt) = refs[15:24]
    (w_ref, d_ref, sums, back, out) = refs[24:]
    part = ff_rows // 2

    def store(t, y, z, x, piece):
        d_ref[y, z, x, t * part : (t + 1) * part, :] = piece

    assemble(store, x, y, nz, 1, *refs[10:15])
    assemble_gate_up(w_ref, x, y, nz, refs[:5], refs[5:10])
    tokens = second_ref.shape[0]
    pair = jnp.concatenate([second_ref[...], got_ref[...]], axis=0)
    deep, n = nz * 2 * 128, w_ref.shape[-1]
    lanes = out.shape[1] // 2
    back[...] = jnp.zeros_like(back)
    out[...] = jnp.zeros_like(out)

    @pl.loop(0, 2)
    def _(half):
        mine = pl.ds(half * (nz // 2), nz // 2)
        down = [d_ref[columns, mine].reshape(n, d_ref.shape[-1]) for columns in range(2)]
        gm = dot_nt(cot_ref[0], down[0]) + dot_nt(cot_ref[1], down[1])
        gate, upward = gate_ref[half], up_ref[half]
        sigma = 1.0 / (1.0 + jnp.exp(-gate))
        grad_gate = (gm * upward * sigma * (1.0 + gate * (1.0 - sigma))).astype(bf16)
        grad_up = (gm * (gate * sigma)).astype(bf16)
        for which, grad in enumerate((grad_gate, grad_up)):
            total = dot_t(pair, grad).astype(bf16)
            for z in range(nz):
                for p in range(2):
                    for t in range(2):
                        at = ((z * 2 + p) * 2 + t) * 64
                        sums[t, half, z, p, which] = total[at : at + 64]
            back[...] += dot_nt(grad, w_ref[which, half].reshape(deep, n))
        for columns in range(2):
            wide = matmul(down[columns], pad_ref[...]).astype(bf16)
            out[:, columns * lanes : (columns + 1) * lanes] += matmul(mixed_ref[half], wide)

    deal(lambda t, y, z, x: sums[t, y, z, x], x, y, nz, *dealt)
    back_ref[...] = back[:tokens]
    back_away_ref[...] = back[tokens:].astype(bf16)
    out_ref[...] = out[:tokens]
    out_away_ref[...] = out[tokens:].astype(bf16)


def attention_backward(
    dims, place_ref, pad_ref, cot_ref, mine_ref, facing_ref, cos_ref, sin_ref, back_ref, back_got_ref, w_ref, wo_ref,
    gains_ref, x_ref, q_ref, k_ref, v_ref, p_ref, att_ref, middle_ref, keep_ref, away_ref, grad_middle_ref, first_ref,
    first_away_ref, wide_q, wide_k, wide_v, wide_g, sums, lefts, rights, outs, back,
):
    nz, rows, width, q_cols, k_cols = dims
    c, x, y = place_ref[0], place_ref[1], place_ref[2]
    tokens = middle_ref.shape[0]
    deep = nz * 2 * 128
    pad = pad_ref[...]
    gains = gains_ref[...]
    middle = middle_ref[...]
    factor = lax.rsqrt(jnp.sum(middle * middle, axis=1, keepdims=True) / width + norm_eps)
    incoming = back_ref[...] + back_got_ref[...].astype(f32)
    gain_second = jnp.sum(incoming * middle * factor, axis=0, keepdims=True)
    scaled = incoming * gains[1:2]
    mean = jnp.sum(scaled * middle, axis=1, keepdims=True) / width
    grad_middle = (
        matmul(cot_ref[...], pad) + factor * scaled - middle * (factor * factor * factor * mean)
    )
    grad_middle_ref[...] = grad_middle
    branch = grad_middle.astype(bf16)
    half_lanes = wo_ref.shape[-1]
    grad_att = dot_nt(branch[:, :half_lanes], wo_ref[0]) + dot_nt(branch[:, half_lanes:], wo_ref[1])
    grad_att = dot_nt(grad_att.astype(bf16), pad).astype(bf16)
    groups = H // KV
    wide_q[...] = jnp.zeros_like(wide_q)
    wide_k[...] = jnp.zeros_like(wide_k)
    wide_g[:, :width] = grad_att
    for g in range(KV):
        at = slice(g * HD, (g + 1) * HD)
        heads = [slice((g * groups + i) * HD, (g * groups + i + 1) * HD) for i in range(groups)]
        grad = jnp.concatenate([wide_g[:, h] for h in heads], axis=0)
        query = jnp.concatenate([q_ref[:, h] for h in heads], axis=0)
        probs = p_ref[g]
        wide_v[:, at] = dot_t(probs.astype(bf16), grad)
        grad_probs = dot_nt(grad, v_ref[:, at])
        row = jnp.sum(probs * grad_probs, axis=1, keepdims=True)
        grad_scores = (probs * (grad_probs - row) * (1.0 / math.sqrt(HD))).astype(bf16)
        wide_k[:, at] = dot_t(grad_scores, query)
        out = matmul(grad_scores, k_ref[:, at])
        for i in range(groups):
            wide_q[:, heads[i]] = out[i * tokens : (i + 1) * tokens]
    cosine, sine = cos_ref[...], sin_ref[...]
    lanes = wide_q.shape[1]
    value = wide_q[...]
    value = value * wide_table(cosine[:tokens], lanes) - swapped(value) * wide_table(
        sine[:tokens], lanes
    )
    wide_q[...] = value
    lanes = wide_k.shape[1]
    value = wide_k[...]
    value = value * wide_table(cosine, lanes) - swapped(value) * wide_table(sine, lanes)
    wide_k[...] = value
    plain = dot_nt(branch, pad)
    first = x_ref[...]
    attended = att_ref[...]
    zeros_q = jnp.zeros((tokens, q_cols), f32)
    zeros_o = jnp.zeros((2 * tokens, q_cols), f32)
    zeros_v = jnp.zeros((tokens, k_cols), f32)
    n = q_cols + k_cols
    for half in range(2):
        of_q = jnp.concatenate([wide_q[:, half * q_cols : (half + 1) * q_cols], zeros_q], axis=0)
        of_k = wide_k[:, half * k_cols : (half + 1) * k_cols]
        of_v = wide_v[:, half * k_cols : (half + 1) * k_cols]
        of_o = plain[:, half * q_cols : (half + 1) * q_cols]
        lefts[half] = jnp.concatenate([of_q, of_k], axis=1).astype(bf16)
        rights[half] = jnp.concatenate([of_v, zeros_o], axis=1).astype(bf16)
        outs[half] = jnp.concatenate([zeros_v, of_o], axis=1).astype(bf16)
    back[...] = jnp.zeros_like(back)

    @pl.loop(0, 2)
    def _(half):
        left, right = lefts[half], rights[half]
        totals = (dot_t(first, left), dot_t(first, right) + dot_t(attended, outs[half]))
        for s in range(2):
            total = totals[s].astype(bf16)
            for z in range(nz):
                for p in range(2):
                    for t in range(2):
                        at = ((z * 2 + p) * 2 + t) * 64
                        sums[s, t, half, z, p] = total[at : at + 64]
            back[...] += dot_nt((left, right)[s], w_ref[s, half].reshape(deep, n))

    hidden = matmul(jnp.concatenate([mine_ref[...], facing_ref[...]], axis=0), pad)
    factor = lax.rsqrt(jnp.sum(hidden * hidden, axis=1, keepdims=True) / width + norm_eps)
    gain_first = jnp.sum(back[...] * hidden * factor, axis=0, keepdims=True)
    first_ref[...] = back[:tokens]
    first_away_ref[...] = back[tokens:].astype(bf16)
    for z in range(nz):
        for p in range(2):
            lane = slice((z * 2 + p) * 128, (z * 2 + p + 1) * 128)
            gain_row = jnp.concatenate(
                [gain_first[:, lane], gain_second[:, lane], jnp.zeros((1, n - 256), f32)], axis=1
            )
            gain_rows = jnp.concatenate(
                [gain_row, jnp.zeros((63 - rows, n), f32)], axis=0
            ).astype(bf16)
            for half in range(2):
                for s in range(2):
                    for t in range(2):
                        sums[s, t, half, z, p, rows:64, :] = gain_rows
    for which, ref in ((c, keep_ref), (1 - c, away_ref)):
        views = (ref.at[0:2], ref.at[2:4], ref.at[4], ref.at[5], ref.at[6:8])
        deal(lambda t, y, z, x, s=which: sums[s, t, y, z, x], x, y, nz, *views)


def run_kernel(body, inputs, outs, scratch):
    moved = sum(math.prod(a.shape) * a.dtype.itemsize for a in inputs)
    vmem = pl.BlockSpec(memory_space=pltpu.VMEM)
    return pl.pallas_call(
        body,
        out_shape=[jax.ShapeDtypeStruct(shape, kind) for shape, kind in outs],
        in_specs=[pl.BlockSpec(memory_space=pltpu.SMEM)] + [vmem] * (len(inputs) - 1),
        out_specs=[vmem] * len(outs),
        scratch_shapes=scratch,
        compiler_params=pltpu.CompilerParams(vmem_limit_bytes=60 << 20),
        cost_estimate=pl.CostEstimate(flops=2 * 10**9, bytes_accessed=moved, transcendentals=0),
    )(*inputs)


def fast_pass(
    tokens, segment_ids, norm_gains, w_query, w_key, w_value, w_out, w_gate, w_up, w_down, cotangent
):
    net = Links()
    nz, c, x, y = net.nz, net.c, net.x, net.y
    local_rows = tokens.shape[1]
    width = tokens.shape[2]
    rows = w_query.shape[0]
    groups = H // KV
    q_cols, k_cols, o_cols = w_query.shape[1], w_key.shape[1], w_out.shape[1]
    attn_cols = q_cols + k_cols
    ff_rows = w_down.shape[0]
    half_ff = w_gate.shape[1] // 2

    mine = tokens[0]
    segments_mine = segment_ids[0]
    segment_row = jnp.pad(
        segments_mine[None].astype(bf16), ((0, 7), (0, width - local_rows))
    )
    facing_pack = net.over_y(jnp.concatenate([mine, segment_row], axis=0))
    facing = facing_pack[:local_rows]
    segments_facing = facing_pack[local_rows, :local_rows].astype(jnp.int32)
    incoming = cotangent[0]
    incoming_got = net.core(incoming)
    incoming_pair = jnp.concatenate([incoming, incoming_got], axis=0)

    def by_core(w):
        starts = range(0, 2 * half_ff, 2 * ff_rows)
        return [
            jnp.concatenate(
                [w[:, at + i * ff_rows : at + (i + 1) * ff_rows] for at in starts], axis=1
            )
            for i in range(2)
        ]

    qk = jnp.concatenate([w_query, w_key], axis=1)
    vo = jnp.concatenate([w_value, w_out], axis=1)
    gate_half, up_half = by_core(w_gate), by_core(w_up)
    gains_row = jnp.pad(norm_gains.astype(bf16), ((0, 0), (0, 64 - rows)))
    gains_row = net.order(c, gains_row, jnp.zeros_like(gains_row), 1).reshape(1, 256)
    gains_row = jnp.pad(gains_row, ((0, 63 - rows), (0, attn_cols - 256)))

    def with_gains(w):
        return jnp.concatenate([w, gains_row], axis=0)

    def tall(w):
        return jnp.pad(w, ((0, 64 - rows), (0, 0)))

    got = net.core(
        jnp.stack(
            [
                with_gains(pick(c, (vo, qk))),
                tall(pick(c, (gate_half[1], gate_half[0]))),
                tall(pick(c, (up_half[1], up_half[0]))),
            ]
        )
    )
    attn_rows = 64

    def chip_pack(own, other):
        return net.order(c, own[None], other[None], 0)

    attn_pack = chip_pack(with_gains(pick(c, (qk, vo))), got[0])
    gate_pack = chip_pack(tall(pick(c, gate_half)), got[1])
    up_pack = chip_pack(tall(pick(c, up_half)), got[2])
    down_pack = w_down.reshape(2, ff_rows // 2, w_down.shape[1])

    attn_line = net.gather_z(attn_pack, 0)
    gate_line = net.gather_z(gate_pack, 0)
    up_line = net.gather_z(up_pack, 1)
    down_line = net.gather_z(down_pack, 1)
    attn_own = net.spread(attn_line, 0)
    attn_other = [net.core(piece) for piece in attn_own]
    gate_parts = net.spread(gate_line, 0)
    up_parts = net.spread(up_line, 1)
    down_parts = net.spread(down_line, 1)

    place = jnp.stack([c, x, y]).astype(jnp.int32)
    both_rows = 2 * local_rows
    blocks = nz * 2
    lanes = blocks * 128
    deep = blocks * 128
    pad = padded_columns(width, rows, 64, 0, width)
    pad_half = padded_columns(o_cols, rows, 64, 0, o_cols)
    pick_half = padded_columns(o_cols, rows, 64, k_cols, attn_cols)
    tables = [
        rope_tables(local_rows, start, HD) for start in (y * local_rows, (1 - y) * local_rows)
    ]
    cosine = jnp.concatenate([t[0][:, 0] for t in tables], axis=0)
    sine = jnp.concatenate([t[1][:, 0] for t in tables], axis=0)
    cosine = jnp.concatenate([cosine] * 4, axis=1)
    sine = jnp.concatenate([-sine, sine] * 2, axis=1)
    own_places = y * local_rows + jnp.arange(local_rows, dtype=jnp.int32)
    facing_places = (1 - y) * local_rows + jnp.arange(local_rows, dtype=jnp.int32)
    key_places = jnp.concatenate([own_places, facing_places])
    segment_all = jnp.concatenate([segments_mine, segments_facing])
    allowed = (
        (key_places[None, :] <= own_places[:, None])
        & (segment_all[None, :] == segments_mine[:, None])
    ).astype(f32)
    dims = (nz, rows, width, q_cols, k_cols)
    wide_k = KV * HD + 64
    (w_attn, w_out_wide, gains, first_norm, query, keys, values, probs, attended, middle, second_norm) = (
        run_kernel(
            functools.partial(attention_forward, dims),
            (place, pad, pick_half, mine, facing, allowed, cosine, sine, *attn_own, *attn_other),
            [
                ((2, 2, nz, 2, 128, attn_cols), bf16),
                ((2, deep, lanes // 2), bf16),
                ((8, lanes), f32),
                ((both_rows, lanes), bf16),
                ((local_rows, lanes), bf16),
                ((both_rows, wide_k), bf16),
                ((both_rows, KV * HD), bf16),
                ((KV, groups * local_rows, both_rows), f32),
                ((local_rows, lanes), bf16),
                ((local_rows, lanes), f32),
                ((local_rows, lanes), bf16),
            ],
            [pltpu.VMEM((local_rows, lanes), f32), pltpu.VMEM((both_rows, wide_k), f32)],
        )
    )

    second_got = net.core(second_norm)
    incoming_halves = jnp.stack(jnp.split(incoming_pair, 2, axis=1))
    ff_dims = (nz, ff_rows)
    chip_w = pltpu.VMEM((2, 2, nz, 2, 128, half_ff), bf16)
    gate, upward, mixed, *down_grads = run_kernel(
        functools.partial(feed_forward, ff_dims),
        (place, second_norm, second_got, incoming_halves, *gate_parts, *up_parts),
        [
            ((2, both_rows, half_ff), f32),
            ((2, both_rows, half_ff), f32),
            ((2, both_rows, half_ff), bf16),
            *pack_shapes(nz, ff_rows // 2, o_cols),
        ],
        [chip_w, pltpu.VMEM((2, 2, nz, 2, ff_rows // 2, o_cols), bf16)],
    )
    down_grad = net.reduce(down_grads).reshape(ff_rows, -1)
    out_mine, out_away, back_mine, back_away, *gu_grads = run_kernel(
        functools.partial(feed_backward, ff_dims),
        (place, pad_half, second_norm, second_got, incoming_halves, gate, upward, mixed,
         *gate_parts, *up_parts, *down_parts),
        [
            ((local_rows, lanes), f32),
            ((local_rows, lanes), bf16),
            ((local_rows, lanes), f32),
            ((local_rows, lanes), bf16),
            *pack_shapes(nz, 2, 64, half_ff),
        ],
        [
            chip_w,
            pltpu.VMEM((2, nz, 2, ff_rows, o_cols), bf16),
            pltpu.VMEM((2, 2, nz, 2, 2, 64, half_ff), bf16),
            pltpu.VMEM((both_rows, lanes), f32),
            pltpu.VMEM((both_rows, lanes), f32),
        ],
    )
    gu_sum = net.reduce(gu_grads)
    back_got = net.core(back_away)
    attn_keep, attn_away, grad_middle, first_mine, first_away = run_kernel(
        functools.partial(attention_backward, dims),
        (place, pad, incoming, mine, facing, cosine, sine, back_mine, back_got, w_attn, w_out_wide, gains,
         first_norm, query, keys, values, probs, attended, middle),
        [
            ((8, nz, attn_rows, attn_cols), bf16),
            ((8, nz, attn_rows, attn_cols), bf16),
            ((local_rows, lanes), f32),
            ((local_rows, lanes), f32),
            ((local_rows, lanes), bf16),
        ],
        [
            pltpu.VMEM((local_rows, lanes), f32),
            pltpu.VMEM((both_rows, wide_k), f32),
            pltpu.VMEM((both_rows, KV * HD), f32),
            pltpu.VMEM((local_rows, lanes), bf16),
            pltpu.VMEM((2, 2, 2, nz, 2, attn_rows, attn_cols), bf16),
            pltpu.VMEM((2, both_rows, attn_cols), bf16),
            pltpu.VMEM((2, both_rows, attn_cols), bf16),
            pltpu.VMEM((2, local_rows, attn_cols), bf16),
            pltpu.VMEM((both_rows, lanes), f32),
        ],
    )
    from_core = net.core(attn_away)

    def both_cores(at):
        return (attn_keep[at].astype(f32) + from_core[at].astype(f32)).astype(bf16)

    attn_both = [both_cores(at) for at in (slice(0, 2), slice(2, 4), 4, 5, slice(6, 8))]
    attn_sum = net.reduce(attn_both)

    def narrow(value):
        return value.reshape(local_rows, 2 * blocks, 64)[:, :, :rows].reshape(local_rows, width)

    out_got = net.core(out_away)
    block_output = narrow(middle + out_mine + out_got.astype(f32)).astype(bf16)
    first_got = net.over_y(first_away)
    grad_first = narrow(first_mine + first_got.astype(f32))
    hidden = mine.astype(f32)
    gain = narrow(jnp.broadcast_to(gains[0:1], (local_rows, lanes)))[0]
    _, pull_first = jax.vjp(normed, hidden, gain)
    input_grad = narrow(grad_middle) + pull_first(grad_first)[0]

    def core_rows(total):
        return pick(c, total), net.core(pick(c, (total[1], total[0])).astype(bf16)).astype(f32)

    gu_mine, gu_got = core_rows(gu_sum)

    def columns(which):
        pair = (gu_mine[which, :rows], gu_got[which, :rows])
        parts = (pick(c, pair), pick(c, pair[::-1]))
        starts = range(0, half_ff, ff_rows)
        return jnp.concatenate(
            [part[:, at : at + ff_rows] for at in starts for part in parts], axis=1
        )

    gu_grad = columns(0), columns(1)
    attn_mine, attn_got = (part[:rows] for part in core_rows(attn_sum))
    qk_grad = pick(c, (attn_mine, attn_got))
    vo_grad = pick(c, (attn_got, attn_mine))
    gain_out = attn_sum[0, rows, :256].reshape(2, 2, 64)
    gain_out = pick(c, (gain_out[:, 0, :rows], gain_out[:, 1, :rows]))
    return (
        block_output[None],
        input_grad[None],
        qk_grad[:, :q_cols],
        qk_grad[:, q_cols:],
        vo_grad[:, :k_cols],
        vo_grad[:, k_cols:],
        gu_grad[0],
        gu_grad[1],
        down_grad,
        gain_out,
    )


def fast_body(*args):
    return fast_pass(*args)


def body(
    tokens, segment_ids, norm_gains, w_query, w_key, w_value, w_out, w_gate, w_up, w_down, cotangent
):
    local_rows = tokens.shape[1]
    groups = H // KV
    scale_factor = 1.0 / math.sqrt(HD)
    offset = lax.axis_index("ctx") * local_rows
    column_parts = (
        lax.all_gather(w_query, "ctx", axis=1, tiled=True),
        lax.all_gather(w_key, "ctx", axis=1, tiled=True),
        lax.all_gather(w_value, "ctx", axis=1, tiled=True),
        lax.all_gather(w_out, "ctx", axis=1, tiled=True),
        lax.all_gather(w_gate, "ctx", axis=1, tiled=True),
        lax.all_gather(w_up, "ctx", axis=1, tiled=True),
        lax.all_gather(w_down, "ctx", axis=1, tiled=True),
    )
    forward_set = (
        lax.all_gather(column_parts[0], "dp", axis=0, tiled=True),
        lax.all_gather(column_parts[1], "dp", axis=0, tiled=True),
        lax.all_gather(column_parts[2], "dp", axis=0, tiled=True),
        lax.all_gather(column_parts[3], "dp", axis=0, tiled=True),
        lax.all_gather(column_parts[4], "dp", axis=0, tiled=True),
        lax.all_gather(column_parts[5], "dp", axis=0, tiled=True),
        lax.all_gather(column_parts[6], "dp", axis=0, tiled=True),
        lax.all_gather(norm_gains.astype(jnp.bfloat16), "dp", axis=1, tiled=True).astype(
            norm_gains.dtype
        ),
    )
    query_full, key_full, value_full, out_full, gate_full, up_full, down_full, gains_full = (
        forward_set
    )
    hidden = tokens[0].astype(jnp.float32)
    own_segments = segment_ids[0]
    first_norm = normed(hidden, gains_full[0]).astype(jnp.bfloat16)
    cosine, sine = rope_tables(local_rows, offset, HD)
    query = rotate(matmul(first_norm, query_full).reshape(local_rows, H, HD), cosine, sine).astype(
        jnp.bfloat16
    )
    keys_local = (
        rotate(matmul(first_norm, key_full).reshape(local_rows, KV, HD), cosine, sine)
        .astype(jnp.bfloat16)
        .reshape(local_rows, KV * HD)
    )
    values_local = matmul(first_norm, value_full).astype(jnp.bfloat16)
    key_all, value_all, segment_all = (
        lax.all_gather(keys_local, "ctx", axis=0, tiled=True),
        lax.all_gather(values_local, "ctx", axis=0, tiled=True),
        lax.all_gather(own_segments, "ctx", axis=0, tiled=True),
    )
    length_all = key_all.shape[0]
    key_grid = key_all.reshape(length_all, KV, HD)
    value_grid = value_all.reshape(length_all, KV, HD)
    grouped = query.reshape(local_rows, KV, groups, HD)
    query_places = offset + jnp.arange(local_rows, dtype=jnp.int32)
    key_places = jnp.arange(length_all, dtype=jnp.int32)
    allowed = (key_places[None, :] <= query_places[:, None]) & (
        segment_all[None, :] == own_segments[:, None]
    )
    scores = score_block(grouped, key_grid, scale_factor)
    totals = jnp.sum(jnp.where(allowed, jnp.exp(scores), 0.0), axis=-1, keepdims=True)
    log_total = jnp.log(totals)
    probs = probabilities(scores, allowed, log_total).astype(jnp.bfloat16)
    attended = jnp.einsum("kgts,skd->tkgd", probs, value_grid, preferred_element_type=jnp.float32)
    attended = attended.reshape(local_rows, H * HD).astype(jnp.bfloat16)
    middle = hidden + matmul(attended, out_full)
    second_norm = normed(middle, gains_full[1]).astype(jnp.bfloat16)
    gate = matmul(second_norm, gate_full)
    upward = matmul(second_norm, up_full)
    sigma = jax.nn.sigmoid(gate)
    activated = gate * sigma
    mixed = (activated * upward).astype(jnp.bfloat16)
    block_output = (middle + matmul(mixed, down_full)).astype(jnp.bfloat16)
    query_back, key_back, value_back, out_back, gate_back, up_back, down_back, gains_back = (
        forward_set
    )
    incoming = cotangent[0]
    grad_down = matmul(mixed.T, incoming)
    grad_mixed = matmul(incoming, down_back.T)
    grad_gate = (grad_mixed * upward * sigma * (1.0 + gate * (1.0 - sigma))).astype(jnp.bfloat16)
    grad_upward = (grad_mixed * activated).astype(jnp.bfloat16)
    grad_wgate = matmul(second_norm.T, grad_gate)
    grad_wup = matmul(second_norm.T, grad_upward)
    grad_second = matmul(grad_gate, gate_back.T) + matmul(grad_upward, up_back.T)
    _, pull_second = jax.vjp(normed, middle, gains_back[1])
    grad_middle_norm, grad_gain_second = pull_second(grad_second)
    grad_middle = incoming.astype(jnp.float32) + grad_middle_norm
    grad_branch = grad_middle.astype(jnp.bfloat16)
    grad_wout = matmul(attended.T, grad_branch)
    grad_attended = (
        matmul(grad_branch, out_back.T).astype(jnp.bfloat16).reshape(local_rows, KV, groups, HD)
    )
    exact_probs = probabilities(score_block(grouped, key_grid, scale_factor), allowed, log_total)
    probs_again = exact_probs.astype(jnp.bfloat16)
    grad_values_all = jnp.einsum(
        "kgts,tkgd->skd", probs_again, grad_attended, preferred_element_type=jnp.float32
    )
    grad_probs = jnp.einsum(
        "tkgd,skd->kgts", grad_attended, value_grid, preferred_element_type=jnp.float32
    )
    row_terms = jnp.sum(exact_probs * grad_probs, axis=-1, keepdims=True)
    grad_scores = (exact_probs * (grad_probs - row_terms) * scale_factor).astype(jnp.bfloat16)
    grad_query = jnp.einsum(
        "kgts,skd->tkgd", grad_scores, key_grid, preferred_element_type=jnp.float32
    )
    grad_query = (
        unrotate(grad_query.reshape(local_rows, H, HD), cosine, sine)
        .reshape(local_rows, H * HD)
        .astype(jnp.bfloat16)
    )
    grad_keys_all = jnp.einsum(
        "kgts,tkgd->skd", grad_scores, grouped, preferred_element_type=jnp.float32
    )
    own_keys, own_values = (
        lax.psum_scatter(
            grad_keys_all.reshape(length_all, KV * HD).astype(jnp.bfloat16),
            "ctx",
            scatter_dimension=0,
            tiled=True,
        ).astype(jnp.float32),
        lax.psum_scatter(
            grad_values_all.reshape(length_all, KV * HD).astype(jnp.bfloat16),
            "ctx",
            scatter_dimension=0,
            tiled=True,
        ).astype(jnp.float32),
    )
    grad_keys = (
        unrotate(own_keys.reshape(local_rows, KV, HD), cosine, sine)
        .reshape(local_rows, KV * HD)
        .astype(jnp.bfloat16)
    )
    grad_values = own_values.astype(jnp.bfloat16)
    grad_wquery = matmul(first_norm.T, grad_query)
    grad_wkey = matmul(first_norm.T, grad_keys)
    grad_wvalue = matmul(first_norm.T, grad_values)
    grad_first = (
        matmul(grad_query, query_back.T)
        + matmul(grad_keys, key_back.T)
        + matmul(grad_values, value_back.T)
    )
    _, pull_first = jax.vjp(normed, hidden, gains_back[0])
    grad_hidden_norm, grad_gain_first = pull_first(grad_first)
    input_grad = grad_middle + grad_hidden_norm
    gain_terms = jnp.stack([grad_gain_first, grad_gain_second])
    gain_copies = jnp.broadcast_to(gain_terms[None], (lax.axis_size("ctx"),) + gain_terms.shape)
    by_cols = (
        lax.psum_scatter(
            grad_wquery.astype(jnp.bfloat16), "ctx", scatter_dimension=1, tiled=True
        ).astype(jnp.float32),
        lax.psum_scatter(
            grad_wkey.astype(jnp.bfloat16), "ctx", scatter_dimension=1, tiled=True
        ).astype(jnp.float32),
        lax.psum_scatter(
            grad_wvalue.astype(jnp.bfloat16), "ctx", scatter_dimension=1, tiled=True
        ).astype(jnp.float32),
        lax.psum_scatter(
            grad_wout.astype(jnp.bfloat16), "ctx", scatter_dimension=1, tiled=True
        ).astype(jnp.float32),
        lax.psum_scatter(
            grad_wgate.astype(jnp.bfloat16), "ctx", scatter_dimension=1, tiled=True
        ).astype(jnp.float32),
        lax.psum_scatter(
            grad_wup.astype(jnp.bfloat16), "ctx", scatter_dimension=1, tiled=True
        ).astype(jnp.float32),
        lax.psum_scatter(
            grad_down.astype(jnp.bfloat16), "ctx", scatter_dimension=1, tiled=True
        ).astype(jnp.float32),
        lax.psum_scatter(
            gain_copies.astype(jnp.bfloat16), "ctx", scatter_dimension=0, tiled=True
        ).astype(jnp.float32),
    )
    finals = (
        lax.psum_scatter(
            by_cols[0].astype(jnp.bfloat16), "dp", scatter_dimension=0, tiled=True
        ).astype(jnp.float32),
        lax.psum_scatter(
            by_cols[1].astype(jnp.bfloat16), "dp", scatter_dimension=0, tiled=True
        ).astype(jnp.float32),
        lax.psum_scatter(
            by_cols[2].astype(jnp.bfloat16), "dp", scatter_dimension=0, tiled=True
        ).astype(jnp.float32),
        lax.psum_scatter(
            by_cols[3].astype(jnp.bfloat16), "dp", scatter_dimension=0, tiled=True
        ).astype(jnp.float32),
        lax.psum_scatter(
            by_cols[4].astype(jnp.bfloat16), "dp", scatter_dimension=0, tiled=True
        ).astype(jnp.float32),
        lax.psum_scatter(
            by_cols[5].astype(jnp.bfloat16), "dp", scatter_dimension=0, tiled=True
        ).astype(jnp.float32),
        lax.psum_scatter(
            by_cols[6].astype(jnp.bfloat16), "dp", scatter_dimension=0, tiled=True
        ).astype(jnp.float32),
        lax.psum_scatter(
            by_cols[7].astype(jnp.bfloat16), "dp", scatter_dimension=2, tiled=True
        ).astype(jnp.float32),
    )
    gain_out = finals[7][0]
    return (
        block_output[None],
        input_grad[None],
        finals[0],
        finals[1],
        finals[2],
        finals[3],
        finals[4],
        finals[5],
        finals[6],
        gain_out,
    )


def solution(mesh):
    two_blocks = mesh.shape["ctx"] == 2 and mesh.shape["dp"] % 4 == 0
    return jax.shard_map(
        fast_body if two_blocks else body,
        mesh=mesh,
        in_specs=(
            P("dp", "ctx", None),
            P("dp", "ctx"),
            P(None, "dp"),
            P("dp", "ctx"),
            P("dp", "ctx"),
            P("dp", "ctx"),
            P("dp", "ctx"),
            P("dp", "ctx"),
            P("dp", "ctx"),
            P("dp", "ctx"),
            P("dp", "ctx", None),
        ),
        out_specs=(
            P("dp", "ctx", None),
            P("dp", "ctx", None),
            P("dp", "ctx"),
            P("dp", "ctx"),
            P("dp", "ctx"),
            P("dp", "ctx"),
            P("dp", "ctx"),
            P("dp", "ctx"),
            P("dp", "ctx"),
            P(None, "dp"),
        ),
        check_vma=False,
    )
```
